32 devices in a mesh: shard: 4 (over y, core), replica: 8 (over z, x).
Axes of the slice: x: 2, y: 2, z: 4, core: 2. Of those that a mesh axis runs over, the one named last changes fastest.
Arguments:
- tokens: bfloat16 [8, 1024, 1024], P('replica', 'shard'), may hold values from -6 to 6
- cotangent: bfloat16 [8, 1024, 1024], P('replica', 'shard'), may hold values from -6 to 6
- lengths: int32 [8], P('replica'), may hold values from 256 to 1024, as said below
- block_order: int32 [8, 8], P('replica'), may hold values from 0 to 7, as said below
- norm1_gain: bfloat16 [1024], P('shard'), may hold values from 0.099609375 to 1.8984375
- query_weight: bfloat16 [1024, 2048], P('shard'), may hold values from -0.1875 to 0.1875
- key_weight: bfloat16 [1024, 1024], P('shard'), may hold values from -0.1875 to 0.1875
- value_weight: bfloat16 [1024, 1024], P('shard'), may hold values from -0.1875 to 0.1875
- output_weight: bfloat16 [2048, 1024], P('shard'), may hold values from -1.5 to 1.5
- query_gain: bfloat16 [128], P('shard'), may hold values from 0.099609375 to 1.8984375
- key_gain: bfloat16 [128], P('shard'), may hold values from 0.099609375 to 1.8984375
- norm2_gain: bfloat16 [1024], P('shard'), may hold values from 0.099609375 to 1.8984375
- gate_weight: bfloat16 [1024, 3072], P('shard'), may hold values from -0.1875 to 0.1875
- up_weight: bfloat16 [1024, 3072], P('shard'), may hold values from -0.1875 to 0.1875
- down_weight: bfloat16 [3072, 1024], P('shard'), may hold values from -0.109375 to 0.109375
Outputs:
- output: bfloat16 [8, 1024, 1024], P('replica', 'shard')
- input_grad: float32 [8, 1024, 1024], P('replica', 'shard')
- norm1_gain_grad: float32 [1024], P('shard')
- query_weight_grad: float32 [1024, 2048], P('shard')
- key_weight_grad: float32 [1024, 1024], P('shard')
- value_weight_grad: float32 [1024, 1024], P('shard')
- output_weight_grad: float32 [2048, 1024], P('shard')
- query_gain_grad: float32 [128], P('shard')
- key_gain_grad: float32 [128], P('shard')
- norm2_gain_grad: float32 [1024], P('shard')
- gate_weight_grad: float32 [1024, 3072], P('shard')
- up_weight_grad: float32 [1024, 3072], P('shard')
- down_weight_grad: float32 [3072, 1024], P('shard')
The draws below stay inside these ranges and needn't reach their ends.
Inputs may be any that keep to these rules, and one draw needn't show every extreme that they name: `lengths`: in every group of 1 sequence one has 1024 valid tokens; valid tokens hold positions 0 to length - 1. `block_order`: each row is a permutation of 0 to 7 in which places 2j and 2j + 1 hold blocks that add up to 7.
All inputs are finite; a program needn't handle non-finite values.
Results may differ from the reference program's by a relative error of at most 0.013.
Values may be sent and summed in bfloat16 or wider, within the bound.
A program may use at most 256 MiB of HBM per device.

```python
import jax
import jax.numpy as jnp
from jax import lax

D = 1024
HEADS = 16
KV = 8
HD = 128
FF = 3072
SLOT = 1024
MIN_LEN = 256
SEQ_GRP = 1
SEQS = 8
BLOCKS = 8


def draw_lengths(key, part):
    first_key, second_key = jax.random.split(jax.random.fold_in(key, 11))
    drawn = jax.random.randint(first_key, (SEQS,), MIN_LEN, SLOT + 1)
    group_count = SEQS // SEQ_GRP
    chosen = jax.random.randint(second_key, (group_count, 1), 0, SEQ_GRP)
    longest = (jnp.arange(SEQ_GRP)[None, :] == chosen).reshape(SEQS)
    return jnp.where(longest, SLOT, drawn).astype(jnp.int32)


def draw_block_order(key, part):
    pair_count = BLOCKS // 2
    seq_keys = jax.random.split(jax.random.fold_in(key, 23), SEQS)
    permuted = jax.vmap(lambda one_key: jax.random.permutation(one_key, pair_count))(seq_keys)
    first_half = permuted.astype(jnp.int32)
    second_half = (BLOCKS - 1 - permuted).astype(jnp.int32)
    return jnp.stack([first_half, second_half], axis=2).reshape(SEQS, BLOCKS).astype(jnp.int32)


def block_levels(rng, shape, shards, low, top_value):
    level, own = 1.0, jax.random.fold_in(rng, 6)
    for axis_at, blocks in shards:
        steps = jnp.exp(jax.random.uniform(jax.random.fold_in(own, axis_at), (blocks,), jnp.float32, low / len(shards), top_value / len(shards)))
        level = level * jnp.repeat(steps, shape[axis_at] // blocks).reshape([-1 if axis == axis_at else 1 for axis in range(len(shape))])
    return level


def bell_draw(key, extent, deviation, bound, shards=(), held_as=jnp.bfloat16):
    array = deviation * jax.random.normal(key, extent, jnp.float32)
    if shards:
        array = array * block_levels(key, extent, shards, -0.22, 0.18)
    return jnp.clip(array, -bound, bound).astype(held_as)


def setup_inputs(seed: int = 0) -> dict:
    seeds = jax.random.split(jax.random.key(seed), 16)
    tokens = bell_draw(seeds[0], (SEQS, SLOT, D), 1.0, 6.0, ((0, 8), (1, 4)))
    cotangent = bell_draw(seeds[1], (SEQS, SLOT, D), 1.0, 6.0, ((0, 8), (1, 4)))
    lengths = draw_lengths(jax.random.fold_in(seeds[15], 71), 0)
    block_order = draw_block_order(jax.random.fold_in(seeds[15], 71), 0)
    norm1_gain = jnp.clip(1.0 + 0.18 * jax.random.normal(seeds[4], (D,), jnp.float32), 0.099609375, 1.8984375).astype(jnp.bfloat16)
    query_weight = bell_draw(seeds[5], (D, HEADS * HD), D ** -0.5, 0.1875, ((0, 4),))
    key_weight = bell_draw(seeds[6], (D, KV * HD), D ** -0.5, 0.1875, ((0, 4),))
    value_weight = bell_draw(seeds[7], (D, KV * HD), D ** -0.5, 0.1875, ((0, 4),))
    output_weight = bell_draw(seeds[8], (HEADS * HD, D), (max(1, HEADS * HD // 128)) ** -0.5, 1.5, ((0, 4),))
    query_gain = jnp.clip(1.0 + 0.18 * jax.random.normal(seeds[9], (HD,), jnp.float32), 0.099609375, 1.8984375).astype(jnp.bfloat16)
    key_gain = jnp.clip(1.0 + 0.18 * jax.random.normal(seeds[10], (HD,), jnp.float32), 0.099609375, 1.8984375).astype(jnp.bfloat16)
    norm2_gain = jnp.clip(1.0 + 0.18 * jax.random.normal(seeds[11], (D,), jnp.float32), 0.099609375, 1.8984375).astype(jnp.bfloat16)
    gate_weight = bell_draw(seeds[12], (D, FF), D ** -0.5, 0.1875, ((0, 4),))
    up_weight = bell_draw(seeds[13], (D, FF), D ** -0.5, 0.1875, ((0, 4),))
    down_weight = bell_draw(seeds[14], (FF, D), FF ** -0.5, 0.109375, ((0, 4),))
    return {"tokens": tokens, "cotangent": cotangent, "lengths": lengths, "block_order": block_order, "norm1_gain": norm1_gain, "query_weight": query_weight, "key_weight": key_weight, "value_weight": value_weight, "output_weight": output_weight, "query_gain": query_gain, "key_gain": key_gain, "norm2_gain": norm2_gain, "gate_weight": gate_weight, "up_weight": up_weight, "down_weight": down_weight}


EPSILON = 1e-06
ROPE_BASE = 1000000.0
PRECISE = lax.Precision.HIGHEST

@jax.custom_vjp
def low(v):
    return lax.optimization_barrier(v.astype(jnp.bfloat16)).astype(jnp.float32)

@jax.custom_vjp
def low_back(v):
    return v

def low_keep(v):
    return (low(v), None)

def low_pass(kept, grad):
    return (grad,)

def back_keep(v):
    return (v, None)

def back_low(kept, grad):
    return (low(grad),)
low.defvjp(low_keep, low_pass)
low_back.defvjp(back_keep, back_low)

def rms_scale(values, gain_vec):
    return values * lax.rsqrt(lax.optimization_barrier(jnp.mean(values * values, axis=-1, keepdims=True)) + EPSILON) * gain_vec

def rotate_half(values, cosine, sine_table):
    middle = values.shape[-1] // 2
    turned = jnp.concatenate([-values[..., middle:], values[..., :middle]], axis=-1)
    return values * cosine + turned * sine_table

def rotary_tables(position, head_width):
    middle = head_width // 2
    exponent = jnp.arange(middle, dtype=jnp.float32) * 2.0 / head_width
    inverse = ROPE_BASE ** (-exponent)
    phases = position.astype(jnp.float32)[..., None] * inverse
    phases = jnp.concatenate([phases, phases], axis=-1)
    return (jnp.cos(phases), jnp.sin(phases))

def block_layer(inputs, weights, position, valid_rows):
    norm1_gain, query_weight, key_weight, value_weight, output_weight, query_gain, key_gain, norm2_gain, gate_weight, up_weight, down_weight = weights
    token_count = inputs.shape[0]
    normed = low(rms_scale(inputs, norm1_gain))
    query_raw = low_back(jnp.dot(normed, query_weight, precision=PRECISE)).reshape(token_count, HEADS, HD)
    key_raw = low_back(jnp.dot(normed, key_weight, precision=PRECISE)).reshape(token_count, KV, HD)
    value_heads = low(low_back(jnp.dot(normed, value_weight, precision=PRECISE))).reshape(token_count, KV, HD)
    cosine, sine_table = rotary_tables(position, HD)
    cosine = cosine[:, None, :]
    sine_table = sine_table[:, None, :]
    query_rot = low(rotate_half(rms_scale(query_raw, query_gain), cosine, sine_table))
    query_rot = query_rot.reshape(token_count, KV, HEADS // KV, HD)
    key_rot = low(rotate_half(rms_scale(key_raw, key_gain), cosine, sine_table))
    scores = low_back(jnp.einsum('qkgd,tkd->kgqt', query_rot, key_rot, precision=PRECISE) * HD ** (-0.5))
    allowed = position[None, :] <= position[:, None]
    scores = jnp.where(allowed, scores, -1e+30)
    row_top = lax.optimization_barrier(jnp.max(scores, axis=-1, keepdims=True))
    log_total = row_top + jnp.log(lax.optimization_barrier(jnp.sum(jnp.exp(scores - row_top), axis=-1, keepdims=True)))
    softmax_w = low(jnp.exp(scores - log_total))
    mixed_heads = jnp.einsum('kgqt,tkd->qkgd', softmax_w, value_heads, precision=PRECISE)
    mixed_heads = low(low_back(mixed_heads.reshape(token_count, HEADS * HD)))
    hidden = inputs + low_back(jnp.dot(mixed_heads, output_weight, precision=PRECISE))
    normed2 = low(rms_scale(hidden, norm2_gain))
    gate_proj = low_back(jnp.dot(normed2, gate_weight, precision=PRECISE))
    up_proj = low_back(jnp.dot(normed2, up_weight, precision=PRECISE))
    active = low(jax.nn.silu(gate_proj) * up_proj)
    branch = low_back(jnp.dot(active, down_weight, precision=PRECISE))
    return valid_rows[:, None] * (hidden + branch)

def reference(tokens, cotangent, lengths, block_order, norm1_gain, query_weight, key_weight, value_weight, output_weight, query_gain, key_gain, norm2_gain, gate_weight, up_weight, down_weight):
    weights = (norm1_gain.astype(jnp.float32), query_weight.astype(jnp.float32), key_weight.astype(jnp.float32), value_weight.astype(jnp.float32), output_weight.astype(jnp.float32), query_gain.astype(jnp.float32), key_gain.astype(jnp.float32), norm2_gain.astype(jnp.float32), gate_weight.astype(jnp.float32), up_weight.astype(jnp.float32), down_weight.astype(jnp.float32))
    block_count = block_order.shape[1]
    block_len = SLOT // block_count
    offsets = jnp.arange(SLOT, dtype=jnp.int32)

    def one_sequence(running, sequence_item):
        inputs, grad_out, length, order_row = sequence_item
        position = order_row[offsets // block_len] * block_len + offsets % block_len
        valid_rows = (position < length).astype(jnp.float32)
        result, pull_back = jax.vjp(lambda inputs_in, weights_in: block_layer(inputs_in, weights_in, position, valid_rows), inputs.astype(jnp.float32), weights)
        grad_in, grad_weights = pull_back(grad_out.astype(jnp.float32))
        running = jax.tree.map(lambda before, extra: before + extra, running, grad_weights)
        return (running, (result.astype(jnp.bfloat16), grad_in))
    zero_grads = jax.tree.map(jnp.zeros_like, weights)
    totals, (output, input_grad) = lax.scan(one_sequence, zero_grads, (tokens, cotangent, lengths, block_order))
    return (output, input_grad, totals[0], totals[1], totals[2], totals[3], totals[4], totals[5], totals[6], totals[7], totals[8], totals[9], totals[10])
```

```python
import jax
import jax.numpy as jnp
from jax import lax
from jax.sharding import PartitionSpec as P

EPSILON = 1e-06
ROPE_BASE = 1000000.0
BF = jnp.bfloat16
F32 = jnp.float32


def rms_scale(values, gain_vec):
    return (
        values * lax.rsqrt(jnp.mean(values * values, axis=-1, keepdims=True) + EPSILON) * gain_vec
    )


def rotate_half(values, cosine, sine_table):
    middle = values.shape[-1] // 2
    turned = jnp.concatenate([-values[..., middle:], values[..., :middle]], axis=-1)
    return values * cosine + turned * sine_table


def rotary_tables(position, head_width):
    middle = head_width // 2
    exponent = jnp.arange(middle, dtype=F32) * 2.0 / head_width
    inverse = ROPE_BASE ** (-exponent)
    phases = position.astype(F32)[..., None] * inverse
    phases = jnp.concatenate([phases, phases], axis=-1)
    return (jnp.cos(phases), jnp.sin(phases))


def mm(a, b):
    return jnp.einsum("ri,io->ro", a, b, preferred_element_type=F32)


def mm_t(a, b):
    return jnp.einsum("ro,io->ri", a, b, preferred_element_type=F32)


def mm_w(a, b):
    return jnp.einsum("ri,ro->io", a, b, preferred_element_type=F32)


def gather_rows(v):
    return lax.all_gather(v, "shard", axis=0, tiled=True)


def scatter_rows(v):
    return lax.psum_scatter(v.astype(BF), "shard", scatter_dimension=0, tiled=True).astype(F32)


def to_columns(w):
    return lax.all_to_all(w, "shard", split_axis=1, concat_axis=0, tiled=True)


def to_rows(g):
    return lax.all_to_all(g, "shard", split_axis=0, concat_axis=1, tiled=True)


def shards(
    tokens,
    cotangent,
    lengths,
    block_order,
    norm1_gain,
    query_weight,
    key_weight,
    value_weight,
    output_weight,
    query_gain,
    key_gain,
    norm2_gain,
    gate_weight,
    up_weight,
    down_weight,
):
    shard_count = lax.axis_size("shard")
    row_count = tokens.shape[1]
    block_count = block_order.shape[1]
    slot_len = row_count * shard_count
    block_len = slot_len // block_count
    head_width = query_gain.shape[0] * shard_count
    score_scale = head_width ** (-0.5)
    gains = lax.all_gather(
        jnp.concatenate([norm1_gain, norm2_gain, query_gain, key_gain]), "shard", axis=0
    )
    wide = norm1_gain.shape[0]
    gain_one = gains[:, :wide].reshape(-1).astype(F32)
    gain_two = gains[:, wide : 2 * wide].reshape(-1).astype(F32)
    gain_query = gains[:, 2 * wide : 2 * wide + query_gain.shape[0]].reshape(-1).astype(F32)
    gain_key = gains[:, 2 * wide + query_gain.shape[0] :].reshape(-1).astype(F32)
    w_qkv = tuple(to_columns(w) for w in (query_weight, key_weight, value_weight))
    w_gate, w_up = to_columns(gate_weight), to_columns(up_weight)
    heads = w_qkv[0].shape[1] // head_width
    kvs = w_qkv[1].shape[1] // head_width
    per = heads // kvs

    offsets = jnp.arange(slot_len, dtype=jnp.int32)
    pos_all = (
        jnp.repeat(block_order[0], block_len, total_repeat_length=slot_len) * block_len
        + offsets % block_len
    )
    pos_local = lax.dynamic_slice_in_dim(pos_all, lax.axis_index("shard") * row_count, row_count)
    valid_rows = (pos_local < lengths[0]).astype(F32)[:, None]
    allowed = pos_all[None, None, None, :] <= pos_all[None, None, :, None]

    inputs = tokens[0].astype(F32)
    normed_f, norm_one_back = jax.vjp(rms_scale, inputs, gain_one)
    normed = gather_rows(normed_f.astype(BF))
    grad_result = cotangent[0].astype(F32) * valid_rows
    grad_branch = gather_rows(grad_result.astype(BF))
    query_raw = mm(normed, w_qkv[0]).reshape(slot_len, heads, head_width)
    key_raw = mm(normed, w_qkv[1]).reshape(slot_len, kvs, head_width)
    value = mm(normed, w_qkv[2]).astype(BF).reshape(slot_len, kvs, head_width)
    cosine, sine = rotary_tables(pos_all, head_width)
    cosine, sine = cosine[:, None, :], sine[:, None, :]

    def turn(q, k, gq, gk):
        return (
            rotate_half(rms_scale(q, gq), cosine, sine),
            rotate_half(rms_scale(k, gk), cosine, sine),
        )

    turned, turn_back = jax.vjp(turn, query_raw, key_raw, gain_query, gain_key)
    query = turned[0].astype(BF).reshape(slot_len, kvs, per, head_width)
    key = turned[1].astype(BF)

    def scores_of():
        raw = jnp.einsum("rkgd,tkd->kgrt", query, key, preferred_element_type=F32) * score_scale
        return jnp.where(allowed, raw, -1e30)

    scores = scores_of()
    row_top = jnp.max(scores, axis=-1, keepdims=True)
    log_total = row_top + jnp.log(jnp.sum(jnp.exp(scores - row_top), axis=-1, keepdims=True))
    probs = jnp.exp(scores - log_total).astype(BF)
    mixed = jnp.einsum("kgrt,tkd->rkgd", probs, value, preferred_element_type=F32)
    mixed = mixed.reshape(slot_len, heads * head_width).astype(BF)
    hidden = inputs + scatter_rows(mm(mixed, output_weight))
    normed2_f, norm_two_back = jax.vjp(rms_scale, hidden, gain_two)
    normed2 = gather_rows(normed2_f.astype(BF))
    active_f, swish_back = jax.vjp(
        lambda a, b: jax.nn.silu(a) * b, mm(normed2, w_gate), mm(normed2, w_up)
    )
    active = active_f.astype(BF)
    output = (valid_rows * (hidden + scatter_rows(mm(active, down_weight)))).astype(BF)
    grad_gate_f, grad_up_f = swish_back(mm_t(grad_branch, down_weight))
    grad_gate, grad_up = grad_gate_f.astype(BF), grad_up_f.astype(BF)
    grad_hidden_norm, grad_gain_two = norm_two_back(
        scatter_rows(mm_t(grad_gate, w_gate) + mm_t(grad_up, w_up))
    )
    grad_hidden = grad_result + grad_hidden_norm
    grad_mixed_in = gather_rows(grad_hidden.astype(BF))
    grad_mixed = mm_t(grad_mixed_in, output_weight).astype(BF)
    grad_mixed = grad_mixed.reshape(slot_len, kvs, per, head_width)
    probs_f = jnp.exp(scores_of() - log_total)
    grad_probs = jnp.einsum("rkgd,tkd->kgrt", grad_mixed, value, preferred_element_type=F32)
    grad_value = jnp.einsum(
        "kgrt,rkgd->tkd", probs_f.astype(BF), grad_mixed, preferred_element_type=F32
    )
    row_inner = jnp.sum(probs_f * grad_probs, axis=-1, keepdims=True)
    grad_scores = (probs_f * (grad_probs - row_inner)).astype(BF)
    grad_query = (
        jnp.einsum("kgrt,tkd->rkgd", grad_scores, key, preferred_element_type=F32) * score_scale
    )
    grad_key = (
        jnp.einsum("kgrt,rkgd->tkd", grad_scores, query, preferred_element_type=F32) * score_scale
    )
    grad_query_raw, grad_key_raw, grad_gain_query, grad_gain_key = turn_back(
        (grad_query.reshape(slot_len, heads, head_width), grad_key)
    )
    grad_query_b = grad_query_raw.reshape(slot_len, -1).astype(BF)
    grad_key_b = grad_key_raw.reshape(slot_len, -1).astype(BF)
    grad_value_b = grad_value.reshape(slot_len, -1).astype(BF)
    grad_normed = (
        mm_t(grad_query_b, w_qkv[0]) + mm_t(grad_key_b, w_qkv[1]) + mm_t(grad_value_b, w_qkv[2])
    )
    grad_inputs_norm, grad_gain_one = norm_one_back(scatter_rows(grad_normed))
    input_grad = grad_hidden + grad_inputs_norm

    def total(v):
        return lax.psum(v.astype(BF), "replica").astype(F32)

    grad_down = total(mm_w(active, grad_branch))
    grad_gate_w = to_rows(total(mm_w(normed2, grad_gate)).astype(BF)).astype(F32)
    grad_up_w = to_rows(total(mm_w(normed2, grad_up)).astype(BF)).astype(F32)
    grad_output_w = total(mm_w(mixed, grad_mixed_in))
    grad_query_w = to_rows(total(mm_w(normed, grad_query_b)).astype(BF)).astype(F32)
    grad_key_w = to_rows(total(mm_w(normed, grad_key_b)).astype(BF)).astype(F32)
    grad_value_w = to_rows(total(mm_w(normed, grad_value_b)).astype(BF)).astype(F32)
    small = jnp.concatenate([grad_gain_one, grad_gain_two, grad_gain_query, grad_gain_key])
    small = lax.psum(small, ("shard", "replica"))
    at = lax.axis_index("shard")
    hw = query_gain.shape[0]

    def own(start, size):
        return lax.dynamic_slice_in_dim(small, start + at * size, size)

    model = wide * shard_count
    return (
        output[None],
        input_grad[None],
        own(0, wide),
        grad_query_w,
        grad_key_w,
        grad_value_w,
        grad_output_w,
        own(2 * model, hw),
        own(2 * model + head_width, hw),
        own(model, wide),
        grad_gate_w,
        grad_up_w,
        grad_down,
    )


def solution(mesh):
    rows, mat, vec = P("replica", "shard", None), P("shard", None), P("shard")
    placed = (rows, rows, P("replica"), P("replica", None), vec, mat, mat, mat, mat)
    placed += (vec, vec, vec, mat, mat, mat)
    outs = (rows, rows, vec, mat, mat, mat, mat, vec, vec, vec, mat, mat, mat)
    return jax.shard_map(shards, mesh=mesh, in_specs=placed, out_specs=outs, check_vma=False)
```

```python
import jax
import jax.numpy as jnp
from jax import lax
from jax.experimental import pallas as pl
from jax.experimental.pallas import tpu as pltpu
from jax.sharding import PartitionSpec as P

EPSILON = 1e-06
ROPE_BASE = 1000000.0
BF = jnp.bfloat16
F32 = jnp.float32


class Topo:
    def __init__(self, shards, replicas):
        self.S=shards; self.R=replicas; self.L=replicas//2
        self.s=lax.axis_index("shard"); r=lax.axis_index("replica")
        self.r=r
        L=self.L
        self.a=lax.div(r,2); self.b=lax.rem(r,2)
        self.m0=L//2-1; self.m1=L//2
        a=self.a
        self.left=a<=self.m0
        self.mid=jnp.logical_or(a==self.m0,a==self.m1)
        self.edge=jnp.logical_or(a==0,a==L-1)
        self.toward=jnp.where(self.left,r+2,r-2)
        self.outward=jnp.where(self.left,r-2,r+2)
        self.h=jnp.where(self.left,0,1)
    def rep(self, r): return (self.s, r)
    def sh(self, k): return (self.s^k, self.r)

def barrier(tp):
    bar=pltpu.get_barrier_semaphore()
    R=tp.R
    ids=[tp.rep(tp.r^1), tp.rep(lax.rem(tp.r+2,R)), tp.rep(lax.rem(tp.r+R-2,R)), tp.sh(1), tp.sh(2), tp.sh(3)]
    for d in ids:
        pl.semaphore_signal(bar, inc=1, device_id=d, device_id_type=pl.DeviceIdType.MESH)
    pl.semaphore_wait(bar, len(ids))

def add_into(dst, a, b, blocks, rows, step):
    def body(i, _):
        q=pl.multiple_of(i*step, step)
        for t in range(blocks):
            dst[t, pl.ds(q,step), :] = (a[t, pl.ds(q,step), :].astype(F32)+b[t, pl.ds(q,step), :].astype(F32)).astype(BF)
        return 0
    lax.fori_loop(0, rows//step, body, 0)

class Chunk:
    def __init__(self, tp, kind, G, out, j, nr, spread, bufs, sems):
        self.tp=tp; self.kind=kind; self.G=G; self.out=out; self.base=j*nr; self.nr=nr; self.hr=nr//2
        self.spread=spread; self.bufs=bufs; self.sem_send, self.sem_recv, self.i=sems
        self.W=G.shape[2]; self.W0=self.W
        self.sent=[]
        self.steps=self.steps_a() if kind=="A" else self.steps_b()
    def half(self, h):
        return self.G.at[:, pl.ds(pl.multiple_of(self.base+h*self.hr,16), self.hr), :]
    def full(self):
        return self.G.at[:, pl.ds(self.base, self.nr), :]
    def out_half(self, h):
        rows=pl.ds(pl.multiple_of(self.base+h*self.hr,16), self.hr)
        return self.out.at[rows, :] if self.spread else self.out.at[:, rows, :]
    def out_piece(self, h, s):
        rows=pl.ds(pl.multiple_of(self.base+h*self.hr,16), self.hr)
        return self.out.at[rows, pl.ds(pl.multiple_of(s*self.W,128), self.W)]
    def copy(self, slot, src, dst, dev):
        return pltpu.make_async_remote_copy(src, dst, self.sem_send.at[self.i*10+slot], self.sem_recv.at[self.i*10+slot], device_id=dev, device_id_type=pl.DeviceIdType.MESH)
    def start(self, cond, slot, src, dst, dev):
        c=self.copy(slot,src,dst,dev)
        if cond is None:
            c.start()
        else:
            pl.when(cond)(lambda: c.start())
        self.sent.append((cond,c))
    def drain(self):
        for cond,c in self.sent:
            if cond is None: c.wait_send()
            else: pl.when(cond)(lambda c=c: c.wait_send())
    def recv(self, slot, ref):
        self.copy(slot, ref, ref, self.tp.rep(self.tp.r^1)).wait_recv()
    def final_out(self, h, F):
        tp=self.tp
        if self.spread:
            for k in (1,2,3):
                blk=tp.s^k
                self.start(tp.mid, 2+k, F.at[blk], self.out_piece(h, tp.s), tp.sh(k))
        @pl.when(tp.mid)
        def _():
            if self.spread:
                pltpu.make_async_copy(F.at[tp.s], self.out_piece(h, tp.s), self.sem_send.at[self.i*10+9]).start()
            else:
                pltpu.make_async_copy(F, self.out_half(h), self.sem_send.at[self.i*10+9]).start()
    def final_wait(self, h, F):
        tp=self.tp
        if self.spread:
            for k in (1,2,3):
                self.copy(2+k, F.at[0], self.out_piece(h, tp.s^k), tp.sh(k)).wait_recv()
            pltpu.make_async_copy(F.at[tp.s], self.out_piece(h, tp.s), self.sem_send.at[self.i*10+9]).wait()
        else:
            pltpu.make_async_copy(F, self.out_half(h), self.sem_send.at[self.i*10+9]).wait()
    def steps_a(self):
        tp=self.tp; b=tp.b; RX,FOLD,MID=self.bufs; xp=tp.rep(tp.r^1)
        not_edge=jnp.logical_not(tp.edge); not_mid=jnp.logical_not(tp.mid)
        has_outer=not_edge
        own=self.half(b)
        def push(cond):
            self.start(jnp.logical_and(cond,tp.mid), 2, own, MID, tp.rep(tp.toward))
            if tp.L>2: self.start(jnp.logical_and(cond,not_mid), 1, own, FOLD, tp.rep(tp.toward))
        def s0():
            self.start(None, 0, self.half(1-b), RX, xp)
        def s1():
            self.recv(0,RX)
            add_into(own, own, RX, 4, self.hr, 16)
            push(tp.edge)
        def s2():
            if tp.L==2: return
            @pl.when(has_outer)
            def _():
                self.recv(1,FOLD)
                add_into(own, own, FOLD, 4, self.hr, 16)
            push(has_outer)
        def s3():
            @pl.when(tp.mid)
            def _():
                self.recv(2,MID)
                add_into(MID, own, MID, 4, self.hr, 16)
            self.final_out(b, MID)
        def s4():
            @pl.when(tp.mid)
            def _():
                self.final_wait(b, MID)
            if tp.L>2: self.start(tp.mid, 6, self.out_half(b), self.out_half(b), tp.rep(tp.outward))
            self.start(tp.mid, 7, self.out_half(b), self.out_half(b), xp)
        def s5():
            if tp.L==2: return
            @pl.when(not_mid)
            def _():
                self.recv(6,self.out_half(b))
            if tp.L>4: self.start(jnp.logical_and(not_mid,not_edge), 6, self.out_half(b), self.out_half(b), tp.rep(tp.outward))
            self.start(not_mid, 7, self.out_half(b), self.out_half(b), xp)
        def s6():
            self.recv(7,self.out_half(1-b))
        return [s0,s1,s2,s3,s4,s5,s6]
    def steps_b(self):
        tp=self.tp; h=tp.h; FOLD,MID,XB=self.bufs; xp=tp.rep(tp.r^1)
        not_edge=jnp.logical_not(tp.edge); not_mid=jnp.logical_not(tp.mid)
        own=self.half(h); full=self.full()
        def push(cond):
            self.start(jnp.logical_and(cond,tp.mid), 2, self.half(1-h), MID, tp.rep(tp.toward))
            if tp.L>2: self.start(jnp.logical_and(cond,not_mid), 1, full, FOLD, tp.rep(tp.toward))
        def s0():
            push(tp.edge)
        def s1():
            if tp.L==2: return
            @pl.when(not_edge)
            def _():
                self.recv(1,FOLD)
                add_into(full, full, FOLD, 4, self.nr, 16)
            push(not_edge)
        def s2():
            @pl.when(tp.mid)
            def _():
                self.recv(2,MID)
                add_into(own, own, MID, 4, self.hr, 16)
            self.start(tp.mid, 0, own, XB, xp)
        def s3():
            @pl.when(tp.mid)
            def _():
                self.recv(0,XB)
                add_into(XB, own, XB, 4, self.hr, 16)
            self.final_out(h, XB)
        def s4():
            @pl.when(tp.mid)
            def _():
                self.final_wait(h, XB)
            self.start(tp.mid, 8, self.out_half(h), self.out_half(h), tp.rep(tp.toward))
            if tp.L>2: self.start(tp.mid, 6, self.out_half(h), self.out_half(h), tp.rep(tp.outward))
        def s5():
            @pl.when(tp.mid)
            def _():
                self.recv(8,self.out_half(1-h))
            if tp.L==2: return
            self.start(tp.mid, 7, self.out_half(1-h), self.out_half(1-h), tp.rep(tp.outward))
            @pl.when(not_mid)
            def _():
                self.recv(6,self.out_half(h))
            if tp.L>4: self.start(jnp.logical_and(not_mid,not_edge), 6, self.out_half(h), self.out_half(h), tp.rep(tp.outward))
        def s6():
            if tp.L==2: return
            @pl.when(not_mid)
            def _():
                self.recv(7,self.out_half(1-h))
            if tp.L>4: self.start(jnp.logical_and(not_mid,not_edge), 7, self.out_half(1-h), self.out_half(1-h), tp.rep(tp.outward))
        return [s0,s1,s2,s3,s4,s5,s6]

ARR=dict(gu=(256,1536,True,64), d=(192,1024,False,64), o=(128,1024,False,64), qkv=(256,1024,True,32))
ORDER=["d","gu","o","qkv"]

def plan():
    chunks=[]; i=0
    for n in ORDER:
        rows,W,sp,nr=ARR[n]
        for j in range(rows//nr):
            chunks.append((n,j,"A" if i%2==0 else "B")); i+=1
    return chunks

def scratch(chunks):
    scr=[]
    for n,j,k in chunks:
        rows,W,sp,nr=ARR[n]
        h=pltpu.VMEM((4,nr//2,W),BF); f=pltpu.VMEM((4,nr,W),BF)
        scr += [h,h,h] if k=="A" else [f,h,h]
    n=len(chunks)
    return scr+[pltpu.SemaphoreType.DMA((n*10,)),pltpu.SemaphoreType.DMA((n*10,))]

def make(S,R):
    chunks=plan(); nb=3*len(chunks)
    def kern(*refs):
        ins=dict(zip(ORDER,refs[:4])); outs=dict(zip(ORDER,refs[4:8]));
        G=dict(zip(ORDER,refs[8:12])); ld=refs[12]
        bufs=refs[13:13+nb]; send,recv=refs[13+nb:]
        tp=Topo(S,R)
        for i,n in enumerate(ORDER):
            pltpu.make_async_copy(ins[n],G[n],ld.at[i]).start()
        barrier(tp)
        for i,n in enumerate(ORDER):
            pltpu.make_async_copy(ins[n],G[n],ld.at[i]).wait()
        cs=[Chunk(tp,k,G[n],outs[n],j,ARR[n][3],ARR[n][2],bufs[3*i:3*i+3],(send,recv,i)) for i,(n,j,k) in enumerate(chunks)]
        ns=7
        for t in range(len(cs)+ns-1):
            for st in range(ns-1,-1,-1):
                i=t-st
                if 0<=i<len(cs): cs[i].steps[st]()
        for c in cs: c.drain()
    out_shape=[jax.ShapeDtypeStruct((ARR[n][0],4*ARR[n][1]) if ARR[n][2] else (4,ARR[n][0],ARR[n][1]),BF) for n in ORDER]
    any_=pl.BlockSpec(memory_space=pl.ANY)
    def call(*gs):
        return pl.pallas_call(kern,out_shape=out_shape,in_specs=[any_]*4,out_specs=[any_]*4,
            scratch_shapes=[pltpu.VMEM((4,ARR[n][0],ARR[n][1]),BF) for n in ORDER]+[pltpu.SemaphoreType.DMA((4,))]+scratch(chunks),
            compiler_params=pltpu.CompilerParams(collective_id=1,has_side_effects=True,vmem_limit_bytes=60<<20),name="grad_sum")(*gs)
    return call


def rms_scale(values, gain_vec):
    return (
        values * lax.rsqrt(jnp.mean(values * values, axis=-1, keepdims=True) + EPSILON) * gain_vec
    )


def rotate_half(values, cosine, sine_table):
    middle = values.shape[-1] // 2
    turned = jnp.concatenate([-values[..., middle:], values[..., :middle]], axis=-1)
    return values * cosine + turned * sine_table


def rotary_tables(position, head_width):
    middle = head_width // 2
    exponent = jnp.arange(middle, dtype=F32) * 2.0 / head_width
    inverse = ROPE_BASE ** (-exponent)
    phases = position.astype(F32)[..., None] * inverse
    phases = jnp.concatenate([phases, phases], axis=-1)
    return (jnp.cos(phases), jnp.sin(phases))


def mm(a, b):
    return jnp.einsum("ri,io->ro", a, b, preferred_element_type=F32)


def mm_t(a, b):
    return jnp.einsum("ro,io->ri", a, b, preferred_element_type=F32)


def mm_w(a, b):
    return jnp.einsum("ri,ro->io", a, b, preferred_element_type=F32)


def gather_rows(v):
    return lax.all_gather(v, "shard", axis=0, tiled=True)


def scatter_rows(v):
    return lax.psum_scatter(v.astype(BF), "shard", scatter_dimension=0, tiled=True).astype(F32)


def to_columns(w):
    return lax.all_to_all(w, "shard", split_axis=1, concat_axis=0, tiled=True)


def to_rows(g):
    return lax.all_to_all(g, "shard", split_axis=0, concat_axis=1, tiled=True)


def shards(
    tokens,
    cotangent,
    lengths,
    block_order,
    norm1_gain,
    query_weight,
    key_weight,
    value_weight,
    output_weight,
    query_gain,
    key_gain,
    norm2_gain,
    gate_weight,
    up_weight,
    down_weight,
):
    shard_count = lax.axis_size("shard")
    row_count = tokens.shape[1]
    block_count = block_order.shape[1]
    slot_len = row_count * shard_count
    block_len = slot_len // block_count
    head_width = query_gain.shape[0] * shard_count
    score_scale = head_width ** (-0.5)
    gains = lax.all_gather(
        jnp.concatenate([norm1_gain, norm2_gain, query_gain, key_gain]), "shard", axis=0
    )
    wide = norm1_gain.shape[0]
    gain_one = gains[:, :wide].reshape(-1).astype(F32)
    gain_two = gains[:, wide : 2 * wide].reshape(-1).astype(F32)
    gain_query = gains[:, 2 * wide : 2 * wide + query_gain.shape[0]].reshape(-1).astype(F32)
    gain_key = gains[:, 2 * wide + query_gain.shape[0] :].reshape(-1).astype(F32)
    w_qkv = tuple(to_columns(w) for w in (query_weight, key_weight, value_weight))
    w_gate, w_up = to_columns(gate_weight), to_columns(up_weight)
    heads = w_qkv[0].shape[1] // head_width
    kvs = w_qkv[1].shape[1] // head_width
    per = heads // kvs

    offsets = jnp.arange(slot_len, dtype=jnp.int32)
    pos_all = (
        jnp.repeat(block_order[0], block_len, total_repeat_length=slot_len) * block_len
        + offsets % block_len
    )
    pos_local = lax.dynamic_slice_in_dim(pos_all, lax.axis_index("shard") * row_count, row_count)
    valid_rows = (pos_local < lengths[0]).astype(F32)[:, None]
    allowed = pos_all[None, None, None, :] <= pos_all[None, None, :, None]

    inputs = tokens[0].astype(F32)
    normed_f, norm_one_back = jax.vjp(rms_scale, inputs, gain_one)
    normed = gather_rows(normed_f.astype(BF))
    grad_result = cotangent[0].astype(F32) * valid_rows
    grad_branch = gather_rows(grad_result.astype(BF))
    query_raw = mm(normed, w_qkv[0]).reshape(slot_len, heads, head_width)
    key_raw = mm(normed, w_qkv[1]).reshape(slot_len, kvs, head_width)
    value = mm(normed, w_qkv[2]).astype(BF).reshape(slot_len, kvs, head_width)
    cosine, sine = rotary_tables(pos_all, head_width)
    cosine, sine = cosine[:, None, :], sine[:, None, :]

    def turn(q, k, gq, gk):
        return (
            rotate_half(rms_scale(q, gq), cosine, sine),
            rotate_half(rms_scale(k, gk), cosine, sine),
        )

    turned, turn_back = jax.vjp(turn, query_raw, key_raw, gain_query, gain_key)
    query = turned[0].astype(BF).reshape(slot_len, kvs, per, head_width)
    key = turned[1].astype(BF)

    def scores_of():
        raw = jnp.einsum("rkgd,tkd->kgrt", query, key, preferred_element_type=F32) * score_scale
        return jnp.where(allowed, raw, -1e30)

    scores = scores_of()
    row_top = jnp.max(scores, axis=-1, keepdims=True)
    log_total = row_top + jnp.log(jnp.sum(jnp.exp(scores - row_top), axis=-1, keepdims=True))
    probs = jnp.exp(scores - log_total).astype(BF)
    mixed = jnp.einsum("kgrt,tkd->rkgd", probs, value, preferred_element_type=F32)
    mixed = mixed.reshape(slot_len, heads * head_width).astype(BF)
    hidden = inputs + scatter_rows(mm(mixed, output_weight))
    normed2_f, norm_two_back = jax.vjp(rms_scale, hidden, gain_two)
    normed2 = gather_rows(normed2_f.astype(BF))
    active_f, swish_back = jax.vjp(
        lambda a, b: jax.nn.silu(a) * b, mm(normed2, w_gate), mm(normed2, w_up)
    )
    active = active_f.astype(BF)
    output = (valid_rows * (hidden + scatter_rows(mm(active, down_weight)))).astype(BF)
    grad_gate_f, grad_up_f = swish_back(mm_t(grad_branch, down_weight))
    grad_gate, grad_up = grad_gate_f.astype(BF), grad_up_f.astype(BF)
    grad_hidden_norm, grad_gain_two = norm_two_back(
        scatter_rows(mm_t(grad_gate, w_gate) + mm_t(grad_up, w_up))
    )
    grad_hidden = grad_result + grad_hidden_norm
    grad_mixed_in = gather_rows(grad_hidden.astype(BF))
    grad_mixed = mm_t(grad_mixed_in, output_weight).astype(BF)
    grad_mixed = grad_mixed.reshape(slot_len, kvs, per, head_width)
    probs_f = jnp.exp(scores_of() - log_total)
    grad_probs = jnp.einsum("rkgd,tkd->kgrt", grad_mixed, value, preferred_element_type=F32)
    grad_value = jnp.einsum(
        "kgrt,rkgd->tkd", probs_f.astype(BF), grad_mixed, preferred_element_type=F32
    )
    row_inner = jnp.sum(probs_f * grad_probs, axis=-1, keepdims=True)
    grad_scores = (probs_f * (grad_probs - row_inner)).astype(BF)
    grad_query = (
        jnp.einsum("kgrt,tkd->rkgd", grad_scores, key, preferred_element_type=F32) * score_scale
    )
    grad_key = (
        jnp.einsum("kgrt,rkgd->tkd", grad_scores, query, preferred_element_type=F32) * score_scale
    )
    grad_query_raw, grad_key_raw, grad_gain_query, grad_gain_key = turn_back(
        (grad_query.reshape(slot_len, heads, head_width), grad_key)
    )
    grad_query_b = grad_query_raw.reshape(slot_len, -1).astype(BF)
    grad_key_b = grad_key_raw.reshape(slot_len, -1).astype(BF)
    grad_value_b = grad_value.reshape(slot_len, -1).astype(BF)
    grad_normed = (
        mm_t(grad_query_b, w_qkv[0]) + mm_t(grad_key_b, w_qkv[1]) + mm_t(grad_value_b, w_qkv[2])
    )
    grad_inputs_norm, grad_gain_one = norm_one_back(scatter_rows(grad_normed))
    input_grad = grad_hidden + grad_inputs_norm

    def part(left, right):
        g = mm_w(left, right).astype(BF)
        return g.reshape(shard_count, g.shape[0] // shard_count, g.shape[1])

    share = {
        "d": part(active, grad_branch),
        "gu": part(normed2, jnp.concatenate([grad_gate, grad_up], axis=1)),
        "o": part(mixed, grad_mixed_in),
        "qkv": part(normed, jnp.concatenate([grad_query_b, grad_key_b, grad_value_b], axis=1)),
    }
    sums = dict(zip(ORDER, make(shard_count, lax.axis_size("replica"))(*[share[n] for n in ORDER])))
    grad_down = sums["d"].astype(F32).reshape(-1, sums["d"].shape[-1])
    grad_output_w = sums["o"].astype(F32).reshape(-1, sums["o"].shape[-1])

    def columns(v, start, width):
        v = v.reshape(v.shape[0], shard_count, -1)[:, :, start : start + width]
        return v.reshape(v.shape[0], -1).astype(F32)

    fw, qw, kw = w_gate.shape[1], w_qkv[0].shape[1], w_qkv[1].shape[1]
    grad_gate_w = columns(sums["gu"], 0, fw)
    grad_up_w = columns(sums["gu"], fw, fw)
    grad_query_w = columns(sums["qkv"], 0, qw)
    grad_key_w = columns(sums["qkv"], qw, kw)
    grad_value_w = columns(sums["qkv"], qw + kw, kw)
    small = jnp.concatenate([grad_gain_one, grad_gain_two, grad_gain_query, grad_gain_key])
    small = lax.psum(small, ("shard", "replica"))
    at = lax.axis_index("shard")
    hw = query_gain.shape[0]

    def own(start, size):
        return lax.dynamic_slice_in_dim(small, start + at * size, size)

    model = wide * shard_count
    return (
        output[None],
        input_grad[None],
        own(0, wide),
        grad_query_w,
        grad_key_w,
        grad_value_w,
        grad_output_w,
        own(2 * model, hw),
        own(2 * model + head_width, hw),
        own(model, wide),
        grad_gate_w,
        grad_up_w,
        grad_down,
    )


def solution(mesh):
    rows, mat, vec = P("replica", "shard", None), P("shard", None), P("shard")
    placed = (rows, rows, P("replica"), P("replica", None), vec, mat, mat, mat, mat)
    placed += (vec, vec, vec, mat, mat, mat)
    outs = (rows, rows, vec, mat, mat, mat, mat, vec, vec, vec, mat, mat, mat)
    return jax.shard_map(shards, mesh=mesh, in_specs=placed, out_specs=outs, check_vma=False)
```

```python
import functools

import jax
import jax.numpy as jnp
import numpy as np
from jax import lax
from jax.experimental import pallas as pl
from jax.experimental.pallas import tpu as pltpu
from jax.sharding import PartitionSpec as P

EPSILON = 1e-06
ROPE_BASE = 1000000.0
BF = jnp.bfloat16
F32 = jnp.float32
MESH = pl.DeviceIdType.MESH


class Topo:
    def __init__(self, shards, replicas):
        self.S=shards; self.R=replicas; self.L=replicas//2
        self.s=lax.axis_index("shard"); r=lax.axis_index("replica")
        self.r=r
        L=self.L
        self.a=lax.div(r,2); self.b=lax.rem(r,2)
        self.m0=L//2-1; self.m1=L//2
        a=self.a
        self.left=a<=self.m0
        self.mid=jnp.logical_or(a==self.m0,a==self.m1)
        self.edge=jnp.logical_or(a==0,a==L-1)
        self.toward=jnp.where(self.left,r+2,r-2)
        self.outward=jnp.where(self.left,r-2,r+2)
        self.h=jnp.where(self.left,0,1)
    def rep(self, r): return (self.s, r)
    def sh(self, k): return (self.s^k, self.r)

def barrier(tp):
    bar=pltpu.get_barrier_semaphore()
    R=tp.R
    ids=[tp.rep(tp.r^1), tp.rep(lax.rem(tp.r+2,R)), tp.rep(lax.rem(tp.r+R-2,R)), tp.sh(1), tp.sh(2), tp.sh(3)]
    for d in ids:
        pl.semaphore_signal(bar, inc=1, device_id=d, device_id_type=pl.DeviceIdType.MESH)
    pl.semaphore_wait(bar, len(ids))

def add_into(dst, a, b, blocks, rows, step):
    def body(i, _):
        q=pl.multiple_of(i*step, step)
        for t in range(blocks):
            dst[t, pl.ds(q,step), :] = (a[t, pl.ds(q,step), :].astype(F32)+b[t, pl.ds(q,step), :].astype(F32)).astype(BF)
        return 0
    lax.fori_loop(0, rows//step, body, 0)

class Chunk:
    def __init__(self, tp, kind, G, out, j, nr, spread, bufs, sems):
        self.tp=tp; self.kind=kind; self.G=G; self.out=out; self.base=j*nr; self.nr=nr; self.hr=nr//2
        self.spread=spread; self.bufs=bufs; self.sem_send, self.sem_recv, self.i=sems
        self.W=G.shape[2]; self.W0=self.W
        self.sent=[]
        self.steps=self.steps_a() if kind=="A" else self.steps_b()
    def half(self, h):
        return self.G.at[:, pl.ds(pl.multiple_of(self.base+h*self.hr,16), self.hr), :]
    def full(self):
        return self.G.at[:, pl.ds(self.base, self.nr), :]
    def out_half(self, h):
        rows=pl.ds(pl.multiple_of(self.base+h*self.hr,16), self.hr)
        return self.out.at[rows, :] if self.spread else self.out.at[:, rows, :]
    def out_piece(self, h, s):
        rows=pl.ds(pl.multiple_of(self.base+h*self.hr,16), self.hr)
        return self.out.at[rows, pl.ds(pl.multiple_of(s*self.W,128), self.W)]
    def copy(self, slot, src, dst, dev):
        return pltpu.make_async_remote_copy(src, dst, self.sem_send.at[self.i*10+slot], self.sem_recv.at[self.i*10+slot], device_id=dev, device_id_type=pl.DeviceIdType.MESH)
    def start(self, cond, slot, src, dst, dev):
        c=self.copy(slot,src,dst,dev)
        if cond is None:
            c.start()
        else:
            pl.when(cond)(lambda: c.start())
        self.sent.append((cond,c))
    def drain(self):
        for cond,c in self.sent:
            if cond is None: c.wait_send()
            else: pl.when(cond)(lambda c=c: c.wait_send())
    def recv(self, slot, ref):
        self.copy(slot, ref, ref, self.tp.rep(self.tp.r^1)).wait_recv()
    def final_out(self, h, F):
        tp=self.tp
        if self.spread:
            for k in (1,2,3):
                blk=tp.s^k
                self.start(tp.mid, 2+k, F.at[blk], self.out_piece(h, tp.s), tp.sh(k))
        @pl.when(tp.mid)
        def _():
            if self.spread:
                pltpu.make_async_copy(F.at[tp.s], self.out_piece(h, tp.s), self.sem_send.at[self.i*10+9]).start()
            else:
                pltpu.make_async_copy(F, self.out_half(h), self.sem_send.at[self.i*10+9]).start()
    def final_wait(self, h, F):
        tp=self.tp
        if self.spread:
            for k in (1,2,3):
                self.copy(2+k, F.at[0], self.out_piece(h, tp.s^k), tp.sh(k)).wait_recv()
            pltpu.make_async_copy(F.at[tp.s], self.out_piece(h, tp.s), self.sem_send.at[self.i*10+9]).wait()
        else:
            pltpu.make_async_copy(F, self.out_half(h), self.sem_send.at[self.i*10+9]).wait()
    def steps_a(self):
        tp=self.tp; b=tp.b; RX,FOLD,MID=self.bufs; xp=tp.rep(tp.r^1)
        not_edge=jnp.logical_not(tp.edge); not_mid=jnp.logical_not(tp.mid)
        has_outer=not_edge
        own=self.half(b)
        def push(cond):
            self.start(jnp.logical_and(cond,tp.mid), 2, own, MID, tp.rep(tp.toward))
            if tp.L>2: self.start(jnp.logical_and(cond,not_mid), 1, own, FOLD, tp.rep(tp.toward))
        def s0():
            self.start(None, 0, self.half(1-b), RX, xp)
        def s1():
            self.recv(0,RX)
            add_into(own, own, RX, 4, self.hr, 16)
            push(tp.edge)
        def s2():
            if tp.L==2: return
            @pl.when(has_outer)
            def _():
                self.recv(1,FOLD)
                add_into(own, own, FOLD, 4, self.hr, 16)
            push(has_outer)
        def s3():
            @pl.when(tp.mid)
            def _():
                self.recv(2,MID)
                add_into(MID, own, MID, 4, self.hr, 16)
            self.final_out(b, MID)
        def s4():
            @pl.when(tp.mid)
            def _():
                self.final_wait(b, MID)
            if tp.L>2: self.start(tp.mid, 6, self.out_half(b), self.out_half(b), tp.rep(tp.outward))
            self.start(tp.mid, 7, self.out_half(b), self.out_half(b), xp)
        def s5():
            if tp.L==2: return
            @pl.when(not_mid)
            def _():
                self.recv(6,self.out_half(b))
            if tp.L>4: self.start(jnp.logical_and(not_mid,not_edge), 6, self.out_half(b), self.out_half(b), tp.rep(tp.outward))
            self.start(not_mid, 7, self.out_half(b), self.out_half(b), xp)
        def s6():
            self.recv(7,self.out_half(1-b))
        return [s0,s1,s2,s3,s4,s5,s6]
    def steps_b(self):
        tp=self.tp; h=tp.h; FOLD,MID,XB=self.bufs; xp=tp.rep(tp.r^1)
        not_edge=jnp.logical_not(tp.edge); not_mid=jnp.logical_not(tp.mid)
        own=self.half(h); full=self.full()
        def push(cond):
            self.start(jnp.logical_and(cond,tp.mid), 2, self.half(1-h), MID, tp.rep(tp.toward))
            if tp.L>2: self.start(jnp.logical_and(cond,not_mid), 1, full, FOLD, tp.rep(tp.toward))
        def s0():
            push(tp.edge)
        def s1():
            if tp.L==2: return
            @pl.when(not_edge)
            def _():
                self.recv(1,FOLD)
                add_into(full, full, FOLD, 4, self.nr, 16)
            push(not_edge)
        def s2():
            @pl.when(tp.mid)
            def _():
                self.recv(2,MID)
                add_into(own, own, MID, 4, self.hr, 16)
            self.start(tp.mid, 0, own, XB, xp)
        def s3():
            @pl.when(tp.mid)
            def _():
                self.recv(0,XB)
                add_into(XB, own, XB, 4, self.hr, 16)
            self.final_out(h, XB)
        def s4():
            @pl.when(tp.mid)
            def _():
                self.final_wait(h, XB)
            self.start(tp.mid, 8, self.out_half(h), self.out_half(h), tp.rep(tp.toward))
            if tp.L>2: self.start(tp.mid, 6, self.out_half(h), self.out_half(h), tp.rep(tp.outward))
        def s5():
            @pl.when(tp.mid)
            def _():
                self.recv(8,self.out_half(1-h))
            if tp.L==2: return
            self.start(tp.mid, 7, self.out_half(1-h), self.out_half(1-h), tp.rep(tp.outward))
            @pl.when(not_mid)
            def _():
                self.recv(6,self.out_half(h))
            if tp.L>4: self.start(jnp.logical_and(not_mid,not_edge), 6, self.out_half(h), self.out_half(h), tp.rep(tp.outward))
        def s6():
            if tp.L==2: return
            @pl.when(not_mid)
            def _():
                self.recv(7,self.out_half(1-h))
            if tp.L>4: self.start(jnp.logical_and(not_mid,not_edge), 7, self.out_half(1-h), self.out_half(1-h), tp.rep(tp.outward))
        return [s0,s1,s2,s3,s4,s5,s6]

ARR=dict(gu=(256,1536,True,64), d=(192,1024,False,64), o=(128,1024,False,64), qkv=(256,1024,True,32))
ORDER=["d","gu","o","qkv"]

def plan():
    chunks=[]; i=0
    for n in ORDER:
        rows,W,sp,nr=ARR[n]
        for j in range(rows//nr):
            chunks.append((n,j,"A" if i%2==0 else "B")); i+=1
    return chunks

def scratch(chunks):
    scr=[]
    for n,j,k in chunks:
        rows,W,sp,nr=ARR[n]
        h=pltpu.VMEM((4,nr//2,W),BF); f=pltpu.VMEM((4,nr,W),BF)
        scr += [h,h,h] if k=="A" else [f,h,h]
    n=len(chunks)
    return scr+[pltpu.SemaphoreType.DMA((n*10,)),pltpu.SemaphoreType.DMA((n*10,))]

def make(S,R):
    chunks=plan(); nb=3*len(chunks)
    def kern(*refs):
        ins=dict(zip(ORDER,refs[:4])); outs=dict(zip(ORDER,refs[4:8]));
        G=dict(zip(ORDER,refs[8:12])); ld=refs[12]
        bufs=refs[13:13+nb]; send,recv=refs[13+nb:]
        tp=Topo(S,R)
        for i,n in enumerate(ORDER):
            pltpu.make_async_copy(ins[n],G[n],ld.at[i]).start()
        barrier(tp)
        for i,n in enumerate(ORDER):
            pltpu.make_async_copy(ins[n],G[n],ld.at[i]).wait()
        cs=[Chunk(tp,k,G[n],outs[n],j,ARR[n][3],ARR[n][2],bufs[3*i:3*i+3],(send,recv,i)) for i,(n,j,k) in enumerate(chunks)]
        ns=7
        for t in range(len(cs)+ns-1):
            for st in range(ns-1,-1,-1):
                i=t-st
                if 0<=i<len(cs): cs[i].steps[st]()
        for c in cs: c.drain()
    out_shape=[jax.ShapeDtypeStruct((ARR[n][0],4*ARR[n][1]) if ARR[n][2] else (4,ARR[n][0],ARR[n][1]),BF) for n in ORDER]
    any_=pl.BlockSpec(memory_space=pl.ANY)
    def call(*gs):
        return pl.pallas_call(kern,out_shape=out_shape,in_specs=[any_]*4,out_specs=[any_]*4,
            scratch_shapes=[pltpu.VMEM((4,ARR[n][0],ARR[n][1]),BF) for n in ORDER]+[pltpu.SemaphoreType.DMA((4,))]+scratch(chunks),
            compiler_params=pltpu.CompilerParams(collective_id=1,has_side_effects=True,vmem_limit_bytes=60<<20),name="grad_sum")(*gs)
    return call


class Net:
    def __init__(self, tp, send, recv):
        self.tp = tp
        self.send = send
        self.recv = recv
        self.k = 0
        self.live = []

    def slot(self):
        self.k += 1
        return self.k - 1

    def make(self, slot, src, dst, dev):
        return pltpu.make_async_remote_copy(
            src, dst, self.send.at[slot], self.recv.at[slot], device_id=dev, device_id_type=MESH
        )

    def push(self, slot, src, dst, dev):
        c = self.make(slot, src, dst, dev)
        c.start()
        self.live.append(c)
        return c

    def arrived(self, slot, ref):
        self.make(slot, ref, ref, self.tp.sh(1)).wait_recv()

    def drain(self):
        for c in self.live:
            c.wait_send()
        self.live = []


def dot(a, b, ca=1, cb=0):
    return lax.dot_general(a, b, (((ca,), (cb,)), ((), ())), preferred_element_type=F32)


def rows_of(t, rows, ch=0, ch_rows=None):
    n = rows if ch_rows is None else ch_rows
    start = t * rows + ch * n
    return pl.ds(start if isinstance(start, int) else pl.multiple_of(start, 128), n)


def fold8(v):
    out = v[0:8]
    for k in range(1, v.shape[0] // 8):
        out = out + v[8 * k : 8 * k + 8]
    return out


def layer_sizes(tokens, query_weight, key_weight, gate_weight, query_gain, shards):
    z = {}
    z["own"] = tokens.shape[0]
    z["D"] = tokens.shape[1]
    z["T"] = z["own"] * shards
    z["HD"] = query_gain.shape[0] * shards
    z["QW"] = query_weight.shape[1] // shards
    z["KW"] = key_weight.shape[1] // shards
    z["FW"] = gate_weight.shape[1] // shards
    return z


def layer_call(z, S, R, args):
    own, D, T, HD, QW, KW, FW = (z[k] for k in ("own", "D", "T", "HD", "QW", "KW", "FW"))
    QKV = QW + 2 * KW
    QK = QW + KW
    heads, kvs = QW // HD, KW // HD
    per = heads // kvs
    BLK = 128
    CH = 128
    NCH = own // CH
    TILE = 256
    scale = float(HD) ** -0.5
    SUB = 32
    GW = 2 * D + 2 * HD

    vm = lambda shape, dtype: pltpu.VMEM(shape, dtype)
    scratch = [
        vm((T // BLK, BLK, D), BF), vm((T // BLK, BLK, D), BF), vm((T // BLK, BLK, D), BF), vm((T // BLK, BLK, D), BF), vm((T, D), BF),
        vm((D, QKV), BF), vm((D, 2 * FW), BF), vm((QW, D), BF), vm((FW, D), BF),
        vm((S, 8, GW), F32), vm((8, GW), F32), vm((T, 2 * HD), F32),
        vm((T, QK), F32), vm((T, QKV), BF), vm((T, HD), F32), vm((T // BLK, BLK, QW), BF), vm((T, QW), BF),
        vm((2, NCH, CH, D), BF), vm((2, NCH, CH, D), BF), vm((NCH, CH, D), BF), vm((2, NCH, CH, D), BF),
        vm((NCH, CH, D), F32), vm((NCH, CH, D), F32), vm((own, D), F32), vm((own, D), BF),
        vm((T, FW), BF), vm((T, 2 * FW), BF), vm((T // BLK, BLK, QKV), BF), vm((T, QW), BF), vm((T, 2 * KW), F32),
        vm((own, FW), F32), vm((T, HD), F32), vm((8, GW), F32), vm((own, 2 * FW), F32),
        vm((own, D), BF), vm((own, D), F32),
        vm((FW, D), BF), vm((D, 2 * FW), BF), vm((QW, D), BF), vm((D, QKV), BF),
        pltpu.SemaphoreType.DMA((140,)), pltpu.SemaphoreType.DMA((140,)), pltpu.SemaphoreType.DMA((24,)),
    ]
    outs = [
        ((own, D), BF), ((own, D), F32), ((8, GW), F32),
        ((FW, D), BF), ((D, 2 * FW), BF), ((QW, D), BF), ((D, QKV), BF),
    ]

    def body(*refs):
        meta, tok_in, cot_in, gains_in, cs_in, wq_in, wk_in, wv_in, wo_in, wg_in, wu_in, wd_in = refs[:12]
        out_o, dx_o, gg_o, gd_o, ggu_o, go_o, gqkv_o = refs[12:19]
        (TOK, GB, N2, GMI, NP, WQKV, WGU, WO, WD, GAIN, GV, CS, RAW, HEADS, LSE, MIXP, MIXS,
         SBC, RBC, SBY, RBYS, HY, HO, HID, GH, ACT, DGU, DQKV, GMP, DKV, DQ, DQH, GG, X, OUTB, DX,
         GD, GGU, GO, GQKV, send, recv, lsem) = refs[19:]
        round_no = [0]
        tp = Topo(S, R)
        net = Net(tp, send, recv)
        s = tp.s
        lk = [0]
        locals_live = []

        def local(src, dst):
            c = pltpu.make_async_copy(src, dst, lsem.at[lk[0]])
            lk[0] += 1
            c.start()
            return c

        me = rows_of(s, own)
        c_tok = [local(tok_in.at[ch * CH : (ch + 1) * CH], TOK.at[NCH * s + ch]) for ch in range(NCH)]
        c_cot = local(cot_in, GH)
        c_gain = local(gains_in, GAIN.at[0])
        c_cs = local(cs_in, CS)
        c_wo = local(wo_in, WO)
        c_wd = local(wd_in, WD)

        def wcols(t):
            return (
                (wq_in, t * QW, QW, WQKV, 0),
                (wk_in, t * KW, KW, WQKV, QW),
                (wv_in, t * KW, KW, WQKV, QK),
                (wg_in, t * FW, FW, WGU, 0),
                (wu_in, t * FW, FW, WGU, FW),
            )

        c_w = []
        for ref, at, w, dst, to in wcols(s):
            c_w.append(
                local(ref.at[:, pl.ds(pl.multiple_of(at, 128), w)], dst.at[me, to : to + w])
            )
        barrier(tp)
        g_slot = [net.slot() for _ in range(3)]
        for k in (1, 2, 3):
            net.push(g_slot[k - 1], gains_in, GAIN.at[k], tp.sh(k))
        gath = {}

        def ag_push(name, buf, ch, src=None):
            r = NCH * s + ch
            k1, k2, k3 = net.slot(), net.slot(), net.slot()
            gath[name, ch] = (k1, k2, k3)
            src = buf.at[r] if src is None else src
            net.push(k2, src, buf.at[r], tp.sh(2))
            net.push(k1, src, buf.at[r], tp.sh(1))

        def ag_relay(name, buf, ch):
            k1, k2, k3 = gath[name, ch]
            r = NCH * (s ^ 2) + ch
            net.arrived(k2, buf.at[r])
            net.push(k3, buf.at[r], buf.at[r], tp.sh(1))

        def ag_near(name, buf, ch):
            net.arrived(gath[name, ch][0], buf.at[NCH * (s ^ 1) + ch])

        def ag_far(name, buf, ch):
            net.arrived(gath[name, ch][2], buf.at[NCH * (s ^ 3) + ch])

        for ch in range(NCH):
            ag_push("tok", TOK, ch, tok_in.at[ch * CH : (ch + 1) * CH])
        half = own // 2
        hb = tp.b * half
        wsl = {}

        def w_push(lo, hi):
            for k in (2, 3, 1):
                t = s ^ k
                for j, (ref, at, w, dst, to) in enumerate(wcols(t)):
                    if not lo <= j < hi:
                        continue
                    wsl[k, j] = net.slot()
                    cols = pl.ds(pl.multiple_of(at, 128), w)
                    if k == 1:
                        net.push(wsl[k, j], ref.at[:, cols], dst.at[me, to : to + w], tp.sh(k))
                    else:
                        src = ref.at[pl.ds(pl.multiple_of(hb, 128), half), cols]
                        r = pl.ds(pl.multiple_of(s * own + hb, 128), half)
                        net.push(wsl[k, j], src, dst.at[r, to : to + w], tp.sh(k))

        def w_relay(lo, hi):
            for k in (2, 3):
                for j, (ref, at, w, dst, to) in enumerate(wcols(s)):
                    if not lo <= j < hi:
                        continue
                    r = pl.ds(pl.multiple_of((s ^ k) * own + hb, 128), half)
                    part = dst.at[r, to : to + w]
                    net.arrived(wsl[k, j], part)
                    wsl[k + 2, j] = net.slot()
                    net.push(wsl[k + 2, j], part, part, tp.rep(tp.r ^ 1))

        def w_wait(lo, hi):
            for j, (ref, at, w, dst, to) in enumerate(wcols(s)):
                if not lo <= j < hi:
                    continue
                net.arrived(wsl[1, j], dst.at[rows_of(s ^ 1, own), to : to + w])
                for k in (2, 3):
                    r = pl.ds(pl.multiple_of((s ^ k) * own + (half - hb), 128), half)
                    net.arrived(wsl[k + 2, j], dst.at[r, to : to + w])

        w_push(0, 3)
        w_push(3, 5)
        c_cot.wait()
        length = meta[16]
        for ch in range(NCH):
            blk = meta[NCH * s + ch]
            def cot_rows(u, _, ch=ch, blk=blk):
                q = pl.multiple_of(u * SUB, SUB)
                pos = blk * BLK + q + lax.broadcasted_iota(jnp.int32, (SUB, D), 0)
                g = GH[pl.ds(ch * CH + q, SUB), :].astype(F32)
                GB[NCH * s + ch, pl.ds(q, SUB), :] = jnp.where(pos < length, g, 0.0).astype(BF)
                return 0

            lax.fori_loop(0, CH // SUB, cot_rows, 0)
            ag_push("gb", GB, ch)
        c_gain.wait()
        for k in (1, 2, 3):
            net.arrived(g_slot[k - 1], GAIN.at[k])
        GV[...] = GAIN[0] + GAIN[1] + GAIN[2] + GAIN[3]
        gain1 = GV[0:1, 0:D]
        gain2 = GV[0:1, D : 2 * D]
        gq = GV[0:1, 2 * D : 2 * D + HD]
        gk = GV[0:1, 2 * D + HD : GW]
        GG[...] = jnp.zeros_like(GG)
        DKV[...] = jnp.zeros_like(DKV)

        for c in c_tok:
            c.wait()
        for c in c_w:
            c.wait()
        for ch in range(NCH):
            ag_relay("tok", TOK, ch)
        w_relay(0, 3)
        for ch in range(NCH):
            ag_near("tok", TOK, ch)
            ag_far("tok", TOK, ch)

        def norm1(i, _):
            src = meta[8 + i]

            def sub(u, _):
                x = TOK[src, pl.ds(pl.multiple_of(u * SUB, SUB), SUB), :].astype(F32)
                r = lax.rsqrt(jnp.mean(x * x, axis=1, keepdims=True) + EPSILON)
                NP[pl.ds(pl.multiple_of(i * BLK + u * SUB, SUB), SUB), :] = (x * r * gain1).astype(BF)
                return 0

            return lax.fori_loop(0, BLK // SUB, sub, 0)

        lax.fori_loop(0, T // BLK, norm1, 0)
        w_wait(0, 3)
        c_cs.wait()

        def proj(i, _):
            r = rows_of(i, TILE)
            raw = dot(NP[r, :], WQKV[...])
            RAW[r, :] = raw[:, :QK]
            HEADS[r, QK:] = raw[:, QK:].astype(BF)

            def sub(u, _):
                rr = pl.ds(pl.multiple_of(i * TILE + u * SUB, SUB), SUB)
                co = CS[rr, 0:HD]
                si = CS[rr, HD : 2 * HD]
                for h in range(heads + kvs):
                    g = gq if h < heads else gk
                    v = RAW[rr, h * HD : (h + 1) * HD]
                    n = v * lax.rsqrt(jnp.mean(v * v, axis=1, keepdims=True) + EPSILON) * g
                    HEADS[rr, h * HD : (h + 1) * HD] = (
                        n * co + pltpu.roll(n, HD // 2, 1) * si
                    ).astype(BF)
                return 0

            return lax.fori_loop(0, TILE // SUB, sub, 0)

        lax.fori_loop(0, T // TILE, proj, 0)

        lane = lax.broadcasted_iota(jnp.int32, (TILE, HD), 1)
        tri = lax.broadcasted_iota(jnp.int32, (TILE, TILE), 1) <= lax.broadcasted_iota(
            jnp.int32, (TILE, TILE), 0
        )

        def masked_scores(q, h_kv_cols, i):
            k = HEADS[0 : (i + 1) * TILE, h_kv_cols]
            sc = dot(q, k, 1, 1) * scale
            last = jnp.where(tri, sc[:, i * TILE :], -1e30)
            return last if i == 0 else jnp.concatenate([sc[:, : i * TILE], last], axis=1)

        def head_cols(h):
            return pl.ds(pl.multiple_of(h * HD, HD), HD)

        def attend(h, _):
            kv = h // per if isinstance(h, int) else lax.div(h, per)
            kc = pl.ds(pl.multiple_of(QW + kv * HD, HD), HD)
            vc = pl.ds(pl.multiple_of(QK + kv * HD, HD), HD)
            for i in range(T // TILE):
                r = rows_of(i, TILE)
                sc = masked_scores(HEADS[r, head_cols(h)], kc, i)
                top = jnp.max(sc, axis=1, keepdims=True)
                e = jnp.exp(sc - top)
                total = jnp.sum(e, axis=1, keepdims=True)
                o = dot(e.astype(BF), HEADS[0 : (i + 1) * TILE, vc]) / total
                MIXP[i * (TILE // BLK) : (i + 1) * (TILE // BLK), :, head_cols(h)] = o.astype(BF).reshape(
                    TILE // BLK, BLK, HD
                )
                lse = top + jnp.log(total)
                LSE[r, :] = jnp.where(lane == h, lse, LSE[r, :])
            return 0

        LSE[...] = jnp.zeros_like(LSE)
        lax.fori_loop(0, heads, attend, 0)
        c_wo.wait()

        def reduce_scatter(partial):
            c_slot = [[net.slot() for _ in range(NCH)] for _ in range(2)]
            y_slot = [net.slot() for _ in range(NCH)]
            round_no[0] += 1
            RBY = RBYS.at[round_no[0] % 2]
            for ch in range(NCH):
                SBC[0, ch] = partial(s ^ 3, ch).astype(BF)
                net.push(c_slot[0][ch], SBC.at[0, ch], RBC.at[0, ch], tp.sh(1))
            for ch in range(NCH):
                HY[ch] = partial(s ^ 2, ch)
            for ch in range(NCH):
                net.arrived(c_slot[0][ch], RBC.at[0, ch])
                SBY[ch] = (HY[ch] + RBC[0, ch].astype(F32)).astype(BF)
                net.push(y_slot[ch], SBY.at[ch], RBY.at[ch], tp.sh(2))
            for ch in range(NCH):
                SBC[1, ch] = partial(s ^ 1, ch).astype(BF)
                net.push(c_slot[1][ch], SBC.at[1, ch], RBC.at[1, ch], tp.sh(1))
            for ch in range(NCH):
                HO[ch] = partial(s, ch)
            for ch in range(NCH):
                net.arrived(c_slot[1][ch], RBC.at[1, ch])
                HO[ch] = HO[ch] + RBC[1, ch].astype(F32)
            return y_slot

        def rs_finish(y_slot, ch):
            RBY = RBYS.at[round_no[0] % 2]
            net.arrived(y_slot[ch], RBY.at[ch])
            HO[ch] = HO[ch] + RBY[ch].astype(F32)

        def mixed_rows(t, ch):
            src = meta[NCH * t + ch]
            v = MIXP[src]
            MIXS[rows_of(t, own, ch, CH), :] = v
            return dot(v, WO[...])

        w_relay(3, 5)
        ys = reduce_scatter(mixed_rows)
        for ch in range(NCH):
            ag_relay("gb", GB, ch)
        for ch in range(NCH):
            rs_finish(ys, ch)

            def norm2(u, _, ch=ch):
                q = pl.ds(pl.multiple_of(u * SUB, SUB), SUB)
                x = TOK[NCH * s + ch, q, :].astype(F32) + HO[ch, q, :]
                HID[pl.ds(pl.multiple_of(ch * CH + u * SUB, SUB), SUB), :] = x
                r = lax.rsqrt(jnp.mean(x * x, axis=1, keepdims=True) + EPSILON)
                N2[NCH * s + ch, q, :] = (x * r * gain2).astype(BF)
                return 0

            lax.fori_loop(0, CH // SUB, norm2, 0)
            ag_push("n2", N2, ch)
        c_wd.wait()
        w_wait(3, 5)
        for ch in range(NCH):
            ag_near("gb", GB, ch)
            ag_far("gb", GB, ch)

        def ffn(t):
            two = pl.ds(NCH * t, NCH)
            X[...] = dot(N2[two].reshape(own, D), WGU[...])
            DQ[...] = dot(GB[two].reshape(own, D), WD[...], 1, 1)

            def sub(u, _):
                q = pl.ds(pl.multiple_of(u * SUB, SUB), SUB)
                at = pl.ds(pl.multiple_of(t * own + u * SUB, SUB), SUB)
                for c in range(0, FW, 256):
                    gate = X[q, c : c + 256]
                    up = X[q, FW + c : FW + c + 256]
                    ga = DQ[q, c : c + 256]
                    sig = 1.0 / (1.0 + jnp.exp(-gate))
                    act = gate * sig
                    ACT[at, c : c + 256] = (act * up).astype(BF)
                    DGU[at, c : c + 256] = (ga * up * (sig * (1.0 + gate * (1.0 - sig)))).astype(BF)
                    DGU[at, FW + c : FW + c + 256] = (ga * act).astype(BF)
                return 0

            lax.fori_loop(0, own // SUB, sub, 0)

        ffn(s)
        for ch in range(NCH):
            ag_near("n2", N2, ch)
        ffn(s ^ 1)
        for ch in range(NCH):
            ag_relay("n2", N2, ch)
        ffn(s ^ 2)
        for ch in range(NCH):
            ag_far("n2", N2, ch)
        ffn(s ^ 3)
        net.drain()

        ys = reduce_scatter(
            lambda t, ch: dot(DGU[rows_of(t, own, ch, CH), :], WGU[...], 1, 1)
        )

        def wgrad(left, right, out, lw, rw):
            def step(i, _):
                cols = pl.ds(pl.multiple_of(i * 256, 256), 256)
                lhs = left[:, :, cols] if len(left.shape) == 3 else left[:, cols]
                rhs = right[...].reshape(T, rw)
                out[cols, :] = dot(lhs.reshape(T, 256), rhs, 0, 0).astype(BF)
                return 0

            lax.fori_loop(0, lw // 256, step, 0)

        wgrad(ACT, GB, GD, FW, D)
        for ch in range(NCH):
            rs_finish(ys, ch)

            def norm2_back(u, acc, ch=ch):
                q = pl.ds(pl.multiple_of(u * SUB, SUB), SUB)
                qo = pl.ds(pl.multiple_of(ch * CH + u * SUB, SUB), SUB)
                x = HID[qo, :]
                du = HO[ch, q, :]
                r = lax.rsqrt(jnp.mean(x * x, axis=1, keepdims=True) + EPSILON)
                gd = du * gain2
                m = jnp.mean(x * gd, axis=1, keepdims=True)
                gh = GB[NCH * s + ch, q, :].astype(F32) + r * gd - x * (r * r * r * m)
                DX[qo, :] = gh
                GMI[NCH * s + ch, q, :] = gh.astype(BF)
                GG[:, D : 2 * D] = GG[:, D : 2 * D] + fold8(du * x * r)
                return acc

            lax.fori_loop(0, CH // SUB, norm2_back, 0)
            ag_push("gmi", GMI, ch)
        wgrad(N2, DGU, GGU, D, 2 * FW)
        for ch in range(NCH):
            ag_relay("gmi", GMI, ch)
        for ch in range(NCH):
            ag_near("gmi", GMI, ch)
            ag_far("gmi", GMI, ch)

        def gmix(i, _):
            a = GMI[meta[8 + 2 * i]]
            b = GMI[meta[9 + 2 * i]]
            GMP[rows_of(i, TILE), :] = dot(
                jnp.concatenate([a, b], axis=0), WO[...], 1, 1
            ).astype(BF)
            return 0

        lax.fori_loop(0, T // TILE, gmix, 0)
        wgrad(MIXS, GMI, GO, QW, D)
        net.drain()
        ys = reduce_scatter(lambda t, ch: dot(ACT[rows_of(t, own, ch, CH), :], WD[...]))

        def head_back(v, du, g):
            r = lax.rsqrt(jnp.mean(v * v, axis=1, keepdims=True) + EPSILON)
            gd = du * g
            m = jnp.mean(v * gd, axis=1, keepdims=True)
            return r * gd - v * (r * r * r * m), fold8(du * v * r)

        def unrotate(g, rr):
            return g * CS[rr, 0:HD] + pltpu.roll(g * CS[rr, HD : 2 * HD], HD // 2, 1)

        def attend_back(h, _):
            kv = lax.div(h, per)
            kc = pl.ds(pl.multiple_of(QW + kv * HD, HD), HD)
            vc = pl.ds(pl.multiple_of(QK + kv * HD, HD), HD)
            dk = pl.ds(pl.multiple_of(kv * HD, HD), HD)
            dv = pl.ds(pl.multiple_of(KW + kv * HD, HD), HD)
            for i in range(T // TILE):
                r = rows_of(i, TILE)
                n = (i + 1) * TILE
                q = HEADS[r, head_cols(h)]
                gm = GMP[r, head_cols(h)]
                lse = jnp.sum(jnp.where(lane == h, LSE[r, :], 0.0), axis=1, keepdims=True)
                p = jnp.exp(masked_scores(q, kc, i) - lse)
                gp = dot(gm, HEADS[0:n, vc], 1, 1)
                inner = jnp.sum(p * gp, axis=1, keepdims=True)
                ds = (p * (gp - inner)).astype(BF)
                DKV[0:n, dv] = DKV[0:n, dv] + dot(p.astype(BF), gm, 0, 0)
                DKV[0:n, dk] = DKV[0:n, dk] + dot(ds, q, 0, 0) * scale
                DQH[r, :] = dot(ds, HEADS[0:n, kc]) * scale
            def sub(u, _):
                rr = pl.ds(pl.multiple_of(u * SUB, SUB), SUB)
                lr = pl.ds(pl.multiple_of(lax.rem(u, BLK // SUB) * SUB, SUB), SUB)
                d, gg = head_back(RAW[rr, head_cols(h)], unrotate(DQH[rr, :], rr), gq)
                DQKV[lax.div(u, BLK // SUB), lr, head_cols(h)] = d.astype(BF)
                GG[:, 2 * D : 2 * D + HD] = GG[:, 2 * D : 2 * D + HD] + gg
                return 0

            lax.fori_loop(0, T // SUB, sub, 0)
            return 0

        lax.fori_loop(0, heads, attend_back, 0)

        def key_back(u, _):
            rr = pl.ds(pl.multiple_of(u * SUB, SUB), SUB)
            lb = lax.div(u, BLK // SUB)
            lr = pl.ds(pl.multiple_of(lax.rem(u, BLK // SUB) * SUB, SUB), SUB)
            for kv in range(kvs):
                c = slice(QW + kv * HD, QW + (kv + 1) * HD)
                d, gg = head_back(
                    RAW[rr, c], unrotate(DKV[rr, kv * HD : (kv + 1) * HD], rr), gk
                )
                DQKV[lb, lr, c] = d.astype(BF)
                GG[:, 2 * D + HD : GW] = GG[:, 2 * D + HD : GW] + gg
            DQKV[lb, lr, QK:QKV] = DKV[rr, KW : 2 * KW].astype(BF)
            return 0

        lax.fori_loop(0, T // SUB, key_back, 0)
        for ch in range(NCH):
            rs_finish(ys, ch)

            def out_rows(u, _, ch=ch):
                q = pl.ds(pl.multiple_of(u * SUB, SUB), SUB)
                qo = pl.ds(pl.multiple_of(ch * CH + u * SUB, SUB), SUB)
                OUTB[qo, :] = (HID[qo, :] + HO[ch, q, :]).astype(BF)
                return 0

            lax.fori_loop(0, CH // SUB, out_rows, 0)
        c_out = local(OUTB, out_o)
        net.drain()

        def back_rows(t, ch):
            src = meta[NCH * t + ch]
            return dot(DQKV[src], WQKV[...], 1, 1)

        ys = reduce_scatter(back_rows)

        def wgrad_qkv(i, _):
            cols = pl.ds(pl.multiple_of(i * 256, 256), 256)
            GQKV[cols, :] = dot(NP[:, cols], DQKV[...].reshape(T, QKV), 0, 0).astype(BF)
            return 0

        lax.fori_loop(0, D // 256, wgrad_qkv, 0)
        for ch in range(NCH):
            rs_finish(ys, ch)

            def norm1_back(u, acc, ch=ch):
                q = pl.ds(pl.multiple_of(u * SUB, SUB), SUB)
                qo = pl.ds(pl.multiple_of(ch * CH + u * SUB, SUB), SUB)
                x = TOK[NCH * s + ch, q, :].astype(F32)
                du = HO[ch, q, :]
                r = lax.rsqrt(jnp.mean(x * x, axis=1, keepdims=True) + EPSILON)
                gd = du * gain1
                m = jnp.mean(x * gd, axis=1, keepdims=True)
                DX[qo, :] = DX[qo, :] + r * gd - x * (r * r * r * m)
                GG[:, 0:D] = GG[:, 0:D] + fold8(du * x * r)
                return acc

            lax.fori_loop(0, CH // SUB, norm1_back, 0)
        c_dx = local(DX, dx_o)
        c_gg = local(GG, gg_o)
        cg = [local(a, b) for a, b in ((GD, gd_o), (GGU, ggu_o), (GO, go_o), (GQKV, gqkv_o))]
        for c in [c_out, c_dx, c_gg] + cg:
            c.wait()
        net.drain()

    any_ = pl.BlockSpec(memory_space=pl.ANY)
    specs = [pl.BlockSpec(memory_space=pltpu.SMEM)] + [any_] * 11
    return pl.pallas_call(
        body,
        out_shape=[jax.ShapeDtypeStruct(*o) for o in outs],
        in_specs=specs,
        out_specs=[any_] * len(outs),
        scratch_shapes=scratch,
        compiler_params=pltpu.CompilerParams(
            collective_id=2, has_side_effects=True, vmem_limit_bytes=64 << 20
        ),
        name="layer",
    )(*args)


def rotary_table(slot_len, head_width):
    middle = head_width // 2
    inverse = np.power(ROPE_BASE, -np.arange(middle) * 2.0 / head_width).astype(np.float32)
    phases = np.arange(slot_len, dtype=np.float32)[:, None] * inverse
    cosine = np.cos(phases.astype(np.float64))
    sine = np.sin(phases.astype(np.float64))
    table = np.concatenate([cosine, cosine, -sine, sine], axis=1)
    return table.astype(np.float32)


def shards(
    tokens,
    cotangent,
    lengths,
    block_order,
    norm1_gain,
    query_weight,
    key_weight,
    value_weight,
    output_weight,
    query_gain,
    key_gain,
    norm2_gain,
    gate_weight,
    up_weight,
    down_weight,
):
    S, R = lax.axis_size("shard"), lax.axis_size("replica")
    at = lax.axis_index("shard")
    z = layer_sizes(tokens[0], query_weight, key_weight, gate_weight, query_gain, S)
    D, HD = z["D"], z["HD"]
    gains = jnp.zeros((8, 2 * D + 2 * HD), F32)
    start = 0
    for g, full in ((norm1_gain, D), (norm2_gain, D), (query_gain, HD), (key_gain, HD)):
        gains = lax.dynamic_update_slice(
            gains, g.astype(F32)[None], (0, start + at * g.shape[0])
        )
        start += full
    order = block_order[0]
    count = order.shape[0]
    place = jnp.arange(count, dtype=jnp.int32)
    inverse = jnp.sum(jnp.where(order[None, :] == place[:, None], place[None, :], 0), axis=1)
    meta = jnp.concatenate([order, inverse, lengths, jnp.zeros((15,), jnp.int32)])
    table = jnp.asarray(rotary_table(z["T"], HD))
    out, dx, gg, gd, ggu, go, gqkv = layer_call(
        z, S, R,
        (meta, tokens[0], cotangent[0], gains, table, query_weight, key_weight, value_weight,
         output_weight, gate_weight, up_weight, down_weight),
    )
    block = z["T"] // count
    mine_blocks = lax.dynamic_slice_in_dim(order, at * (z["own"] // block), z["own"] // block)
    position = mine_blocks[:, None] * block + jnp.arange(block, dtype=jnp.int32)[None, :]
    valid = position.reshape(-1, 1) < lengths[0]
    out = jnp.where(valid, out, jnp.zeros_like(out))
    share = {"d": gd, "gu": ggu, "o": go, "qkv": gqkv}
    share = {k: v.reshape(S, v.shape[0] // S, v.shape[1]) for k, v in share.items()}
    sums = dict(zip(ORDER, make(S, R)(*[share[n] for n in ORDER])))
    grad_down = sums["d"].astype(F32).reshape(-1, D)
    grad_output_w = sums["o"].astype(F32).reshape(-1, D)

    def columns(v, first, width):
        v = v.reshape(v.shape[0], S, -1)[:, :, first : first + width]
        return v.reshape(v.shape[0], -1).astype(F32)

    FW, QW, KW = z["FW"], z["QW"], z["KW"]
    small = lax.psum(jnp.sum(gg, axis=0), ("shard", "replica"))

    def mine(first, size):
        return lax.dynamic_slice_in_dim(small, first + at * size, size)

    return (
        out[None],
        dx[None],
        mine(0, D // S),
        columns(sums["qkv"], 0, QW),
        columns(sums["qkv"], QW, KW),
        columns(sums["qkv"], QW + KW, KW),
        grad_output_w,
        mine(2 * D, HD // S),
        mine(2 * D + HD, HD // S),
        mine(D, D // S),
        columns(sums["gu"], 0, FW),
        columns(sums["gu"], FW, FW),
        grad_down,
    )


def solution(mesh):
    rows, mat, vec = P("replica", "shard", None), P("shard", None), P("shard")
    placed = (rows, rows, P("replica"), P("replica", None), vec, mat, mat, mat, mat)
    placed += (vec, vec, vec, mat, mat, mat)
    outs = (rows, rows, vec, mat, mat, mat, mat, vec, vec, vec, mat, mat, mat)
    return jax.shard_map(shards, mesh=mesh, in_specs=placed, out_specs=outs, check_vma=False)
```

```python
import functools

import jax
import jax.numpy as jnp
import numpy as np
from jax import lax
from jax.experimental import pallas as pl
from jax.experimental.pallas import tpu as pltpu
from jax.sharding import PartitionSpec as P

EPSILON = 1e-06
ROPE_BASE = 1000000.0
BF = jnp.bfloat16
F32 = jnp.float32
MESH = pl.DeviceIdType.MESH


class Topo:
    def __init__(self, shards, replicas):
        self.S = shards
        self.R = replicas
        self.L = replicas // 2
        self.s = lax.axis_index("shard")
        r = lax.axis_index("replica")
        self.r = r
        L = self.L
        a = lax.div(r, 2)
        self.b = lax.rem(r, 2)
        left = a <= L // 2 - 1
        self.mid = jnp.logical_or(a == L // 2 - 1, a == L // 2)
        self.edge = jnp.logical_or(a == 0, a == L - 1)
        self.inner = jnp.logical_not(self.edge)
        self.side = jnp.logical_not(self.mid)
        self.toward = jnp.where(left, r + 2, r - 2)
        self.outward = jnp.where(left, r - 2, r + 2)
        self.h = jnp.where(left, 0, 1)

    def rep(self, r):
        return (self.s, r)

    def sh(self, k):
        return (self.s ^ k, self.r)


def barrier(tp):
    bar = pltpu.get_barrier_semaphore()
    ids = [tp.rep(lax.rem(tp.r + k, tp.R)) for k in range(1, tp.R)]
    ids += [tp.sh(1), tp.sh(2), tp.sh(3)]
    for d in ids:
        pl.semaphore_signal(bar, inc=1, device_id=d, device_id_type=MESH)
    pl.semaphore_wait(bar, len(ids))


def add_rows(dst, a, b):
    blocks, parts, rows, _ = a.shape

    def body(i, _):
        q = pl.ds(pl.multiple_of(i * 16, 16), 16)
        for w in range(blocks):
            for t in range(parts):
                dst[w, t, q, :] = (a[w, t, q, :].astype(F32) + b[w, t, q, :].astype(F32)).astype(BF)
        return 0

    lax.fori_loop(0, rows // 16, body, 0)


class Chunk:
    def __init__(self, tp, kind, G, out, base, nr, spread, bufs, send, recv, at):
        self.tp, self.G, self.out, self.base, self.nr, self.hr = tp, G, out, base, nr, nr // 2
        self.spread, self.bufs, self.send, self.recv_sem, self.at = spread, bufs, send, recv, at
        self.W = G.shape[3]
        self.sent = []
        self.steps = self.steps_a() if kind == "A" else self.steps_b()

    def rows(self, h):
        return pl.ds(pl.multiple_of(self.base + h * self.hr, 16), self.hr)

    def half(self, h):
        return self.G.at[:, :, self.rows(h), :]

    def out_half(self, h):
        return self.out.at[:, self.rows(h), :] if self.spread else self.out.at[:, :, self.rows(h), :]

    def out_piece(self, h, s):
        return self.out.at[:, self.rows(h), pl.ds(pl.multiple_of(s * self.W, 128), self.W)]

    def copy(self, slot, src, dst, dev):
        k = self.at + slot
        return pltpu.make_async_remote_copy(
            src, dst, self.send.at[k], self.recv_sem.at[k], device_id=dev, device_id_type=MESH
        )

    def start(self, cond, slot, src, dst, dev):
        c = self.copy(slot, src, dst, dev)
        if cond is None:
            c.start()
        else:
            pl.when(cond)(lambda: c.start())
        self.sent.append((cond, c))

    def drain(self):
        for cond, c in self.sent:
            if cond is None:
                c.wait_send()
            else:
                pl.when(cond)(lambda c=c: c.wait_send())

    def arrived(self, slot, ref):
        self.copy(slot, ref, ref, self.tp.rep(self.tp.r ^ 1)).wait_recv()

    def local(self, src, dst):
        return pltpu.make_async_copy(src, dst, self.send.at[self.at + 9])

    def final_out(self, h, F):
        tp = self.tp
        if self.spread:
            for k in (1, 2, 3):
                self.start(tp.mid, 2 + k, F.at[:, tp.s ^ k], self.out_piece(h, tp.s), tp.sh(k))

        @pl.when(tp.mid)
        def _():
            if self.spread:
                self.local(F.at[:, tp.s], self.out_piece(h, tp.s)).start()
            else:
                self.local(F, self.out_half(h)).start()

    def final_wait(self, h, F):
        tp = self.tp
        if self.spread:
            for k in (1, 2, 3):
                self.arrived(2 + k, self.out_piece(h, tp.s ^ k))
            self.local(F.at[:, tp.s], self.out_piece(h, tp.s)).wait()
        else:
            self.local(F, self.out_half(h)).wait()

    def steps_a(self):
        tp = self.tp
        b = tp.b
        RX, FOLD, MID = self.bufs
        xp = tp.rep(tp.r ^ 1)
        own = self.half(b)
        both = jnp.logical_and

        def onward(cond):
            self.start(both(cond, tp.mid), 2, own, MID, tp.rep(tp.toward))
            if tp.L > 2:
                self.start(both(cond, tp.side), 1, own, FOLD, tp.rep(tp.toward))

        def s0():
            self.start(None, 0, self.half(1 - b), RX, xp)

        def s1():
            self.arrived(0, RX)
            add_rows(own, own, RX)
            onward(tp.edge)

        def s2():
            if tp.L == 2:
                return

            @pl.when(tp.inner)
            def _():
                self.arrived(1, FOLD)
                add_rows(own, own, FOLD)

            onward(tp.inner)

        def s3():
            @pl.when(tp.mid)
            def _():
                self.arrived(2, MID)
                add_rows(MID, own, MID)

            self.final_out(b, MID)

        def s4():
            pl.when(tp.mid)(lambda: self.final_wait(b, MID))
            if tp.L > 2:
                self.start(tp.mid, 6, self.out_half(b), self.out_half(b), tp.rep(tp.outward))
            self.start(tp.mid, 7, self.out_half(b), self.out_half(b), xp)

        def s5():
            if tp.L == 2:
                return
            pl.when(tp.side)(lambda: self.arrived(6, self.out_half(b)))
            if tp.L > 4:
                self.start(
                    both(tp.side, tp.inner), 6, self.out_half(b), self.out_half(b), tp.rep(tp.outward)
                )
            self.start(tp.side, 7, self.out_half(b), self.out_half(b), xp)

        def s6():
            self.arrived(7, self.out_half(1 - b))

        return [s0, s1, s2, s3, s4, s5, s6]

    def steps_b(self):
        tp = self.tp
        h = tp.h
        FOLD, MID, XB = self.bufs
        xp = tp.rep(tp.r ^ 1)
        own, other = self.half(h), self.half(1 - h)
        full = self.G.at[:, :, self.base : self.base + self.nr, :]
        both = jnp.logical_and

        def onward(cond):
            self.start(both(cond, tp.mid), 2, other, MID, tp.rep(tp.toward))
            if tp.L > 2:
                self.start(both(cond, tp.side), 1, full, FOLD, tp.rep(tp.toward))

        def s0():
            onward(tp.edge)

        def s1():
            if tp.L == 2:
                return

            @pl.when(tp.inner)
            def _():
                self.arrived(1, FOLD)
                add_rows(full, full, FOLD)

            onward(tp.inner)

        def s2():
            @pl.when(tp.mid)
            def _():
                self.arrived(2, MID)
                add_rows(own, own, MID)

            self.start(tp.mid, 0, own, XB, xp)

        def s3():
            @pl.when(tp.mid)
            def _():
                self.arrived(0, XB)
                add_rows(XB, own, XB)

            self.final_out(h, XB)

        def s4():
            pl.when(tp.mid)(lambda: self.final_wait(h, XB))
            self.start(tp.mid, 8, self.out_half(h), self.out_half(h), tp.rep(tp.toward))
            if tp.L > 2:
                self.start(tp.mid, 6, self.out_half(h), self.out_half(h), tp.rep(tp.outward))

        def s5():
            pl.when(tp.mid)(lambda: self.arrived(8, self.out_half(1 - h)))
            if tp.L == 2:
                return
            self.start(tp.mid, 7, self.out_half(1 - h), self.out_half(1 - h), tp.rep(tp.outward))
            pl.when(tp.side)(lambda: self.arrived(6, self.out_half(h)))
            if tp.L > 4:
                self.start(
                    both(tp.side, tp.inner), 6, self.out_half(h), self.out_half(h), tp.rep(tp.outward)
                )

        def s6():
            if tp.L == 2:
                return
            pl.when(tp.side)(lambda: self.arrived(7, self.out_half(1 - h)))
            if tp.L > 4:
                self.start(
                    both(tp.side, tp.inner),
                    7,
                    self.out_half(1 - h),
                    self.out_half(1 - h),
                    tp.rep(tp.outward),
                )

        return [s0, s1, s2, s3, s4, s5, s6]


class Ticks:
    def __init__(self, chunks, stride):
        self.chunks, self.stride, self.t = chunks, stride, 0
        self.end = len(chunks) + 6 * stride

    def run(self, count=1):
        for _ in range(count):
            if self.t >= self.end:
                return
            for k in range(6, -1, -1):
                i = self.t - k * self.stride
                if 0 <= i < len(self.chunks):
                    self.chunks[i].steps[k]()
            self.t += 1

    def finish(self):
        self.run(self.end - self.t)
        for c in self.chunks:
            c.drain()


class Net:
    def __init__(self, tp, send, recv):
        self.tp = tp
        self.send = send
        self.recv = recv
        self.k = 0
        self.live = []

    def slot(self):
        self.k += 1
        return self.k - 1

    def make(self, slot, src, dst, dev):
        return pltpu.make_async_remote_copy(
            src, dst, self.send.at[slot], self.recv.at[slot], device_id=dev, device_id_type=MESH
        )

    def push(self, slot, src, dst, dev):
        c = self.make(slot, src, dst, dev)
        c.start()
        self.live.append(c)
        return c

    def arrived(self, slot, ref):
        self.make(slot, ref, ref, self.tp.sh(1)).wait_recv()

    def drain(self):
        for c in self.live:
            c.wait_send()
        self.live = []


def dot(a, b, ca=1, cb=0):
    return lax.dot_general(a, b, (((ca,), (cb,)), ((), ())), preferred_element_type=F32)


def rows_of(t, rows, ch=0, ch_rows=None):
    n = rows if ch_rows is None else ch_rows
    start = t * rows + ch * n
    return pl.ds(start if isinstance(start, int) else pl.multiple_of(start, 128), n)


def fold8(v):
    out = v[0:8]
    for k in range(1, v.shape[0] // 8):
        out = out + v[8 * k : 8 * k + 8]
    return out


def layer_sizes(tokens, query_weight, key_weight, gate_weight, query_gain, shards):
    z = {}
    z["own"] = tokens.shape[0]
    z["D"] = tokens.shape[1]
    z["T"] = z["own"] * shards
    z["HD"] = query_gain.shape[0] * shards
    z["QW"] = query_weight.shape[1] // shards
    z["KW"] = key_weight.shape[1] // shards
    z["FW"] = gate_weight.shape[1] // shards
    return z


def layer_call(z, S, R, args):
    own, D, T, HD, QW, KW, FW = (z[k] for k in ("own", "D", "T", "HD", "QW", "KW", "FW"))
    QKV = QW + 2 * KW
    QK = QW + KW
    heads, kvs = QW // HD, KW // HD
    per = heads // kvs
    BLK = 128
    CH = 128
    NCH = own // CH
    TILE = 256
    scale = float(HD) ** -0.5
    SUB = 32
    GW = 2 * D + 2 * HD
    GN = 2 * own + 2 * HD

    vm = lambda shape, dtype: pltpu.VMEM(shape, dtype)
    scratch = [
        vm((T // BLK, BLK, D), BF), vm((T // BLK, BLK, D), BF), vm((T // BLK, BLK, D), BF), vm((T, D), BF),
        vm((D, QKV), BF), vm((D, 2 * FW), BF), vm((QW, D), BF), vm((FW, D), BF),
        vm((S, 8, GW), F32), vm((8, GW), F32), vm((T, 2 * HD), F32),
        vm((T, QK), BF), vm((T, QKV), BF), vm((T, HD), F32), vm((T // BLK, BLK, QW), BF), vm((T, QW), BF),
        vm((2, NCH, CH, D), BF), vm((2, NCH, CH, D), BF), vm((NCH, CH, D), BF), vm((2, NCH, CH, D), BF),
        vm((NCH, CH, D), F32), vm((own, D), F32), vm((own, D), BF),
        vm((T, FW), BF), vm((T // BLK, BLK, 2 * FW), BF), vm((T, 2 * KW), F32),
        vm((TILE, HD), F32), vm((8, GW), F32), vm((own, max(QK, 768)), F32),
        vm((own, D), F32),
        vm((S, 8, GN), F32),
        pltpu.SemaphoreType.DMA((160,)), pltpu.SemaphoreType.DMA((160,)), pltpu.SemaphoreType.DMA((24,)),
    ]
    grads = [
        ((1, S, FW // S, D), 32, False),
        ((2, S, D // S, FW), 32, True),
        ((1, S, QW // S, D), 32, False),
        ((1, S, D // S, QW), 64, True),
        ((2, S, D // S, KW), 64, True),
    ]
    outs = [((own, D), BF), ((own, D), F32), ((R, 8, GN), F32)]
    FIXED = len(scratch)
    plan = []
    for j, (shape, nr, spread) in enumerate(grads):
        w, _, rows, width = shape
        outs.append(((w, rows, S * width) if spread else shape, BF))
        scratch.append(vm(shape, BF))
        for base in range(0, rows, nr):
            plan.append((j, base, "AB"[len(plan) % 2]))
    for j, base, kind in plan:
        (w, _, rows, width), nr, _ = grads[j]
        half = vm((w, S, nr // 2, width), BF)
        scratch += [half, half, half] if kind == "A" else [vm((w, S, nr, width), BF), half, half]
    sems = pltpu.SemaphoreType.DMA((10 * len(plan),))
    scratch += [sems, sems]

    def body(*refs):
        meta, tok_in, cot_in, gains_in, cs_in, wq_in, wk_in, wv_in, wo_in, wg_in, wu_in, wd_in = refs[:12]
        out_o, dx_o, gg_o = refs[12:15]
        grad_o = refs[15:20]
        (TOK, GB, N2, NP, WQKV, WGU, WO, WD, GAIN, GV, CS, RAW, HEADS, LSE, MIXP, MIXS,
         SBC, RBC, SBY, RBYS, HO, HID, GH, ACT, DGU, DKV, DQH, GG, X, DX,
         GS, send, recv, lsem) = refs[20:20 + FIXED]
        G = refs[20 + FIXED : 25 + FIXED]
        GD, GGU, GO, GQ, GKV = G
        bufs = refs[25 + FIXED : -2]
        GMI, GMP, DQKV = TOK, MIXP, DGU
        round_no = [0]
        tp = Topo(S, R)
        net = Net(tp, send, recv)
        chunks = []
        for i, (j, base, kind) in enumerate(plan):
            shape, nr, spread = grads[j]
            chunks.append(
                Chunk(tp, kind, G[j], grad_o[j], base, nr, spread, bufs[3 * i : 3 * i + 3], refs[-2], refs[-1], 10 * i)
            )
        ticks = Ticks(chunks, 2)
        s = tp.s
        lk = [0]
        locals_live = []

        def local(src, dst):
            c = pltpu.make_async_copy(src, dst, lsem.at[lk[0]])
            lk[0] += 1
            c.start()
            return c

        me = rows_of(s, own)
        c_tok = [local(tok_in.at[ch * CH : (ch + 1) * CH], TOK.at[NCH * s + ch]) for ch in range(NCH)]
        c_cot = local(cot_in, GH)
        c_gain = local(gains_in, GAIN.at[0])
        c_cs = local(cs_in, CS)
        c_wo = local(wo_in, WO)
        c_wd = local(wd_in, WD)

        def wcols(t):
            return (
                (wq_in, t * QW, QW, WQKV, 0),
                (wk_in, t * KW, KW, WQKV, QW),
                (wv_in, t * KW, KW, WQKV, QK),
                (wg_in, t * FW, FW, WGU, 0),
                (wu_in, t * FW, FW, WGU, FW),
            )

        c_w = []
        for ref, at, w, dst, to in wcols(s):
            c_w.append(
                local(ref.at[:, pl.ds(pl.multiple_of(at, 128), w)], dst.at[me, to : to + w])
            )
        barrier(tp)
        g_slot = [net.slot() for _ in range(3)]
        for k in (1, 2, 3):
            net.push(g_slot[k - 1], gains_in, GAIN.at[k], tp.sh(k))
        gath = {}

        def ag_push(name, buf, ch, src=None):
            r = NCH * s + ch
            k1, k2, k3 = net.slot(), net.slot(), net.slot()
            gath[name, ch] = (k1, k2, k3)
            src = buf.at[r] if src is None else src
            net.push(k2, src, buf.at[r], tp.sh(2))
            net.push(k1, src, buf.at[r], tp.sh(1))

        def ag_relay(name, buf, ch):
            k1, k2, k3 = gath[name, ch]
            r = NCH * (s ^ 2) + ch
            net.arrived(k2, buf.at[r])
            net.push(k3, buf.at[r], buf.at[r], tp.sh(1))

        def ag_near(name, buf, ch):
            net.arrived(gath[name, ch][0], buf.at[NCH * (s ^ 1) + ch])

        def ag_far(name, buf, ch):
            net.arrived(gath[name, ch][2], buf.at[NCH * (s ^ 3) + ch])

        for ch in range(NCH):
            ag_push("tok", TOK, ch, tok_in.at[ch * CH : (ch + 1) * CH])
        half = own // 2
        hb = tp.b * half
        wsl = {}

        def w_push(lo, hi):
            for k in (2, 3, 1):
                t = s ^ k
                for j, (ref, at, w, dst, to) in enumerate(wcols(t)):
                    if not lo <= j < hi:
                        continue
                    wsl[k, j] = net.slot()
                    cols = pl.ds(pl.multiple_of(at, 128), w)
                    if k == 1:
                        net.push(wsl[k, j], ref.at[:, cols], dst.at[me, to : to + w], tp.sh(k))
                    else:
                        src = ref.at[pl.ds(pl.multiple_of(hb, 128), half), cols]
                        r = pl.ds(pl.multiple_of(s * own + hb, 128), half)
                        net.push(wsl[k, j], src, dst.at[r, to : to + w], tp.sh(k))

        def w_relay(lo, hi):
            for k in (2, 3):
                for j, (ref, at, w, dst, to) in enumerate(wcols(s)):
                    if not lo <= j < hi:
                        continue
                    r = pl.ds(pl.multiple_of((s ^ k) * own + hb, 128), half)
                    part = dst.at[r, to : to + w]
                    net.arrived(wsl[k, j], part)
                    wsl[k + 2, j] = net.slot()
                    net.push(wsl[k + 2, j], part, part, tp.rep(tp.r ^ 1))

        def w_wait(lo, hi):
            for j, (ref, at, w, dst, to) in enumerate(wcols(s)):
                if not lo <= j < hi:
                    continue
                net.arrived(wsl[1, j], dst.at[rows_of(s ^ 1, own), to : to + w])
                for k in (2, 3):
                    r = pl.ds(pl.multiple_of((s ^ k) * own + (half - hb), 128), half)
                    net.arrived(wsl[k + 2, j], dst.at[r, to : to + w])

        w_push(0, 3)
        w_push(3, 5)
        c_cot.wait()
        length = meta[16]
        for ch in range(NCH):
            blk = meta[NCH * s + ch]
            def cot_rows(u, _, ch=ch, blk=blk):
                q = pl.multiple_of(u * SUB, SUB)
                pos = blk * BLK + q + lax.broadcasted_iota(jnp.int32, (SUB, D), 0)
                g = GH[pl.ds(ch * CH + q, SUB), :].astype(F32)
                GB[NCH * s + ch, pl.ds(q, SUB), :] = jnp.where(pos < length, g, 0.0).astype(BF)
                return 0

            lax.fori_loop(0, CH // SUB, cot_rows, 0)
            ag_push("gb", GB, ch)
        c_gain.wait()
        for k in (1, 2, 3):
            net.arrived(g_slot[k - 1], GAIN.at[k])
        GV[...] = GAIN[0] + GAIN[1] + GAIN[2] + GAIN[3]
        gain1 = GV[0:1, 0:D]
        gain2 = GV[0:1, D : 2 * D]
        gq = GV[0:1, 2 * D : 2 * D + HD]
        gk = GV[0:1, 2 * D + HD : GW]
        GG[...] = jnp.zeros_like(GG)
        DKV[...] = jnp.zeros_like(DKV)

        for c in c_tok:
            c.wait()
        for c in c_w:
            c.wait()
        for ch in range(NCH):
            ag_relay("tok", TOK, ch)
        w_relay(0, 3)
        for ch in range(NCH):
            ag_near("tok", TOK, ch)
            ag_far("tok", TOK, ch)

        def norm1(i, _):
            src = meta[8 + i]

            def sub(u, _):
                x = TOK[src, pl.ds(pl.multiple_of(u * SUB, SUB), SUB), :].astype(F32)
                r = lax.rsqrt(jnp.mean(x * x, axis=1, keepdims=True) + EPSILON)
                NP[pl.ds(pl.multiple_of(i * BLK + u * SUB, SUB), SUB), :] = (x * r * gain1).astype(BF)
                return 0

            return lax.fori_loop(0, BLK // SUB, sub, 0)

        lax.fori_loop(0, T // BLK, norm1, 0)
        w_wait(0, 3)
        c_cs.wait()

        def proj(i, _):
            r = rows_of(i, TILE)
            raw = dot(NP[r, :], WQKV[...])
            X[:, 0:QK] = raw[:, :QK]
            HEADS[r, QK:] = raw[:, QK:].astype(BF)

            def sub(u, _):
                rr = pl.ds(pl.multiple_of(i * TILE + u * SUB, SUB), SUB)
                co = CS[rr, 0:HD]
                si = CS[rr, HD : 2 * HD]
                for h in range(heads + kvs):
                    g = gq if h < heads else gk
                    v = X[pl.ds(pl.multiple_of(u * SUB, SUB), SUB), h * HD : (h + 1) * HD]
                    RAW[rr, h * HD : (h + 1) * HD] = v.astype(BF)
                    n = v * lax.rsqrt(jnp.mean(v * v, axis=1, keepdims=True) + EPSILON) * g
                    HEADS[rr, h * HD : (h + 1) * HD] = (
                        n * co + pltpu.roll(n, HD // 2, 1) * si
                    ).astype(BF)
                return 0

            return lax.fori_loop(0, TILE // SUB, sub, 0)

        lax.fori_loop(0, T // TILE, proj, 0)

        lane = lax.broadcasted_iota(jnp.int32, (TILE, HD), 1)
        tri = lax.broadcasted_iota(jnp.int32, (TILE, TILE), 1) <= lax.broadcasted_iota(
            jnp.int32, (TILE, TILE), 0
        )

        def masked_scores(q, h_kv_cols, i):
            k = HEADS[0 : (i + 1) * TILE, h_kv_cols]
            sc = dot(q, k, 1, 1) * scale
            last = jnp.where(tri, sc[:, i * TILE :], -1e30)
            return last if i == 0 else jnp.concatenate([sc[:, : i * TILE], last], axis=1)

        def head_cols(h):
            return pl.ds(h * HD if isinstance(h, int) else pl.multiple_of(h * HD, HD), HD)

        def attend(h, _):
            kv = h // per if isinstance(h, int) else lax.div(h, per)
            kc = pl.ds(pl.multiple_of(QW + kv * HD, HD), HD)
            vc = pl.ds(pl.multiple_of(QK + kv * HD, HD), HD)
            for i in range(T // TILE):
                r = rows_of(i, TILE)
                sc = masked_scores(HEADS[r, head_cols(h)], kc, i)
                top = jnp.max(sc, axis=1, keepdims=True)
                e = jnp.exp(sc - top)
                total = jnp.sum(e, axis=1, keepdims=True)
                o = dot(e.astype(BF), HEADS[0 : (i + 1) * TILE, vc]) / total
                MIXP[i * (TILE // BLK) : (i + 1) * (TILE // BLK), :, head_cols(h)] = o.astype(BF).reshape(
                    TILE // BLK, BLK, HD
                )
                lse = top + jnp.log(total)
                LSE[r, :] = jnp.where(lane == h, lse, LSE[r, :])
            return 0

        LSE[...] = jnp.zeros_like(LSE)
        lax.fori_loop(0, heads, attend, 0)
        c_wo.wait()

        def reduce_scatter(partial):
            c_slot = [[net.slot() for _ in range(NCH)] for _ in range(2)]
            y_slot = [net.slot() for _ in range(NCH)]
            round_no[0] += 1
            RBY = RBYS.at[round_no[0] % 2]
            for ch in range(NCH):
                SBC[0, ch] = partial(s ^ 3, ch).astype(BF)
                net.push(c_slot[0][ch], SBC.at[0, ch], RBC.at[0, ch], tp.sh(1))
            for ch in range(NCH):
                part = partial(s ^ 2, ch)
                net.arrived(c_slot[0][ch], RBC.at[0, ch])
                SBY[ch] = (part + RBC[0, ch].astype(F32)).astype(BF)
                net.push(y_slot[ch], SBY.at[ch], RBY.at[ch], tp.sh(2))
            for ch in range(NCH):
                SBC[1, ch] = partial(s ^ 1, ch).astype(BF)
                net.push(c_slot[1][ch], SBC.at[1, ch], RBC.at[1, ch], tp.sh(1))
            for ch in range(NCH):
                HO[ch] = partial(s, ch)
            for ch in range(NCH):
                net.arrived(c_slot[1][ch], RBC.at[1, ch])
                HO[ch] = HO[ch] + RBC[1, ch].astype(F32)
            return y_slot

        def rs_finish(y_slot, ch):
            RBY = RBYS.at[round_no[0] % 2]
            net.arrived(y_slot[ch], RBY.at[ch])
            HO[ch] = HO[ch] + RBY[ch].astype(F32)

        def mixed_rows(t, ch):
            src = meta[NCH * t + ch]
            v = MIXP[src]
            MIXS[rows_of(t, own, ch, CH), :] = v
            return dot(v, WO[...])

        w_relay(3, 5)
        ys = reduce_scatter(mixed_rows)
        for ch in range(NCH):
            ag_relay("gb", GB, ch)
        for ch in range(NCH):
            rs_finish(ys, ch)

            def norm2(u, _, ch=ch):
                q = pl.ds(pl.multiple_of(u * SUB, SUB), SUB)
                x = TOK[NCH * s + ch, q, :].astype(F32) + HO[ch, q, :]
                qo = pl.ds(pl.multiple_of(ch * CH + u * SUB, SUB), SUB)
                HID[qo, :] = x
                GH[qo, :] = TOK[NCH * s + ch, q, :]
                r = lax.rsqrt(jnp.mean(x * x, axis=1, keepdims=True) + EPSILON)
                N2[NCH * s + ch, q, :] = (x * r * gain2).astype(BF)
                return 0

            lax.fori_loop(0, CH // SUB, norm2, 0)
            ag_push("n2", N2, ch)
        c_wd.wait()
        w_wait(3, 5)
        for ch in range(NCH):
            ag_near("gb", GB, ch)
            ag_far("gb", GB, ch)

        def ffn(t):
            two = pl.ds(NCH * t, NCH)
            for c in range(0, FW, 256):
                x = N2[two].reshape(own, D)
                X[:, 0:256] = dot(x, WGU[:, c : c + 256])
                X[:, 256:512] = dot(x, WGU[:, FW + c : FW + c + 256])
                X[:, 512:768] = dot(GB[two].reshape(own, D), WD[c : c + 256, :], 1, 1)

                def sub(u, _, c=c):
                    q = pl.ds(pl.multiple_of(u * SUB, SUB), SUB)
                    at = pl.ds(pl.multiple_of(t * own + u * SUB, SUB), SUB)
                    db = NCH * t + lax.div(u, BLK // SUB)
                    dr = pl.ds(pl.multiple_of(lax.rem(u, BLK // SUB) * SUB, SUB), SUB)
                    gate, up, ga = X[q, 0:256], X[q, 256:512], X[q, 512:768]
                    sig = 1.0 / (1.0 + jnp.exp(-gate))
                    act = gate * sig
                    ACT[at, c : c + 256] = (act * up).astype(BF)
                    DGU[db, dr, c : c + 256] = (ga * up * (sig + act * (1.0 - sig))).astype(BF)
                    DGU[db, dr, FW + c : FW + c + 256] = (ga * act).astype(BF)
                    return 0

                lax.fori_loop(0, own // SUB, sub, 0)

        ffn(s)
        for ch in range(NCH):
            ag_near("n2", N2, ch)
        ffn(s ^ 1)
        for ch in range(NCH):
            ag_relay("n2", N2, ch)
        ffn(s ^ 2)
        for ch in range(NCH):
            ag_far("n2", N2, ch)
        ffn(s ^ 3)
        net.drain()

        ys = reduce_scatter(
            lambda t, ch: dot(DGU[NCH * t + ch], WGU[...], 1, 1)
        )

        def flat(ref, cols):
            v = ref[:, :, cols] if len(ref.shape) == 3 else ref[:, cols]
            return v.reshape(T, v.shape[-1])

        for t in range(S):
            n = FW // S
            GD[0, t] = dot(ACT[:, t * n : (t + 1) * n], GB[...].reshape(T, D), 0, 0).astype(BF)
        ticks.run(2)
        for ch in range(NCH):
            rs_finish(ys, ch)

            def norm2_back(u, acc, ch=ch):
                q = pl.ds(pl.multiple_of(u * SUB, SUB), SUB)
                qo = pl.ds(pl.multiple_of(ch * CH + u * SUB, SUB), SUB)
                x = HID[qo, :]
                du = HO[ch, q, :]
                r = lax.rsqrt(jnp.mean(x * x, axis=1, keepdims=True) + EPSILON)
                gd = du * gain2
                m = jnp.mean(x * gd, axis=1, keepdims=True)
                gh = GB[NCH * s + ch, q, :].astype(F32) + r * gd - x * (r * r * r * m)
                DX[qo, :] = gh
                GMI[NCH * s + ch, q, :] = gh.astype(BF)
                GG[:, D : 2 * D] = GG[:, D : 2 * D] + fold8(du * x * r)
                return acc

            lax.fori_loop(0, CH // SUB, norm2_back, 0)
            ag_push("gmi", GMI, ch)
            ticks.run()

        def wgrad_ffn(t, _):
            cols = pl.ds(pl.multiple_of(t * (D // S), 256), D // S)
            g = dot(flat(N2, cols), DGU[...].reshape(T, 2 * FW), 0, 0).astype(BF)
            GGU[0, t] = g[:, :FW]
            GGU[1, t] = g[:, FW:]
            return 0

        lax.fori_loop(0, S, wgrad_ffn, 0)
        ticks.run()
        for ch in range(NCH):
            ag_relay("gmi", GMI, ch)
        ticks.run()
        for ch in range(NCH):
            ag_near("gmi", GMI, ch)
            ag_far("gmi", GMI, ch)

        def gmix(i, _):
            a = GMI[meta[8 + 2 * i]]
            b = GMI[meta[9 + 2 * i]]
            gm = dot(jnp.concatenate([a, b], axis=0), WO[...], 1, 1).astype(BF)
            GMP[2 * i] = gm[:BLK]
            GMP[2 * i + 1] = gm[BLK:]
            return 0

        lax.fori_loop(0, T // TILE, gmix, 0)
        for t in range(S):
            n = QW // S
            GO[0, t] = dot(MIXS[:, t * n : (t + 1) * n], GMI[...].reshape(T, D), 0, 0).astype(BF)
        ticks.run()
        net.drain()
        ys = reduce_scatter(lambda t, ch: dot(ACT[rows_of(t, own, ch, CH), :], WD[...]))

        def head_back(v, du, g):
            r = lax.rsqrt(jnp.mean(v * v, axis=1, keepdims=True) + EPSILON)
            gd = du * g
            m = jnp.mean(v * gd, axis=1, keepdims=True)
            return r * gd - v * (r * r * r * m), fold8(du * v * r)

        def unrotate(g, rr):
            return g * CS[rr, 0:HD] + pltpu.roll(g * CS[rr, HD : 2 * HD], HD // 2, 1)

        def attend_back(h):
            kv = h // per
            kc = pl.ds(QW + kv * HD, HD)
            vc = pl.ds(QK + kv * HD, HD)
            dk = pl.ds(kv * HD, HD)
            dv = pl.ds(KW + kv * HD, HD)
            for i in range(T // TILE):
                r = rows_of(i, TILE)
                n = (i + 1) * TILE
                q = HEADS[r, head_cols(h)]
                gm = GMP[2 * i : 2 * i + 2, :, head_cols(h)].reshape(TILE, HD)
                lse = jnp.sum(jnp.where(lane == h, LSE[r, :], 0.0), axis=1, keepdims=True)
                p = jnp.exp(masked_scores(q, kc, i) - lse)
                gp = dot(gm, HEADS[0:n, vc], 1, 1)
                inner = jnp.sum(p * gp, axis=1, keepdims=True)
                ds = (p * (gp - inner)).astype(BF)
                DKV[0:n, dv] = DKV[0:n, dv] + dot(p.astype(BF), gm, 0, 0)
                DKV[0:n, dk] = DKV[0:n, dk] + dot(ds, q, 0, 0) * scale
                DQH[...] = dot(ds, HEADS[0:n, kc]) * scale

                def sub(u, _, i=i):
                    q = pl.ds(pl.multiple_of(u * SUB, SUB), SUB)
                    rr = pl.ds(pl.multiple_of(i * TILE + u * SUB, SUB), SUB)
                    db = i * (TILE // BLK) + lax.div(u, BLK // SUB)
                    dr = pl.ds(pl.multiple_of(lax.rem(u, BLK // SUB) * SUB, SUB), SUB)
                    raw = RAW[rr, head_cols(h)].astype(F32)
                    d, gg = head_back(raw, unrotate(DQH[q, :], rr), gq)
                    DQKV[db, dr, head_cols(h)] = d.astype(BF)
                    GG[:, 2 * D : 2 * D + HD] = GG[:, 2 * D : 2 * D + HD] + gg
                    return 0

                lax.fori_loop(0, TILE // SUB, sub, 0)
                if i % 2 == 1:
                    ticks.run()

        for h in range(heads):
            attend_back(h)

        def key_back(u, _):
            rr = pl.ds(pl.multiple_of(u * SUB, SUB), SUB)
            lb = lax.div(u, BLK // SUB)
            lr = pl.ds(pl.multiple_of(lax.rem(u, BLK // SUB) * SUB, SUB), SUB)
            for kv in range(kvs):
                c = slice(QW + kv * HD, QW + (kv + 1) * HD)
                d, gg = head_back(
                    RAW[rr, c].astype(F32), unrotate(DKV[rr, kv * HD : (kv + 1) * HD], rr), gk
                )
                DQKV[lb, lr, c] = d.astype(BF)
                GG[:, 2 * D + HD : GW] = GG[:, 2 * D + HD : GW] + gg
            DQKV[lb, lr, QK:QKV] = DKV[rr, KW : 2 * KW].astype(BF)
            return 0

        lax.fori_loop(0, T // SUB, key_back, 0)
        for ch in range(NCH):
            rs_finish(ys, ch)

            def out_rows(u, _, ch=ch):
                q = pl.ds(pl.multiple_of(u * SUB, SUB), SUB)
                qo = pl.ds(pl.multiple_of(ch * CH + u * SUB, SUB), SUB)
                GB[NCH * s + ch, q, :] = (HID[qo, :] + HO[ch, q, :]).astype(BF)
                return 0

            lax.fori_loop(0, CH // SUB, out_rows, 0)
        c_out = [local(GB.at[NCH * s + ch], out_o.at[ch * CH : (ch + 1) * CH]) for ch in range(NCH)]
        net.drain()
        ticks.run()

        def back_rows(t, ch):
            src = meta[NCH * t + ch]
            return dot(DQKV[src, :, 0:QKV], WQKV[...], 1, 1)

        ys = reduce_scatter(back_rows)

        def wgrad_qkv(t, _):
            cols = pl.ds(pl.multiple_of(t * (D // S), 256), D // S)
            g = dot(NP[:, cols], flat(DQKV, slice(0, QKV)), 0, 0).astype(BF)
            GQ[0, t] = g[:, :QW]
            GKV[0, t] = g[:, QW:QK]
            GKV[1, t] = g[:, QK:]
            return 0

        lax.fori_loop(0, S, wgrad_qkv, 0)
        ticks.run(2)
        for ch in range(NCH):
            rs_finish(ys, ch)

            def norm1_back(u, acc, ch=ch):
                q = pl.ds(pl.multiple_of(u * SUB, SUB), SUB)
                qo = pl.ds(pl.multiple_of(ch * CH + u * SUB, SUB), SUB)
                x = GH[qo, :].astype(F32)
                du = HO[ch, q, :]
                r = lax.rsqrt(jnp.mean(x * x, axis=1, keepdims=True) + EPSILON)
                gd = du * gain1
                m = jnp.mean(x * gd, axis=1, keepdims=True)
                DX[qo, :] = DX[qo, :] + r * gd - x * (r * r * r * m)
                GG[:, 0:D] = GG[:, 0:D] + fold8(du * x * r)
                return acc

            lax.fori_loop(0, CH // SUB, norm1_back, 0)
            ticks.run()
        c_dx = local(DX, dx_o)
        def gain_part(t):
            c = pl.multiple_of(t * own, 256)
            return (
                (GG.at[:, pl.ds(c, own)], 0, own),
                (GG.at[:, pl.ds(pl.multiple_of(D + c, 256), own)], own, own),
                (GG.at[:, 2 * D : GW], 2 * own, 2 * HD),
            )

        n_slot = {}
        for k in (1, 2, 3):
            for j, (src, to, w) in enumerate(gain_part(s ^ k)):
                n_slot[k, j] = net.slot()
                net.push(n_slot[k, j], src, GS.at[k, :, to : to + w], tp.sh(k))
        mine = [local(src, GS.at[0, :, to : to + w]) for src, to, w in gain_part(s)]
        ticks.run()
        for c in mine:
            c.wait()
        for k in (1, 2, 3):
            for j, (src, to, w) in enumerate(gain_part(s ^ k)):
                net.arrived(n_slot[k, j], GS.at[k, :, to : to + w])
        GS[0] = (GS[0] + GS[1]) + (GS[2] + GS[3])
        r_slot = [net.slot() for _ in range(R)]
        for k in range(1, R):
            net.push(r_slot[k], GS.at[0], gg_o.at[tp.r], tp.rep(lax.rem(tp.r + k, R)))
        c_gg = local(GS.at[0], gg_o.at[tp.r])
        ticks.run()
        for k in range(1, R):
            net.arrived(r_slot[k], gg_o.at[lax.rem(tp.r + R - k, R)])
        ticks.finish()
        for c in c_out + [c_dx, c_gg]:
            c.wait()
        net.drain()

    any_ = pl.BlockSpec(memory_space=pl.ANY)
    specs = [pl.BlockSpec(memory_space=pltpu.SMEM)] + [any_] * 11
    return pl.pallas_call(
        body,
        out_shape=[jax.ShapeDtypeStruct(*o) for o in outs],
        in_specs=specs,
        out_specs=[any_] * len(outs),
        scratch_shapes=scratch,
        compiler_params=pltpu.CompilerParams(
            collective_id=2, has_side_effects=True, vmem_limit_bytes=64 << 20
        ),
        name="layer",
    )(*args)


def rotary_table(slot_len, head_width):
    middle = head_width // 2
    inverse = np.power(ROPE_BASE, -np.arange(middle) * 2.0 / head_width).astype(np.float32)
    phases = np.arange(slot_len, dtype=np.float32)[:, None] * inverse
    cosine = np.cos(phases.astype(np.float64))
    sine = np.sin(phases.astype(np.float64))
    table = np.concatenate([cosine, cosine, -sine, sine], axis=1)
    return table.astype(np.float32)


def shards(
    tokens,
    cotangent,
    lengths,
    block_order,
    norm1_gain,
    query_weight,
    key_weight,
    value_weight,
    output_weight,
    query_gain,
    key_gain,
    norm2_gain,
    gate_weight,
    up_weight,
    down_weight,
):
    S, R = lax.axis_size("shard"), lax.axis_size("replica")
    at = lax.axis_index("shard")
    z = layer_sizes(tokens[0], query_weight, key_weight, gate_weight, query_gain, S)
    D, HD = z["D"], z["HD"]
    full = []
    for g, size in ((norm1_gain, D), (norm2_gain, D), (query_gain, HD), (key_gain, HD)):
        owner = jnp.arange(size, dtype=jnp.int32) // g.shape[0]
        full.append(jnp.where(owner == at, jnp.tile(g.astype(F32), S), 0.0))
    gains = jnp.broadcast_to(jnp.concatenate(full)[None], (8, 2 * D + 2 * HD))
    order = block_order[0]
    count = order.shape[0]
    place = jnp.arange(count, dtype=jnp.int32)
    inverse = jnp.sum(jnp.where(order[None, :] == place[:, None], place[None, :], 0), axis=1)
    meta = jnp.concatenate([order, inverse, lengths, jnp.zeros((15,), jnp.int32)])
    table = jnp.asarray(rotary_table(z["T"], HD))
    out, dx, gg, gd, ggu, go, gq, gkv = layer_call(
        z, S, R,
        (meta, tokens[0], cotangent[0], gains, table, query_weight, key_weight, value_weight,
         output_weight, gate_weight, up_weight, down_weight),
    )
    block = z["T"] // count
    mine_blocks = lax.dynamic_slice_in_dim(order, at * (z["own"] // block), z["own"] // block)
    position = mine_blocks[:, None] * block + jnp.arange(block, dtype=jnp.int32)[None, :]
    valid = position.reshape(-1, 1) < lengths[0]
    out = jnp.where(valid, out, jnp.zeros_like(out))
    small = jnp.sum(gg, axis=(0, 1))
    own, hw = z["own"], HD // S

    def mine(first):
        return lax.dynamic_slice_in_dim(small, first + at * hw, hw)

    return (
        out[None],
        dx[None],
        small[:own],
        gq[0].astype(F32),
        gkv[0].astype(F32),
        gkv[1].astype(F32),
        go.astype(F32).reshape(-1, D),
        mine(2 * own),
        mine(2 * own + HD),
        small[own : 2 * own],
        ggu[0].astype(F32),
        ggu[1].astype(F32),
        gd.astype(F32).reshape(-1, D),
    )


def solution(mesh):
    rows, mat, vec = P("replica", "shard", None), P("shard", None), P("shard")
    placed = (rows, rows, P("replica"), P("replica", None), vec, mat, mat, mat, mat)
    placed += (vec, vec, vec, mat, mat, mat)
    outs = (rows, rows, vec, mat, mat, mat, mat, vec, vec, vec, mat, mat, mat)
    return jax.shard_map(shards, mesh=mesh, in_specs=placed, out_specs=outs, check_vma=False)
```

```python
import functools

import jax
import jax.numpy as jnp
import numpy as np
from jax import lax
from jax.experimental import pallas as pl
from jax.experimental.pallas import tpu as pltpu
from jax.sharding import PartitionSpec as P

EPSILON = 1e-06
ROPE_BASE = 1000000.0
BF = jnp.bfloat16
F32 = jnp.float32
MESH = pl.DeviceIdType.MESH


class Topo:
    def __init__(self, shards, replicas):
        self.S = shards
        self.R = replicas
        self.L = replicas // 2
        self.s = lax.axis_index("shard")
        r = lax.axis_index("replica")
        self.r = r
        L = self.L
        a = lax.div(r, 2)
        self.b = lax.rem(r, 2)
        left = a <= L // 2 - 1
        self.mid = jnp.logical_or(a == L // 2 - 1, a == L // 2)
        self.edge = jnp.logical_or(a == 0, a == L - 1)
        self.inner = jnp.logical_not(self.edge)
        self.side = jnp.logical_not(self.mid)
        self.toward = jnp.where(left, r + 2, r - 2)
        self.outward = jnp.where(left, r - 2, r + 2)
        self.h = jnp.where(left, 0, 1)

    def rep(self, r):
        return (self.s, r)

    def sh(self, k):
        return (self.s ^ k, self.r)


def barrier(tp):
    bar = pltpu.get_barrier_semaphore()
    ids = [tp.rep(lax.rem(tp.r + k, tp.R)) for k in range(1, tp.R)]
    ids += [tp.sh(1), tp.sh(2), tp.sh(3)]
    for d in ids:
        pl.semaphore_signal(bar, inc=1, device_id=d, device_id_type=MESH)
    pl.semaphore_wait(bar, len(ids))


def add_rows(dst, a, b):
    blocks, parts, rows, _ = a.shape

    def body(i, _):
        q = pl.ds(pl.multiple_of(i * 16, 16), 16)
        for w in range(blocks):
            for t in range(parts):
                dst[w, t, q, :] = (a[w, t, q, :].astype(F32) + b[w, t, q, :].astype(F32)).astype(BF)
        return 0

    lax.fori_loop(0, rows // 16, body, 0)


class Chunk:
    def __init__(self, tp, kind, G, out, base, nr, spread, bufs, send, recv, at):
        self.tp, self.G, self.out, self.base, self.nr, self.hr = tp, G, out, base, nr, nr // 2
        self.spread, self.bufs, self.send, self.recv_sem, self.at = spread, bufs, send, recv, at
        self.W = G.shape[3]
        self.sent = []
        self.steps = self.steps_a() if kind == "A" else self.steps_b()

    def rows(self, h):
        return pl.ds(pl.multiple_of(self.base + h * self.hr, 16), self.hr)

    def half(self, h):
        return self.G.at[:, :, self.rows(h), :]

    def out_half(self, h):
        return self.out.at[:, self.rows(h), :] if self.spread else self.out.at[:, :, self.rows(h), :]

    def out_piece(self, h, s):
        return self.out.at[:, self.rows(h), pl.ds(pl.multiple_of(s * self.W, 128), self.W)]

    def copy(self, slot, src, dst, dev):
        k = self.at + slot
        return pltpu.make_async_remote_copy(
            src, dst, self.send.at[k], self.recv_sem.at[k], device_id=dev, device_id_type=MESH
        )

    def start(self, cond, slot, src, dst, dev):
        c = self.copy(slot, src, dst, dev)
        if cond is None:
            c.start()
        else:
            pl.when(cond)(lambda: c.start())
        self.sent.append((cond, c))

    def drain(self):
        for cond, c in self.sent:
            if cond is None:
                c.wait_send()
            else:
                pl.when(cond)(lambda c=c: c.wait_send())

    def arrived(self, slot, ref):
        self.copy(slot, ref, ref, self.tp.rep(self.tp.r ^ 1)).wait_recv()

    def local(self, src, dst):
        return pltpu.make_async_copy(src, dst, self.send.at[self.at + 9])

    def final_out(self, h, F):
        tp = self.tp
        if self.spread:
            for k in (1, 2, 3):
                self.start(tp.mid, 2 + k, F.at[:, tp.s ^ k], self.out_piece(h, tp.s), tp.sh(k))

        @pl.when(tp.mid)
        def _():
            if self.spread:
                self.local(F.at[:, tp.s], self.out_piece(h, tp.s)).start()
            else:
                self.local(F, self.out_half(h)).start()

    def final_wait(self, h, F):
        tp = self.tp
        if self.spread:
            for k in (1, 2, 3):
                self.arrived(2 + k, self.out_piece(h, tp.s ^ k))
            self.local(F.at[:, tp.s], self.out_piece(h, tp.s)).wait()
        else:
            self.local(F, self.out_half(h)).wait()

    def steps_a(self):
        tp = self.tp
        b = tp.b
        RX, FOLD, MID = self.bufs
        xp = tp.rep(tp.r ^ 1)
        own = self.half(b)
        both = jnp.logical_and

        def onward(cond):
            self.start(both(cond, tp.mid), 2, own, MID, tp.rep(tp.toward))
            if tp.L > 2:
                self.start(both(cond, tp.side), 1, own, FOLD, tp.rep(tp.toward))

        def s0():
            self.start(None, 0, self.half(1 - b), RX, xp)

        def s1():
            self.arrived(0, RX)
            add_rows(own, own, RX)
            onward(tp.edge)

        def s2():
            if tp.L == 2:
                return

            @pl.when(tp.inner)
            def _():
                self.arrived(1, FOLD)
                add_rows(own, own, FOLD)

            onward(tp.inner)

        def s3():
            @pl.when(tp.mid)
            def _():
                self.arrived(2, MID)
                add_rows(MID, own, MID)

            self.final_out(b, MID)

        def s4():
            pl.when(tp.mid)(lambda: self.final_wait(b, MID))
            if tp.L > 2:
                self.start(tp.mid, 6, self.out_half(b), self.out_half(b), tp.rep(tp.outward))
            self.start(tp.mid, 7, self.out_half(b), self.out_half(b), xp)

        def s5():
            if tp.L == 2:
                return
            pl.when(tp.side)(lambda: self.arrived(6, self.out_half(b)))
            if tp.L > 4:
                self.start(
                    both(tp.side, tp.inner), 6, self.out_half(b), self.out_half(b), tp.rep(tp.outward)
                )
            self.start(tp.side, 7, self.out_half(b), self.out_half(b), xp)

        def s6():
            self.arrived(7, self.out_half(1 - b))

        return [s0, s1, s2, s3, s4, s5, s6]

    def steps_b(self):
        tp = self.tp
        h = tp.h
        FOLD, MID, XB = self.bufs
        xp = tp.rep(tp.r ^ 1)
        own, other = self.half(h), self.half(1 - h)
        full = self.G.at[:, :, self.base : self.base + self.nr, :]
        both = jnp.logical_and

        def onward(cond):
            self.start(both(cond, tp.mid), 2, other, MID, tp.rep(tp.toward))
            if tp.L > 2:
                self.start(both(cond, tp.side), 1, full, FOLD, tp.rep(tp.toward))

        def s0():
            onward(tp.edge)

        def s1():
            if tp.L == 2:
                return

            @pl.when(tp.inner)
            def _():
                self.arrived(1, FOLD)
                add_rows(full, full, FOLD)

            onward(tp.inner)

        def s2():
            @pl.when(tp.mid)
            def _():
                self.arrived(2, MID)
                add_rows(own, own, MID)

            self.start(tp.mid, 0, own, XB, xp)

        def s3():
            @pl.when(tp.mid)
            def _():
                self.arrived(0, XB)
                add_rows(XB, own, XB)

            self.final_out(h, XB)

        def s4():
            pl.when(tp.mid)(lambda: self.final_wait(h, XB))
            self.start(tp.mid, 8, self.out_half(h), self.out_half(h), tp.rep(tp.toward))
            if tp.L > 2:
                self.start(tp.mid, 6, self.out_half(h), self.out_half(h), tp.rep(tp.outward))

        def s5():
            pl.when(tp.mid)(lambda: self.arrived(8, self.out_half(1 - h)))
            if tp.L == 2:
                return
            self.start(tp.mid, 7, self.out_half(1 - h), self.out_half(1 - h), tp.rep(tp.outward))
            pl.when(tp.side)(lambda: self.arrived(6, self.out_half(h)))
            if tp.L > 4:
                self.start(
                    both(tp.side, tp.inner), 6, self.out_half(h), self.out_half(h), tp.rep(tp.outward)
                )

        def s6():
            if tp.L == 2:
                return
            pl.when(tp.side)(lambda: self.arrived(7, self.out_half(1 - h)))
            if tp.L > 4:
                self.start(
                    both(tp.side, tp.inner),
                    7,
                    self.out_half(1 - h),
                    self.out_half(1 - h),
                    tp.rep(tp.outward),
                )

        return [s0, s1, s2, s3, s4, s5, s6]


class Ticks:
    def __init__(self, chunks, stride):
        self.chunks, self.stride, self.t, self.limit = chunks, stride, 0, 0
        self.begun = []

    def run(self, count=1):
        for _ in range(count):
            if len(self.begun) < min(self.limit, len(self.chunks)):
                self.begun.append(self.t)
            for k in range(6, -1, -1):
                for chunk, begun in zip(self.chunks, self.begun):
                    if begun == self.t - k * self.stride:
                        chunk.steps[k]()
            self.t += 1

    def finish(self):
        self.limit = len(self.chunks)
        while len(self.begun) < self.limit or self.t <= self.begun[-1] + 6 * self.stride:
            self.run()
        for c in self.chunks:
            c.drain()


class Net:
    def __init__(self, tp, send, recv):
        self.tp = tp
        self.send = send
        self.recv = recv
        self.k = 0
        self.live = []

    def slot(self):
        self.k += 1
        return self.k - 1

    def make(self, slot, src, dst, dev):
        return pltpu.make_async_remote_copy(
            src, dst, self.send.at[slot], self.recv.at[slot], device_id=dev, device_id_type=MESH
        )

    def push(self, slot, src, dst, dev):
        c = self.make(slot, src, dst, dev)
        c.start()
        self.live.append(c)
        return c

    def arrived(self, slot, ref):
        self.make(slot, ref, ref, self.tp.sh(1)).wait_recv()

    def drain(self, some=None):
        for c in self.live if some is None else some:
            c.wait_send()
        self.live = [] if some is None else [c for c in self.live if all(c is not d for d in some)]


def dot(a, b, ca=1, cb=0):
    return lax.dot_general(a, b, (((ca,), (cb,)), ((), ())), preferred_element_type=F32)


def rows_of(t, rows, ch=0, ch_rows=None):
    n = rows if ch_rows is None else ch_rows
    start = t * rows + ch * n
    return pl.ds(start if isinstance(start, int) else pl.multiple_of(start, 128), n)


def fold8(v):
    out = v[0:8]
    for k in range(1, v.shape[0] // 8):
        out = out + v[8 * k : 8 * k + 8]
    return out


def layer_sizes(tokens, query_weight, key_weight, gate_weight, query_gain, shards):
    z = {}
    z["own"] = tokens.shape[0]
    z["D"] = tokens.shape[1]
    z["T"] = z["own"] * shards
    z["HD"] = query_gain.shape[0] * shards
    z["QW"] = query_weight.shape[1] // shards
    z["KW"] = key_weight.shape[1] // shards
    z["FW"] = gate_weight.shape[1] // shards
    return z


def layer_call(z, S, R, args):
    own, D, T, HD, QW, KW, FW = (z[k] for k in ("own", "D", "T", "HD", "QW", "KW", "FW"))
    QKV = QW + 2 * KW
    QK = QW + KW
    heads, kvs = QW // HD, KW // HD
    per = heads // kvs
    BLK = 128
    CH = 128
    TA = (0, 2, 4)
    NCH = own // CH
    TILE = 256
    scale = float(HD) ** -0.5
    SUB = 32
    GW = 2 * D + 2 * HD
    GN = 2 * own + 2 * HD

    vm = lambda shape, dtype: pltpu.VMEM(shape, dtype)
    scratch = [
        vm((T // BLK, BLK, D), BF), vm((T // BLK, BLK, D), BF), vm((T // BLK, BLK, D), BF), vm((T, D), BF),
        vm((D, QKV), BF), vm((D, 2 * FW), BF), vm((QW, D), BF), vm((FW, D), BF),
        vm((S, 8, GW), F32), vm((8, GW), F32), vm((T, HD), F32),
        vm((T, QK), BF), vm((T, QKV), BF), vm((T, HD), F32), vm((T // BLK, BLK, QW), BF), vm((T, QW), BF),
        vm((NCH, CH, D), BF), vm((2, NCH, CH, D), BF), vm((NCH, CH, D), BF), vm((2, NCH, CH, D), BF),
        vm((NCH, CH, D), F32), vm((own, D), F32), vm((own, D), BF),
        vm((T, FW), BF), vm((T // BLK, BLK, 2 * FW), BF), vm((T, 2 * KW), F32),
        vm((HD, per * TILE), F32), vm((8, T), F32), vm((8, GW), F32), vm((2 * own, max(QK, 768)), F32),
        vm((own, D), F32),
        vm((S, 8, GN), F32),
        pltpu.SemaphoreType.DMA((160,)), pltpu.SemaphoreType.DMA((160,)), pltpu.SemaphoreType.DMA((24,)),
    ]
    grads = [
        ((1, S, FW // S, D), 32, False),
        ((2, S, D // S, FW), 32, True),
        ((1, S, QW // S, D), 32, False),
        ((1, S, D // S, QW), 32, True),
        ((2, S, D // S, KW), 32, True),
    ]
    outs = [((own, D), BF), ((own, D), F32), ((R, 8, GN), F32)]
    FIXED = len(scratch)
    plan = []
    for j, (shape, nr, spread) in enumerate(grads):
        w, _, rows, width = shape
        outs.append(((w, rows, S * width) if spread else shape, BF))
        scratch.append(vm(shape, BF))
        for base in range(0, rows, nr):
            plan.append((j, base, "AB"[len(plan) % 2]))
    for j, base, kind in plan:
        (w, _, rows, width), nr, _ = grads[j]
        half = vm((w, S, nr // 2, width), BF)
        scratch += [half, half, half] if kind == "A" else [vm((w, S, nr, width), BF), half, half]
    sems = pltpu.SemaphoreType.DMA((10 * len(plan),))
    scratch += [sems, sems]

    def body(*refs):
        meta, tok_in, cot_in, gains_in, cs_in, wq_in, wk_in, wv_in, wo_in, wg_in, wu_in, wd_in = refs[:12]
        out_o, dx_o, gg_o = refs[12:15]
        grad_o = refs[15:20]
        (TOK, GB, N2, NP, WQKV, WGU, WO, WD, GAIN, GV, CS, RAW, HEADS, LSE, MIXP, MIXS,
         SBC, RBC, SBY, RBYS, HO, HID, GH, ACT, DGU, DKV, DQT, LT, GG, X, DX,
         GS, send, recv, lsem) = refs[20:20 + FIXED]
        G = refs[20 + FIXED : 25 + FIXED]
        GD, GGU, GO, GQ, GKV = G
        bufs = refs[25 + FIXED : -2]
        GMI, GMP, DQKV = TOK, MIXP, DGU
        round_no = [0]
        tp = Topo(S, R)
        net = Net(tp, send, recv)
        chunks = []
        for i, (j, base, kind) in enumerate(plan):
            shape, nr, spread = grads[j]
            chunks.append(
                Chunk(tp, kind, G[j], grad_o[j], base, nr, spread, bufs[3 * i : 3 * i + 3], refs[-2], refs[-1], 10 * i)
            )
        ticks = Ticks(chunks, 2)
        ready = [sum(1 for p in plan if p[0] <= j) for j in range(len(grads))]
        s = tp.s
        lk = [0]
        locals_live = []

        def local(src, dst):
            c = pltpu.make_async_copy(src, dst, lsem.at[lk[0]])
            lk[0] += 1
            c.start()
            return c

        me = rows_of(s, own)
        def wcols(t):
            return (
                (wq_in, t * QW, QW, WQKV, 0),
                (wk_in, t * KW, KW, WQKV, QW),
                (wv_in, t * KW, KW, WQKV, QK),
                (wg_in, t * FW, FW, WGU, 0),
                (wu_in, t * FW, FW, WGU, FW),
            )

        def w_local(lo, hi):
            return [
                local(ref.at[:, pl.ds(pl.multiple_of(at, 128), w)], dst.at[me, to : to + w])
                for ref, at, w, dst, to in wcols(s)[lo:hi]
            ]

        barrier(tp)
        g_slot = [net.slot() for _ in range(3)]
        for k in (1, 2, 3):
            net.push(g_slot[k - 1], gains_in, GAIN.at[k], tp.sh(k))
        gath = {}

        def ag_push(name, buf, ch, src=None):
            r = NCH * s + ch
            k1, k2, k3 = net.slot(), net.slot(), net.slot()
            gath[name, ch] = (k1, k2, k3)
            src = buf.at[r] if src is None else src
            c = net.push(k2, src, buf.at[r], tp.sh(2))
            net.push(k1, src, buf.at[r], tp.sh(1))
            return c

        def ag_relay(name, buf, ch):
            k1, k2, k3 = gath[name, ch]
            r = NCH * (s ^ 2) + ch
            net.arrived(k2, buf.at[r])
            net.push(k3, buf.at[r], buf.at[r], tp.sh(1))

        def ag_near(name, buf, ch):
            net.arrived(gath[name, ch][0], buf.at[NCH * (s ^ 1) + ch])

        def ag_far(name, buf, ch):
            net.arrived(gath[name, ch][2], buf.at[NCH * (s ^ 3) + ch])

        half = own // 2
        quarter = own // 4
        zb = lax.rem(lax.div(tp.r, 2), 2)
        fsl = {}

        def f_part(k, j, z, x):
            _, _, w, dst, to = wcols(s)[j]
            at = (s ^ k) * own + z * half + x * quarter
            return dst.at[pl.ds(pl.multiple_of(at, quarter), quarter), to : to + w]

        def f_push(lo, hi):
            far = []
            for k in (2, 3, 1):
                for j, (ref, at, w, dst, to) in enumerate(wcols(s ^ k)):
                    if not lo <= j < hi:
                        continue
                    fsl[k, j] = [net.slot() for _ in range(4)]
                    cols = pl.ds(pl.multiple_of(at, 128), w)
                    if k == 1:
                        net.push(fsl[k, j][0], ref.at[:, cols], dst.at[me, to : to + w], tp.sh(k))
                    else:
                        q0 = zb * half + tp.b * quarter
                        src = ref.at[pl.ds(pl.multiple_of(q0, quarter), quarter), cols]
                        r = pl.ds(pl.multiple_of(s * own + q0, quarter), quarter)
                        far.append(net.push(fsl[k, j][0], src, dst.at[r, to : to + w], tp.sh(k)))
            return far

        def f_relay(lo, hi):
            for k in (2, 3):
                for j in range(lo, hi):
                    part = f_part(k, j, zb, tp.b)
                    net.arrived(fsl[k, j][0], part)
                    net.push(fsl[k, j][1], part, part, tp.rep(tp.r ^ 1))
                    net.push(fsl[k, j][2], part, part, tp.rep(tp.r ^ 2))

        def f_relay_far(lo, hi):
            for k in (2, 3):
                for j in range(lo, hi):
                    part = f_part(k, j, zb, 1 - tp.b)
                    net.arrived(fsl[k, j][1], part)
                    net.push(fsl[k, j][3], part, part, tp.rep(tp.r ^ 2))

        def f_wait(lo, hi):
            for j in range(lo, hi):
                _, _, w, dst, to = wcols(s)[j]
                net.arrived(fsl[1, j][0], dst.at[rows_of(s ^ 1, own), to : to + w])
                for k in (2, 3):
                    net.arrived(fsl[k, j][2], f_part(k, j, 1 - zb, tp.b))
                    net.arrived(fsl[k, j][3], f_part(k, j, 1 - zb, 1 - tp.b))

        c_gain = local(gains_in, GAIN.at[0])
        c_tok = [
            local(tok_in.at[ch * CH : (ch + 1) * CH], TOK.at[NCH * s + ch]) for ch in range(NCH)
        ]
        c_cot = local(cot_in, GH)
        far = f_push(0, 3)
        net.drain(far)
        for ch in range(NCH):
            ag_push("tok", TOK, ch, tok_in.at[ch * CH : (ch + 1) * CH])
        f_relay(0, 3)
        c_w = w_local(0, 3)
        c_cs = local(cs_in, CS)
        c_cot.wait()
        length = meta[16]
        for ch in range(NCH):
            blk = meta[NCH * s + ch]
            def cot_rows(u, _, ch=ch, blk=blk):
                q = pl.multiple_of(u * SUB, SUB)
                pos = blk * BLK + q + lax.broadcasted_iota(jnp.int32, (SUB, D), 0)
                g = GH[pl.ds(ch * CH + q, SUB), :].astype(F32)
                GB[NCH * s + ch, pl.ds(q, SUB), :] = jnp.where(pos < length, g, 0.0).astype(BF)
                return 0

            lax.fori_loop(0, CH // SUB, cot_rows, 0)
        c_gain.wait()
        for k in (1, 2, 3):
            net.arrived(g_slot[k - 1], GAIN.at[k])
        GV[...] = GAIN[0] + GAIN[1] + GAIN[2] + GAIN[3]
        gain1 = GV[0:1, 0:D]
        gain2 = GV[0:1, D : 2 * D]
        gq = GV[0:1, 2 * D : 2 * D + HD]
        gk = GV[0:1, 2 * D + HD : GW]
        GG[...] = jnp.zeros_like(GG)
        DKV[...] = jnp.zeros_like(DKV)

        for c in c_tok:
            c.wait()
        for c in c_w:
            c.wait()
        for ch in range(NCH):
            ag_relay("tok", TOK, ch)
        f_relay_far(0, 3)
        for ch in range(NCH):
            ag_near("tok", TOK, ch)
            ag_far("tok", TOK, ch)

        def norm1(i, _):
            src = meta[8 + i]

            def sub(u, _):
                x = TOK[src, pl.ds(pl.multiple_of(u * SUB, SUB), SUB), :].astype(F32)
                r = lax.rsqrt(jnp.mean(x * x, axis=1, keepdims=True) + EPSILON)
                NP[pl.ds(pl.multiple_of(i * BLK + u * SUB, SUB), SUB), :] = (x * r * gain1).astype(BF)
                return 0

            return lax.fori_loop(0, BLK // SUB, sub, 0)

        lax.fori_loop(0, T // BLK, norm1, 0)
        f_wait(0, 3)
        f_push(3, 5)
        for ch in range(NCH):
            ag_push("gb", GB, ch)
        c_wo = local(wo_in, WO)
        c_f = w_local(3, 5)
        c_wd = local(wd_in, WD)
        c_cs.wait()

        def rotation(rr):
            v = CS[rr, :]
            w = pltpu.roll(v, HD // 2, 1)
            low = lax.broadcasted_iota(jnp.int32, v.shape, 1) < HD // 2
            return jnp.where(low, v, w), jnp.where(low, -w, v)

        def proj(i, _):
            r = rows_of(i, TILE)
            raw = dot(NP[r, :], WQKV[...])
            X[0:TILE, 0:QK] = raw[:, :QK]
            HEADS[r, QK:] = raw[:, QK:].astype(BF)

            def sub(u, _):
                rr = pl.ds(pl.multiple_of(i * TILE + u * (2 * SUB), (2 * SUB)), (2 * SUB))
                co, si = rotation(rr)
                for h in range(heads + kvs):
                    g = gq if h < heads else gk
                    v = X[pl.ds(pl.multiple_of(u * (2 * SUB), (2 * SUB)), (2 * SUB)), h * HD : (h + 1) * HD]
                    RAW[rr, h * HD : (h + 1) * HD] = v.astype(BF)
                    n = v * lax.rsqrt(jnp.mean(v * v, axis=1, keepdims=True) + EPSILON) * g
                    HEADS[rr, h * HD : (h + 1) * HD] = (
                        n * co + pltpu.roll(n, HD // 2, 1) * si
                    ).astype(BF)
                return 0

            return lax.fori_loop(0, TILE // (2 * SUB), sub, 0)

        lax.fori_loop(0, T // TILE, proj, 0)

        f_relay(3, 5)
        lane = lax.broadcasted_iota(jnp.int32, (TILE, HD), 1)
        tri = lax.broadcasted_iota(jnp.int32, (TILE, TILE), 1) <= lax.broadcasted_iota(
            jnp.int32, (TILE, TILE), 0
        )

        def masked_scores(q, h_kv_cols, i):
            k = HEADS[0 : (i + 1) * TILE, h_kv_cols]
            sc = dot(q, k, 1, 1) * scale
            last = jnp.where(tri, sc[:, i * TILE :], -1e30)
            return last if i == 0 else jnp.concatenate([sc[:, : i * TILE], last], axis=1)

        def head_cols(h):
            return pl.ds(h * HD if isinstance(h, int) else pl.multiple_of(h * HD, HD), HD)

        def attend(h, _):
            kv = h // per if isinstance(h, int) else lax.div(h, per)
            kc = pl.ds(pl.multiple_of(QW + kv * HD, HD), HD)
            vc = pl.ds(pl.multiple_of(QK + kv * HD, HD), HD)
            for i in range(T // TILE):
                r = rows_of(i, TILE)
                sc = masked_scores(HEADS[r, head_cols(h)], kc, i)
                top = jnp.max(sc, axis=1, keepdims=True)
                e = jnp.exp(sc - top)
                total = jnp.sum(e, axis=1, keepdims=True)
                o = dot(e.astype(BF), HEADS[0 : (i + 1) * TILE, vc]) / total
                MIXP[i * (TILE // BLK) : (i + 1) * (TILE // BLK), :, head_cols(h)] = o.astype(BF).reshape(
                    TILE // BLK, BLK, HD
                )
                lse = top + jnp.log(total)
                LSE[r, :] = jnp.where(lane == h, lse, LSE[r, :])
            return 0

        LSE[...] = jnp.zeros_like(LSE)
        lax.fori_loop(0, heads, attend, 0)
        c_wo.wait()

        def reduce_scatter(partial):
            c_slot = [[net.slot() for _ in range(NCH)] for _ in range(2)]
            y_slot = [net.slot() for _ in range(NCH)]
            round_no[0] += 1
            sent = []
            RBY = RBYS.at[round_no[0] % 2]
            for ch in range(NCH):
                SBC[ch] = partial(s ^ 3, ch).astype(BF)
                sent.append(net.push(c_slot[0][ch], SBC.at[ch], RBC.at[0, ch], tp.sh(1)))
            for ch in range(NCH):
                part = partial(s ^ 2, ch)
                net.arrived(c_slot[0][ch], RBC.at[0, ch])
                SBY[ch] = (part + RBC[0, ch].astype(F32)).astype(BF)
                net.push(y_slot[ch], SBY.at[ch], RBY.at[ch], tp.sh(2))
            for ch in range(NCH):
                part = partial(s ^ 1, ch).astype(BF)
                net.drain([sent[ch]])
                SBC[ch] = part
                net.push(c_slot[1][ch], SBC.at[ch], RBC.at[1, ch], tp.sh(1))
            for ch in range(NCH):
                HO[ch] = partial(s, ch)
            for ch in range(NCH):
                net.arrived(c_slot[1][ch], RBC.at[1, ch])
                HO[ch] = HO[ch] + RBC[1, ch].astype(F32)
            return y_slot

        def rs_finish(y_slot, ch):
            RBY = RBYS.at[round_no[0] % 2]
            net.arrived(y_slot[ch], RBY.at[ch])
            HO[ch] = HO[ch] + RBY[ch].astype(F32)

        def mixed_rows(t, ch):
            src = meta[NCH * t + ch]
            v = MIXP[src]
            MIXS[rows_of(t, own, ch, CH), :] = v
            return dot(v, WO[...])

        f_relay_far(3, 5)
        ys = reduce_scatter(mixed_rows)
        for ch in range(NCH):
            ag_relay("gb", GB, ch)
        for ch in range(NCH):
            rs_finish(ys, ch)

            def norm2(u, _, ch=ch):
                q = pl.ds(pl.multiple_of(u * SUB, SUB), SUB)
                x = TOK[NCH * s + ch, q, :].astype(F32) + HO[ch, q, :]
                qo = pl.ds(pl.multiple_of(ch * CH + u * SUB, SUB), SUB)
                HID[qo, :] = x
                GH[qo, :] = TOK[NCH * s + ch, q, :]
                r = lax.rsqrt(jnp.mean(x * x, axis=1, keepdims=True) + EPSILON)
                N2[NCH * s + ch, q, :] = (x * r * gain2).astype(BF)
                return 0

            lax.fori_loop(0, CH // SUB, norm2, 0)
            ag_push("n2", N2, ch)
        c_wd.wait()
        for c in c_f:
            c.wait()
        f_wait(3, 5)
        for ch in range(NCH):
            ag_near("gb", GB, ch)
            ag_far("gb", GB, ch)

        def ffn(t):
            pair = pl.ds(2 * NCH * t, 2 * NCH)
            n = 2 * own
            for c in range(0, FW, 256):
                x = N2[pair].reshape(n, D)
                X[:, 0:256] = dot(x, WGU[:, c : c + 256])
                X[:, 256:512] = dot(x, WGU[:, FW + c : FW + c + 256])
                X[:, 512:768] = dot(GB[pair].reshape(n, D), WD[c : c + 256, :], 1, 1)

                def sub(u, _, c=c):
                    q = pl.ds(pl.multiple_of(u * 64, 64), 64)
                    at = pl.ds(pl.multiple_of(t * n + u * 64, 64), 64)
                    db = 2 * NCH * t + lax.div(u, BLK // 64)
                    dr = pl.ds(pl.multiple_of(lax.rem(u, BLK // 64) * 64, 64), 64)
                    gate, up, ga = X[q, 0:256], X[q, 256:512], X[q, 512:768]
                    sig = 1.0 / (1.0 + jnp.exp(-gate))
                    act = gate * sig
                    ACT[at, c : c + 256] = (act * up).astype(BF)
                    DGU[db, dr, c : c + 256] = (ga * up * (sig + act * (1.0 - sig))).astype(BF)
                    DGU[db, dr, FW + c : FW + c + 256] = (ga * act).astype(BF)
                    return 0

                lax.fori_loop(0, n // 64, sub, 0)

        chip = lax.div(s, 2)
        for ch in range(NCH):
            ag_near("n2", N2, ch)
        ffn(chip)
        for ch in range(NCH):
            ag_relay("n2", N2, ch)
        for ch in range(NCH):
            ag_far("n2", N2, ch)
        ffn(1 - chip)
        net.drain()

        ys = reduce_scatter(
            lambda t, ch: dot(DGU[NCH * t + ch], WGU[...], 1, 1)
        )

        def flat(ref, cols):
            v = ref[:, :, cols] if len(ref.shape) == 3 else ref[:, cols]
            return v.reshape(T, v.shape[-1])

        for t in range(S):
            n = FW // S
            GD[0, t] = dot(ACT[:, t * n : (t + 1) * n], GB[...].reshape(T, D), 0, 0).astype(BF)
        ticks.limit = ready[0]
        ticks.run(2)
        for ch in range(NCH):
            rs_finish(ys, ch)

            def norm2_back(u, acc, ch=ch):
                q = pl.ds(pl.multiple_of(u * SUB, SUB), SUB)
                qo = pl.ds(pl.multiple_of(ch * CH + u * SUB, SUB), SUB)
                x = HID[qo, :]
                du = HO[ch, q, :]
                r = lax.rsqrt(jnp.mean(x * x, axis=1, keepdims=True) + EPSILON)
                gd = du * gain2
                m = jnp.mean(x * gd, axis=1, keepdims=True)
                gh = GB[NCH * s + ch, q, :].astype(F32) + r * gd - x * (r * r * r * m)
                DX[qo, :] = gh
                GMI[NCH * s + ch, q, :] = gh.astype(BF)
                GG[:, D : 2 * D] = GG[:, D : 2 * D] + fold8(du * x * r)
                return acc

            lax.fori_loop(0, CH // SUB, norm2_back, 0)
            ag_push("gmi", GMI, ch)
            ticks.run()

        def wgrad_ffn(t, _):
            cols = pl.ds(pl.multiple_of(t * (D // S), 256), D // S)
            g = dot(flat(N2, cols), DGU[...].reshape(T, 2 * FW), 0, 0).astype(BF)
            GGU[0, t] = g[:, :FW]
            GGU[1, t] = g[:, FW:]
            return 0

        lax.fori_loop(0, S, wgrad_ffn, 0)
        ticks.limit = ready[1]
        ticks.run()
        for ch in range(NCH):
            ag_relay("gmi", GMI, ch)
        ticks.run()
        for ch in range(NCH):
            ag_near("gmi", GMI, ch)
            ag_far("gmi", GMI, ch)

        def gmix(i, _):
            a = GMI[meta[8 + 2 * i]]
            b = GMI[meta[9 + 2 * i]]
            gm = dot(jnp.concatenate([a, b], axis=0), WO[...], 1, 1).astype(BF)
            two = pl.ds(2 * i, 2)
            prod = gm.astype(F32) * MIXP[two].reshape(TILE, QW).astype(F32)
            r = rows_of(i, TILE)
            stat = LSE[r, :]
            for h in range(heads):
                inner = jnp.sum(prod[:, h * HD : (h + 1) * HD], axis=1, keepdims=True)
                stat = jnp.where(lane == heads + h, inner, stat)
            LSE[r, :] = stat
            GMP[two] = gm.reshape(2, BLK, QW)
            return 0

        lax.fori_loop(0, T // TILE, gmix, 0)
        for t in range(S):
            n = QW // S
            GO[0, t] = dot(MIXS[:, t * n : (t + 1) * n], GMI[...].reshape(T, D), 0, 0).astype(BF)
        ticks.limit = ready[2]
        ticks.run()
        net.drain()
        ys = reduce_scatter(lambda t, ch: dot(ACT[rows_of(t, own, ch, CH), :], WD[...]))

        def head_back(v, du, g):
            r = lax.rsqrt(jnp.mean(v * v, axis=1, keepdims=True) + EPSILON)
            gd = du * g
            m = jnp.mean(v * gd, axis=1, keepdims=True)
            return r * gd - v * (r * r * r * m), fold8(du * v * r)

        def unrotate(g, rr):
            co, si = rotation(rr)
            return g * co + pltpu.roll(g * si, HD // 2, 1)

        for k in range(T // HD):
            LT[:, k * HD : (k + 1) * HD] = LSE[k * HD : (k + 1) * HD, :].T[0:8]
        below = lax.broadcasted_iota(jnp.int32, (TILE, TILE), 0) <= lax.broadcasted_iota(
            jnp.int32, (TILE, TILE), 1
        )
        below = jnp.concatenate([below] * per, axis=1)

        def attend_back(kv, i):
            hs = [kv * per + k for k in range(per)]
            r = rows_of(i, TILE)
            q2 = jnp.concatenate([HEADS[r, head_cols(h)] for h in hs], axis=0)
            gm2 = jnp.concatenate(
                [GMP[2 * i : 2 * i + 2, :, head_cols(h)].reshape(TILE, HD) for h in hs], axis=0
            )
            lse2 = jnp.concatenate([LT[h : h + 1, i * TILE : (i + 1) * TILE] for h in hs], axis=1)
            in2 = jnp.concatenate(
                [LT[heads + h : heads + h + 1, i * TILE : (i + 1) * TILE] for h in hs], axis=1
            )

            def block(j, diagonal):
                rj = rows_of(j, TILE)
                kj = HEADS[rj, QW + kv * HD : QW + (kv + 1) * HD]
                vj = HEADS[rj, QK + kv * HD : QK + (kv + 1) * HD]
                sc = dot(kj, q2, 1, 1) * scale
                if diagonal:
                    sc = jnp.where(below, sc, -1e30)
                p = jnp.exp(sc - lse2)
                ds = (p * (dot(vj, gm2, 1, 1) - in2)).astype(BF)
                ck = slice(kv * HD, (kv + 1) * HD)
                cv = slice(KW + kv * HD, KW + (kv + 1) * HD)
                DKV[rj, cv] = DKV[rj, cv] + dot(p.astype(BF), gm2)
                DKV[rj, ck] = DKV[rj, ck] + dot(ds, q2) * scale
                return dot(kj, ds, 0, 0) * scale

            DQT[...] = block(i, True)
            if i:

                def off(j, _):
                    DQT[...] = DQT[...] + block(j, False)
                    return 0

                lax.fori_loop(0, i, off, 0)
            for k, h in enumerate(hs):
                dq = unrotate(DQT[:, k * TILE : (k + 1) * TILE].T, r)
                d, gg = head_back(RAW[r, head_cols(h)].astype(F32), dq, gq)
                DQKV[2 * i : 2 * i + 2, :, head_cols(h)] = d.astype(BF).reshape(2, BLK, HD)
                GG[:, 2 * D : 2 * D + HD] = GG[:, 2 * D : 2 * D + HD] + gg

        for kv in range(kvs):
            for i in range(T // TILE):
                attend_back(kv, i)
                ticks.run(2 if (kv * (T // TILE) + i) in TA else 1)

        def key_back(u, _):
            rr = rows_of(u, BLK)
            for kv in range(kvs):
                c = slice(QW + kv * HD, QW + (kv + 1) * HD)
                d, gg = head_back(
                    RAW[rr, c].astype(F32), unrotate(DKV[rr, kv * HD : (kv + 1) * HD], rr), gk
                )
                DQKV[u, :, c] = d.astype(BF)
                GG[:, 2 * D + HD : GW] = GG[:, 2 * D + HD : GW] + gg
            DQKV[u, :, QK:QKV] = DKV[rr, KW : 2 * KW].astype(BF)
            return 0

        lax.fori_loop(0, T // BLK, key_back, 0)
        for ch in range(NCH):
            rs_finish(ys, ch)

            def out_rows(u, _, ch=ch):
                q = pl.ds(pl.multiple_of(u * SUB, SUB), SUB)
                qo = pl.ds(pl.multiple_of(ch * CH + u * SUB, SUB), SUB)
                GB[NCH * s + ch, q, :] = (HID[qo, :] + HO[ch, q, :]).astype(BF)
                return 0

            lax.fori_loop(0, CH // SUB, out_rows, 0)
        c_out = [local(GB.at[NCH * s + ch], out_o.at[ch * CH : (ch + 1) * CH]) for ch in range(NCH)]
        net.drain()
        ticks.run()

        def back_rows(t, ch):
            src = meta[NCH * t + ch]
            return dot(DQKV[src, :, 0:QKV], WQKV[...], 1, 1)

        ys = reduce_scatter(back_rows)

        def wgrad_qkv(t, _):
            cols = pl.ds(pl.multiple_of(t * (D // S), 256), D // S)
            g = dot(NP[:, cols], flat(DQKV, slice(0, QKV)), 0, 0).astype(BF)
            GQ[0, t] = g[:, :QW]
            GKV[0, t] = g[:, QW:QK]
            GKV[1, t] = g[:, QK:]
            return 0

        lax.fori_loop(0, S, wgrad_qkv, 0)
        ticks.limit = ready[4]
        ticks.run(2)
        for ch in range(NCH):
            rs_finish(ys, ch)

            def norm1_back(u, acc, ch=ch):
                q = pl.ds(pl.multiple_of(u * SUB, SUB), SUB)
                qo = pl.ds(pl.multiple_of(ch * CH + u * SUB, SUB), SUB)
                x = GH[qo, :].astype(F32)
                du = HO[ch, q, :]
                r = lax.rsqrt(jnp.mean(x * x, axis=1, keepdims=True) + EPSILON)
                gd = du * gain1
                m = jnp.mean(x * gd, axis=1, keepdims=True)
                DX[qo, :] = DX[qo, :] + r * gd - x * (r * r * r * m)
                GG[:, 0:D] = GG[:, 0:D] + fold8(du * x * r)
                return acc

            lax.fori_loop(0, CH // SUB, norm1_back, 0)
            ticks.run()
        c_dx = local(DX, dx_o)
        def gain_part(t):
            c = pl.multiple_of(t * own, 256)
            return (
                (GG.at[:, pl.ds(c, own)], 0, own),
                (GG.at[:, pl.ds(pl.multiple_of(D + c, 256), own)], own, own),
                (GG.at[:, 2 * D : GW], 2 * own, 2 * HD),
            )

        n_slot = {}
        for k in (1, 2, 3):
            for j, (src, to, w) in enumerate(gain_part(s ^ k)):
                n_slot[k, j] = net.slot()
                net.push(n_slot[k, j], src, GS.at[k, :, to : to + w], tp.sh(k))
        mine = [local(src, GS.at[0, :, to : to + w]) for src, to, w in gain_part(s)]
        ticks.run()
        for c in mine:
            c.wait()
        for k in (1, 2, 3):
            for j, (src, to, w) in enumerate(gain_part(s ^ k)):
                net.arrived(n_slot[k, j], GS.at[k, :, to : to + w])
        GS[0] = (GS[0] + GS[1]) + (GS[2] + GS[3])
        r_slot = [net.slot() for _ in range(R)]
        for k in range(1, R):
            net.push(r_slot[k], GS.at[0], gg_o.at[tp.r], tp.rep(lax.rem(tp.r + k, R)))
        c_gg = local(GS.at[0], gg_o.at[tp.r])
        ticks.run()
        for k in range(1, R):
            net.arrived(r_slot[k], gg_o.at[lax.rem(tp.r + R - k, R)])
        ticks.finish()
        for c in c_out + [c_dx, c_gg]:
            c.wait()
        net.drain()

    any_ = pl.BlockSpec(memory_space=pl.ANY)
    specs = [pl.BlockSpec(memory_space=pltpu.SMEM)] + [any_] * 11
    return pl.pallas_call(
        body,
        out_shape=[jax.ShapeDtypeStruct(*o) for o in outs],
        in_specs=specs,
        out_specs=[any_] * len(outs),
        scratch_shapes=scratch,
        compiler_params=pltpu.CompilerParams(
            collective_id=2, has_side_effects=True, vmem_limit_bytes=64 << 20
        ),
        name="layer",
    )(*args)


def rotary_table(slot_len, head_width):
    middle = head_width // 2
    inverse = np.power(ROPE_BASE, -np.arange(middle) * 2.0 / head_width).astype(np.float32)
    phases = np.arange(slot_len, dtype=np.float32)[:, None] * inverse
    cosine = np.cos(phases.astype(np.float64))
    sine = np.sin(phases.astype(np.float64))
    table = np.concatenate([cosine, sine], axis=1)
    return table.astype(np.float32)


def shards(
    tokens,
    cotangent,
    lengths,
    block_order,
    norm1_gain,
    query_weight,
    key_weight,
    value_weight,
    output_weight,
    query_gain,
    key_gain,
    norm2_gain,
    gate_weight,
    up_weight,
    down_weight,
):
    S, R = lax.axis_size("shard"), lax.axis_size("replica")
    at = lax.axis_index("shard")
    z = layer_sizes(tokens[0], query_weight, key_weight, gate_weight, query_gain, S)
    D, HD = z["D"], z["HD"]
    full = []
    for g, size in ((norm1_gain, D), (norm2_gain, D), (query_gain, HD), (key_gain, HD)):
        owner = jnp.arange(size, dtype=jnp.int32) // g.shape[0]
        full.append(jnp.where(owner == at, jnp.tile(g.astype(F32), S), 0.0))
    gains = jnp.broadcast_to(jnp.concatenate(full)[None], (8, 2 * D + 2 * HD))
    order = block_order[0]
    count = order.shape[0]
    place = jnp.arange(count, dtype=jnp.int32)
    inverse = jnp.sum(jnp.where(order[None, :] == place[:, None], place[None, :], 0), axis=1)
    meta = jnp.concatenate([order, inverse, lengths, jnp.zeros((15,), jnp.int32)])
    table = jnp.asarray(rotary_table(z["T"], HD))
    out, dx, gg, gd, ggu, go, gq, gkv = layer_call(
        z, S, R,
        (meta, tokens[0], cotangent[0], gains, table, query_weight, key_weight, value_weight,
         output_weight, gate_weight, up_weight, down_weight),
    )
    block = z["T"] // count
    mine_blocks = lax.dynamic_slice_in_dim(order, at * (z["own"] // block), z["own"] // block)
    position = mine_blocks[:, None] * block + jnp.arange(block, dtype=jnp.int32)[None, :]
    valid = position.reshape(-1, 1) < lengths[0]
    out = jnp.where(valid, out, jnp.zeros_like(out))
    small = jnp.sum(gg, axis=(0, 1))
    own, hw = z["own"], HD // S

    def mine(first):
        return lax.dynamic_slice_in_dim(small, first + at * hw, hw)

    return (
        out[None],
        dx[None],
        small[:own],
        gq[0].astype(F32),
        gkv[0].astype(F32),
        gkv[1].astype(F32),
        go.astype(F32).reshape(-1, D),
        mine(2 * own),
        mine(2 * own + HD),
        small[own : 2 * own],
        ggu[0].astype(F32),
        ggu[1].astype(F32),
        gd.astype(F32).reshape(-1, D),
    )


def solution(mesh):
    rows, mat, vec = P("replica", "shard", None), P("shard", None), P("shard")
    placed = (rows, rows, P("replica"), P("replica", None), vec, mat, mat, mat, mat)
    placed += (vec, vec, vec, mat, mat, mat)
    outs = (rows, rows, vec, mat, mat, mat, mat, vec, vec, vec, mat, mat, mat)
    return jax.shard_map(shards, mesh=mesh, in_specs=placed, out_specs=outs, check_vma=False)
```

```python
import functools

import jax
import jax.numpy as jnp
import numpy as np
from jax import lax
from jax.experimental import pallas as pl
from jax.experimental.pallas import tpu as pltpu
from jax.sharding import PartitionSpec as P

EPSILON = 1e-06
ROPE_BASE = 1000000.0
BF = jnp.bfloat16
F32 = jnp.float32
MESH = pl.DeviceIdType.MESH


class Topo:
    def __init__(self, shards, replicas):
        self.S = shards
        self.R = replicas
        self.L = replicas // 2
        self.s = lax.axis_index("shard")
        r = lax.axis_index("replica")
        self.r = r
        L = self.L
        a = lax.div(r, 2)
        self.b = lax.rem(r, 2)
        left = a <= L // 2 - 1
        self.mid = jnp.logical_or(a == L // 2 - 1, a == L // 2)
        self.edge = jnp.logical_or(a == 0, a == L - 1)
        self.inner = jnp.logical_not(self.edge)
        self.side = jnp.logical_not(self.mid)
        self.toward = jnp.where(left, r + 2, r - 2)
        self.outward = jnp.where(left, r - 2, r + 2)
        self.h = jnp.where(left, 0, 1)

    def rep(self, r):
        return (self.s, r)

    def sh(self, k):
        return (self.s ^ k, self.r)


def barrier(tp):
    bar = pltpu.get_barrier_semaphore()
    ids = [tp.rep(lax.rem(tp.r + k, tp.R)) for k in range(1, tp.R)]
    ids += [tp.sh(1), tp.sh(2), tp.sh(3)]
    for d in ids:
        pl.semaphore_signal(bar, inc=1, device_id=d, device_id_type=MESH)
    pl.semaphore_wait(bar, len(ids))


def add_rows(dst, a, b):
    blocks, parts, rows, _ = a.shape

    def body(i, _):
        q = pl.ds(pl.multiple_of(i * 16, 16), 16)
        for w in range(blocks):
            for t in range(parts):
                dst[w, t, q, :] = (a[w, t, q, :].astype(F32) + b[w, t, q, :].astype(F32)).astype(BF)
        return 0

    lax.fori_loop(0, rows // 16, body, 0)


class Chunk:
    def __init__(self, tp, kind, G, out, base, nr, spread, bufs, send, recv, at):
        self.tp, self.G, self.out, self.base, self.nr, self.hr = tp, G, out, base, nr, nr // 2
        self.spread, self.bufs, self.send, self.recv_sem, self.at = spread, bufs, send, recv, at
        self.W = G.shape[3]
        self.sent = []
        self.steps = self.steps_a() if kind == "A" else self.steps_b()

    def rows(self, h):
        return pl.ds(pl.multiple_of(self.base + h * self.hr, 16), self.hr)

    def half(self, h):
        return self.G.at[:, :, self.rows(h), :]

    def out_half(self, h):
        return self.out.at[:, self.rows(h), :] if self.spread else self.out.at[:, :, self.rows(h), :]

    def out_piece(self, h, s):
        return self.out.at[:, self.rows(h), pl.ds(pl.multiple_of(s * self.W, 128), self.W)]

    def copy(self, slot, src, dst, dev):
        k = self.at + slot
        return pltpu.make_async_remote_copy(
            src, dst, self.send.at[k], self.recv_sem.at[k], device_id=dev, device_id_type=MESH
        )

    def start(self, cond, slot, src, dst, dev):
        c = self.copy(slot, src, dst, dev)
        if cond is None:
            c.start()
        else:
            pl.when(cond)(lambda: c.start())
        self.sent.append((cond, c))

    def drain(self):
        for cond, c in self.sent:
            if cond is None:
                c.wait_send()
            else:
                pl.when(cond)(lambda c=c: c.wait_send())

    def arrived(self, slot, ref):
        self.copy(slot, ref, ref, self.tp.rep(self.tp.r ^ 1)).wait_recv()

    def local(self, src, dst):
        return pltpu.make_async_copy(src, dst, self.send.at[self.at + 9])

    def final_out(self, h, F):
        tp = self.tp
        if self.spread:
            for k in (1, 2, 3):
                self.start(tp.mid, 2 + k, F.at[:, tp.s ^ k], self.out_piece(h, tp.s), tp.sh(k))

        @pl.when(tp.mid)
        def _():
            if self.spread:
                self.local(F.at[:, tp.s], self.out_piece(h, tp.s)).start()
            else:
                self.local(F, self.out_half(h)).start()

    def final_wait(self, h, F):
        tp = self.tp
        if self.spread:
            for k in (1, 2, 3):
                self.arrived(2 + k, self.out_piece(h, tp.s ^ k))
            self.local(F.at[:, tp.s], self.out_piece(h, tp.s)).wait()
        else:
            self.local(F, self.out_half(h)).wait()

    def steps_a(self):
        tp = self.tp
        b = tp.b
        RX, FOLD, MID = self.bufs
        xp = tp.rep(tp.r ^ 1)
        own = self.half(b)
        both = jnp.logical_and

        def onward(cond):
            self.start(both(cond, tp.mid), 2, own, MID, tp.rep(tp.toward))
            if tp.L > 2:
                self.start(both(cond, tp.side), 1, own, FOLD, tp.rep(tp.toward))

        def s0():
            self.start(None, 0, self.half(1 - b), RX, xp)

        def s1():
            self.arrived(0, RX)
            add_rows(own, own, RX)
            onward(tp.edge)

        def s2():
            if tp.L == 2:
                return

            @pl.when(tp.inner)
            def _():
                self.arrived(1, FOLD)
                add_rows(own, own, FOLD)

            onward(tp.inner)

        def s3():
            @pl.when(tp.mid)
            def _():
                self.arrived(2, MID)
                add_rows(MID, own, MID)

            self.final_out(b, MID)

        def s4():
            pl.when(tp.mid)(lambda: self.final_wait(b, MID))
            if tp.L > 2:
                self.start(tp.mid, 6, self.out_half(b), self.out_half(b), tp.rep(tp.outward))
            self.start(tp.mid, 7, self.out_half(b), self.out_half(b), xp)

        def s5():
            if tp.L == 2:
                return
            pl.when(tp.side)(lambda: self.arrived(6, self.out_half(b)))
            if tp.L > 4:
                self.start(
                    both(tp.side, tp.inner), 6, self.out_half(b), self.out_half(b), tp.rep(tp.outward)
                )
            self.start(tp.side, 7, self.out_half(b), self.out_half(b), xp)

        def s6():
            self.arrived(7, self.out_half(1 - b))

        return [s0, s1, s2, s3, s4, s5, s6]

    def steps_b(self):
        tp = self.tp
        h = tp.h
        FOLD, MID, XB = self.bufs
        xp = tp.rep(tp.r ^ 1)
        own, other = self.half(h), self.half(1 - h)
        full = self.G.at[:, :, self.base : self.base + self.nr, :]
        both = jnp.logical_and

        def onward(cond):
            self.start(both(cond, tp.mid), 2, other, MID, tp.rep(tp.toward))
            if tp.L > 2:
                self.start(both(cond, tp.side), 1, full, FOLD, tp.rep(tp.toward))

        def s0():
            onward(tp.edge)

        def s1():
            if tp.L == 2:
                return

            @pl.when(tp.inner)
            def _():
                self.arrived(1, FOLD)
                add_rows(full, full, FOLD)

            onward(tp.inner)

        def s2():
            @pl.when(tp.mid)
            def _():
                self.arrived(2, MID)
                add_rows(own, own, MID)

            self.start(tp.mid, 0, own, XB, xp)

        def s3():
            @pl.when(tp.mid)
            def _():
                self.arrived(0, XB)
                add_rows(XB, own, XB)

            self.final_out(h, XB)

        def s4():
            pl.when(tp.mid)(lambda: self.final_wait(h, XB))
            self.start(tp.mid, 8, self.out_half(h), self.out_half(h), tp.rep(tp.toward))
            if tp.L > 2:
                self.start(tp.mid, 6, self.out_half(h), self.out_half(h), tp.rep(tp.outward))

        def s5():
            pl.when(tp.mid)(lambda: self.arrived(8, self.out_half(1 - h)))
            if tp.L == 2:
                return
            self.start(tp.mid, 7, self.out_half(1 - h), self.out_half(1 - h), tp.rep(tp.outward))
            pl.when(tp.side)(lambda: self.arrived(6, self.out_half(h)))
            if tp.L > 4:
                self.start(
                    both(tp.side, tp.inner), 6, self.out_half(h), self.out_half(h), tp.rep(tp.outward)
                )

        def s6():
            if tp.L == 2:
                return
            pl.when(tp.side)(lambda: self.arrived(7, self.out_half(1 - h)))
            if tp.L > 4:
                self.start(
                    both(tp.side, tp.inner),
                    7,
                    self.out_half(1 - h),
                    self.out_half(1 - h),
                    tp.rep(tp.outward),
                )

        return [s0, s1, s2, s3, s4, s5, s6]


class Ticks:
    def __init__(self, chunks, stride):
        self.chunks, self.stride, self.t, self.limit = chunks, stride, 0, 0
        self.begun = []

    def run(self, count=1):
        for _ in range(count):
            if len(self.begun) < min(self.limit, len(self.chunks)):
                self.begun.append(self.t)
            for k in range(6, -1, -1):
                for chunk, begun in zip(self.chunks, self.begun):
                    if begun == self.t - k * self.stride:
                        chunk.steps[k]()
            self.t += 1

    def finish(self):
        self.limit = len(self.chunks)
        while len(self.begun) < self.limit or self.t <= self.begun[-1] + 6 * self.stride:
            self.run()
        for c in self.chunks:
            c.drain()


class Net:
    def __init__(self, tp, send, recv):
        self.tp = tp
        self.send = send
        self.recv = recv
        self.k = 0
        self.live = []

    def slot(self):
        self.k += 1
        return self.k - 1

    def make(self, slot, src, dst, dev):
        return pltpu.make_async_remote_copy(
            src, dst, self.send.at[slot], self.recv.at[slot], device_id=dev, device_id_type=MESH
        )

    def push(self, slot, src, dst, dev):
        c = self.make(slot, src, dst, dev)
        c.start()
        self.live.append(c)
        return c

    def arrived(self, slot, ref):
        self.make(slot, ref, ref, self.tp.sh(1)).wait_recv()

    def drain(self, some=None):
        for c in self.live if some is None else some:
            c.wait_send()
        self.live = [] if some is None else [c for c in self.live if all(c is not d for d in some)]


def dot(a, b, ca=1, cb=0):
    return lax.dot_general(a, b, (((ca,), (cb,)), ((), ())), preferred_element_type=F32)


def rows_of(t, rows, ch=0, ch_rows=None):
    n = rows if ch_rows is None else ch_rows
    start = t * rows + ch * n
    return pl.ds(start if isinstance(start, int) else pl.multiple_of(start, 128), n)


def fold8(v):
    out = v[0:8]
    for k in range(1, v.shape[0] // 8):
        out = out + v[8 * k : 8 * k + 8]
    return out


def layer_sizes(tokens, query_weight, key_weight, gate_weight, query_gain, shards):
    z = {}
    z["own"] = tokens.shape[0]
    z["D"] = tokens.shape[1]
    z["T"] = z["own"] * shards
    z["HD"] = query_gain.shape[0] * shards
    z["QW"] = query_weight.shape[1] // shards
    z["KW"] = key_weight.shape[1] // shards
    z["FW"] = gate_weight.shape[1] // shards
    return z


def layer_call(z, S, R, args):
    own, D, T, HD, QW, KW, FW = (z[k] for k in ("own", "D", "T", "HD", "QW", "KW", "FW"))
    QKV = QW + 2 * KW
    QK = QW + KW
    heads, kvs = QW // HD, KW // HD
    per = heads // kvs
    BLK = 128
    CH = 128
    TA = (0, 2, 4)
    NCH = own // CH
    TILE = 256
    scale = float(HD) ** -0.5
    SUB = 32
    GW = 2 * D + 2 * HD
    GN = 2 * own + 2 * HD

    vm = lambda shape, dtype: pltpu.VMEM(shape, dtype)
    scratch = [
        vm((T // BLK, BLK, D), BF), vm((T // BLK, BLK, D), BF), vm((T // BLK, BLK, D), BF), vm((T, D), BF),
        vm((D, QKV), BF), vm((D, 2 * FW), BF), vm((QW, D), BF), vm((FW, D), BF),
        vm((S, 8, 2 * own + HD), F32), vm((8, GW), F32), vm((T, HD), F32),
        vm((T, QK), BF), vm((T, QKV), BF), vm((T, HD), F32), vm((T // BLK, BLK, QW), BF), vm((T, QW), BF),
        vm((NCH, CH, D), BF), vm((2, NCH, CH, D), BF), vm((NCH, CH, D), BF), vm((2, NCH, CH, D), BF),
        vm((NCH, CH, D), F32), vm((own, D), F32), vm((own, D), BF),
        vm((T, FW), BF), vm((T // BLK, BLK, 2 * FW), BF), vm((T, 2 * KW), F32),
        vm((HD, per * TILE), F32), vm((8, T), F32), vm((8, GW), F32), vm((2 * own, max(QK, 768)), F32),
        vm((own, D), F32),
        vm((S, 8, GN), F32),
        pltpu.SemaphoreType.DMA((160,)), pltpu.SemaphoreType.DMA((160,)), pltpu.SemaphoreType.DMA((24,)),
    ]
    grads = [
        ((1, S, FW // S, D), 32, False),
        ((2, S, D // S, FW), 32, True),
        ((1, S, QW // S, D), 32, False),
        ((1, S, D // S, QW), 64, True),
        ((2, S, D // S, KW), 64, True),
    ]
    outs = [((own, D), BF), ((own, D), F32), ((R, 8, GN), F32)]
    FIXED = len(scratch)
    plan = []
    for j, (shape, nr, spread) in enumerate(grads):
        w, _, rows, width = shape
        outs.append(((w, rows, S * width) if spread else shape, BF))
        scratch.append(vm(shape, BF))
        for base in range(0, rows, nr):
            plan.append((j, base, "AB"[len(plan) % 2]))
    for j, base, kind in plan:
        (w, _, rows, width), nr, _ = grads[j]
        half = vm((w, S, nr // 2, width), BF)
        scratch += [half, half, half] if kind == "A" else [vm((w, S, nr, width), BF), half, half]
    sems = pltpu.SemaphoreType.DMA((10 * len(plan),))
    scratch += [sems, sems]

    def body(*refs):
        meta, tok_in, cot_in, gains_in, cs_in, wq_in, wk_in, wv_in, wo_in, wg_in, wu_in, wd_in = refs[:12]
        out_o, dx_o, gg_o = refs[12:15]
        grad_o = refs[15:20]
        (TOK, GB, N2, NP, WQKV, WGU, WO, WD, GAIN, GV, CS, RAW, HEADS, LSE, MIXP, MIXS,
         SBC, RBC, SBY, RBYS, HO, HID, GH, ACT, DGU, DKV, DQT, LT, GG, X, DX,
         GS, send, recv, lsem) = refs[20:20 + FIXED]
        G = refs[20 + FIXED : 25 + FIXED]
        GD, GGU, GO, GQ, GKV = G
        bufs = refs[25 + FIXED : -2]
        GMI, GMP, DQKV = TOK, MIXP, DGU
        round_no = [0]
        tp = Topo(S, R)
        net = Net(tp, send, recv)
        chunks = []
        for i, (j, base, kind) in enumerate(plan):
            shape, nr, spread = grads[j]
            chunks.append(
                Chunk(tp, kind, G[j], grad_o[j], base, nr, spread, bufs[3 * i : 3 * i + 3], refs[-2], refs[-1], 10 * i)
            )
        ticks = Ticks(chunks, 2)
        ready = [sum(1 for p in plan if p[0] <= j) for j in range(len(grads))]
        s = tp.s
        lk = [0]
        locals_live = []

        def local(src, dst):
            c = pltpu.make_async_copy(src, dst, lsem.at[lk[0]])
            lk[0] += 1
            c.start()
            return c

        me = rows_of(s, own)
        def wcols(t):
            return (
                (wq_in, t * QW, QW, WQKV, 0),
                (wk_in, t * KW, KW, WQKV, QW),
                (wv_in, t * KW, KW, WQKV, QK),
                (wg_in, t * FW, FW, WGU, 0),
                (wu_in, t * FW, FW, WGU, FW),
            )

        def w_local(lo, hi):
            return [
                local(ref.at[:, pl.ds(pl.multiple_of(at, 128), w)], dst.at[me, to : to + w])
                for ref, at, w, dst, to in wcols(s)[lo:hi]
            ]

        barrier(tp)
        g_slot = [net.slot() for _ in range(3)]
        for k in (1, 2, 3):
            net.push(g_slot[k - 1], gains_in, GAIN.at[s], tp.sh(k))
        gath = {}

        def ag_push(name, buf, ch, src=None):
            r = NCH * s + ch
            k1, k2, k3 = net.slot(), net.slot(), net.slot()
            gath[name, ch] = (k1, k2, k3)
            src = buf.at[r] if src is None else src
            c = net.push(k2, src, buf.at[r], tp.sh(2))
            net.push(k1, src, buf.at[r], tp.sh(1))
            return c

        def ag_relay(name, buf, ch):
            k1, k2, k3 = gath[name, ch]
            r = NCH * (s ^ 2) + ch
            net.arrived(k2, buf.at[r])
            net.push(k3, buf.at[r], buf.at[r], tp.sh(1))

        def ag_near(name, buf, ch):
            net.arrived(gath[name, ch][0], buf.at[NCH * (s ^ 1) + ch])

        def ag_far(name, buf, ch):
            net.arrived(gath[name, ch][2], buf.at[NCH * (s ^ 3) + ch])

        half = own // 2
        quarter = own // 4
        zb = lax.rem(lax.div(tp.r, 2), 2)
        fsl = {}

        def f_part(k, j, z, x):
            _, _, w, dst, to = wcols(s)[j]
            at = (s ^ k) * own + z * half + x * quarter
            return dst.at[pl.ds(pl.multiple_of(at, quarter), quarter), to : to + w]

        def f_push(lo, hi):
            far = []
            for k in (2, 3, 1):
                for j, (ref, at, w, dst, to) in enumerate(wcols(s ^ k)):
                    if not lo <= j < hi:
                        continue
                    fsl[k, j] = [net.slot() for _ in range(4)]
                    cols = pl.ds(pl.multiple_of(at, 128), w)
                    if k == 1:
                        net.push(fsl[k, j][0], ref.at[:, cols], dst.at[me, to : to + w], tp.sh(k))
                    else:
                        q0 = zb * half + tp.b * quarter
                        src = ref.at[pl.ds(pl.multiple_of(q0, quarter), quarter), cols]
                        r = pl.ds(pl.multiple_of(s * own + q0, quarter), quarter)
                        far.append(net.push(fsl[k, j][0], src, dst.at[r, to : to + w], tp.sh(k)))
            return far

        def f_relay(lo, hi):
            for k in (2, 3):
                for j in range(lo, hi):
                    part = f_part(k, j, zb, tp.b)
                    net.arrived(fsl[k, j][0], part)
                    net.push(fsl[k, j][1], part, part, tp.rep(tp.r ^ 1))
                    net.push(fsl[k, j][2], part, part, tp.rep(tp.r ^ 2))

        def f_relay_far(lo, hi):
            for k in (2, 3):
                for j in range(lo, hi):
                    part = f_part(k, j, zb, 1 - tp.b)
                    net.arrived(fsl[k, j][1], part)
                    net.push(fsl[k, j][3], part, part, tp.rep(tp.r ^ 2))

        def f_wait(lo, hi):
            for j in range(lo, hi):
                _, _, w, dst, to = wcols(s)[j]
                net.arrived(fsl[1, j][0], dst.at[rows_of(s ^ 1, own), to : to + w])
                for k in (2, 3):
                    net.arrived(fsl[k, j][2], f_part(k, j, 1 - zb, tp.b))
                    net.arrived(fsl[k, j][3], f_part(k, j, 1 - zb, 1 - tp.b))

        c_gain = local(gains_in, GAIN.at[s])
        c_tok = [
            local(tok_in.at[ch * CH : (ch + 1) * CH], TOK.at[NCH * s + ch]) for ch in range(NCH)
        ]
        c_cot = local(cot_in, GH)
        far = f_push(0, 3)
        net.drain(far)
        for ch in range(NCH):
            ag_push("tok", TOK, ch, tok_in.at[ch * CH : (ch + 1) * CH])
        f_relay(0, 3)
        c_w = w_local(0, 3)
        c_cs = local(cs_in, CS)
        c_cot.wait()
        length = meta[16]
        for ch in range(NCH):
            blk = meta[NCH * s + ch]
            def cot_rows(u, _, ch=ch, blk=blk):
                q = pl.multiple_of(u * SUB, SUB)
                pos = blk * BLK + q + lax.broadcasted_iota(jnp.int32, (SUB, D), 0)
                g = GH[pl.ds(ch * CH + q, SUB), :].astype(F32)
                GB[NCH * s + ch, pl.ds(q, SUB), :] = jnp.where(pos < length, g, 0.0).astype(BF)
                return 0

            lax.fori_loop(0, CH // SUB, cot_rows, 0)
        c_gain.wait()
        for k in (1, 2, 3):
            net.arrived(g_slot[k - 1], GAIN.at[s ^ k])
        at8 = lax.broadcasted_iota(jnp.int32, (8, HD), 1)
        hw = HD // S
        both = [jnp.zeros((8, HD), F32), jnp.zeros((8, HD), F32)]
        for t in range(S):
            GV[:, t * own : (t + 1) * own] = GAIN[t, :, 0:own]
            GV[:, D + t * own : D + (t + 1) * own] = GAIN[t, :, own : 2 * own]
            v = GAIN[t, :, 2 * own : 2 * own + HD]
            here = jnp.logical_and(at8 >= t * hw, at8 < (t + 1) * hw)
            for j in range(2):
                turn = (t * hw - j * hw) % HD
                moved = pltpu.roll(v, turn, 1) if turn else v
                both[j] = jnp.where(here, moved, both[j])
        GV[:, 2 * D : 2 * D + HD] = both[0]
        GV[:, 2 * D + HD : GW] = both[1]
        gain1 = GV[0:1, 0:D]
        gain2 = GV[0:1, D : 2 * D]
        gq = GV[0:1, 2 * D : 2 * D + HD]
        gk = GV[0:1, 2 * D + HD : GW]
        GG[...] = jnp.zeros_like(GG)
        DKV[...] = jnp.zeros_like(DKV)

        for c in c_tok:
            c.wait()
        for c in c_w:
            c.wait()
        for ch in range(NCH):
            ag_relay("tok", TOK, ch)
        f_relay_far(0, 3)
        for ch in range(NCH):
            ag_near("tok", TOK, ch)
            ag_far("tok", TOK, ch)

        def norm1(i, _):
            src = meta[8 + i]

            def sub(u, _):
                x = TOK[src, pl.ds(pl.multiple_of(u * SUB, SUB), SUB), :].astype(F32)
                r = lax.rsqrt(jnp.mean(x * x, axis=1, keepdims=True) + EPSILON)
                NP[pl.ds(pl.multiple_of(i * BLK + u * SUB, SUB), SUB), :] = (x * r * gain1).astype(BF)
                return 0

            return lax.fori_loop(0, BLK // SUB, sub, 0)

        lax.fori_loop(0, T // BLK, norm1, 0)
        f_wait(0, 3)
        f_push(3, 5)
        for ch in range(NCH):
            ag_push("gb", GB, ch)
        c_wo = local(wo_in, WO)
        c_f = w_local(3, 5)
        c_wd = local(wd_in, WD)
        c_cs.wait()

        def rotation(rr):
            v = CS[rr, :]
            w = pltpu.roll(v, HD // 2, 1)
            low = lax.broadcasted_iota(jnp.int32, v.shape, 1) < HD // 2
            return jnp.where(low, v, w), jnp.where(low, -w, v)

        def proj(i, _):
            r = rows_of(i, TILE)
            raw = dot(NP[r, :], WQKV[...])
            X[0:TILE, 0:QK] = raw[:, :QK]
            HEADS[r, QK:] = raw[:, QK:].astype(BF)

            def sub(u, _):
                rr = pl.ds(pl.multiple_of(i * TILE + u * (2 * SUB), (2 * SUB)), (2 * SUB))
                co, si = rotation(rr)
                for h in range(heads + kvs):
                    g = gq if h < heads else gk
                    v = X[pl.ds(pl.multiple_of(u * (2 * SUB), (2 * SUB)), (2 * SUB)), h * HD : (h + 1) * HD]
                    RAW[rr, h * HD : (h + 1) * HD] = v.astype(BF)
                    n = v * lax.rsqrt(jnp.mean(v * v, axis=1, keepdims=True) + EPSILON) * g
                    HEADS[rr, h * HD : (h + 1) * HD] = (
                        n * co + pltpu.roll(n, HD // 2, 1) * si
                    ).astype(BF)
                return 0

            return lax.fori_loop(0, TILE // (2 * SUB), sub, 0)

        lax.fori_loop(0, T // TILE, proj, 0)

        f_relay(3, 5)
        lane = lax.broadcasted_iota(jnp.int32, (TILE, HD), 1)
        tri = lax.broadcasted_iota(jnp.int32, (TILE, TILE), 1) <= lax.broadcasted_iota(
            jnp.int32, (TILE, TILE), 0
        )

        def masked_scores(q, h_kv_cols, i):
            k = HEADS[0 : (i + 1) * TILE, h_kv_cols]
            sc = dot(q, k, 1, 1) * scale
            last = jnp.where(tri, sc[:, i * TILE :], -1e30)
            return last if i == 0 else jnp.concatenate([sc[:, : i * TILE], last], axis=1)

        def head_cols(h):
            return pl.ds(h * HD if isinstance(h, int) else pl.multiple_of(h * HD, HD), HD)

        def attend(h, _):
            kv = h // per if isinstance(h, int) else lax.div(h, per)
            kc = pl.ds(pl.multiple_of(QW + kv * HD, HD), HD)
            vc = pl.ds(pl.multiple_of(QK + kv * HD, HD), HD)
            for i in range(T // TILE):
                r = rows_of(i, TILE)
                sc = masked_scores(HEADS[r, head_cols(h)], kc, i)
                top = jnp.max(sc, axis=1, keepdims=True)
                e = jnp.exp(sc - top)
                total = jnp.sum(e, axis=1, keepdims=True)
                o = dot(e.astype(BF), HEADS[0 : (i + 1) * TILE, vc]) / total
                MIXP[i * (TILE // BLK) : (i + 1) * (TILE // BLK), :, head_cols(h)] = o.astype(BF).reshape(
                    TILE // BLK, BLK, HD
                )
                lse = top + jnp.log(total)
                LSE[r, :] = jnp.where(lane == h, lse, LSE[r, :])
            return 0

        LSE[...] = jnp.zeros_like(LSE)
        lax.fori_loop(0, heads, attend, 0)
        c_wo.wait()

        def reduce_scatter(partial):
            c_slot = [[net.slot() for _ in range(NCH)] for _ in range(2)]
            y_slot = [net.slot() for _ in range(NCH)]
            round_no[0] += 1
            sent = []
            RBY = RBYS.at[round_no[0] % 2]
            for ch in range(NCH):
                SBC[ch] = partial(s ^ 3, ch).astype(BF)
                sent.append(net.push(c_slot[0][ch], SBC.at[ch], RBC.at[0, ch], tp.sh(1)))
            for ch in range(NCH):
                part = partial(s ^ 2, ch)
                net.arrived(c_slot[0][ch], RBC.at[0, ch])
                SBY[ch] = (part + RBC[0, ch].astype(F32)).astype(BF)
                net.push(y_slot[ch], SBY.at[ch], RBY.at[ch], tp.sh(2))
            for ch in range(NCH):
                part = partial(s ^ 1, ch).astype(BF)
                net.drain([sent[ch]])
                SBC[ch] = part
                net.push(c_slot[1][ch], SBC.at[ch], RBC.at[1, ch], tp.sh(1))
            for ch in range(NCH):
                HO[ch] = partial(s, ch)
            for ch in range(NCH):
                net.arrived(c_slot[1][ch], RBC.at[1, ch])
                HO[ch] = HO[ch] + RBC[1, ch].astype(F32)
            return y_slot

        def rs_finish(y_slot, ch):
            RBY = RBYS.at[round_no[0] % 2]
            net.arrived(y_slot[ch], RBY.at[ch])
            HO[ch] = HO[ch] + RBY[ch].astype(F32)

        def mixed_rows(t, ch):
            src = meta[NCH * t + ch]
            v = MIXP[src]
            MIXS[rows_of(t, own, ch, CH), :] = v
            return dot(v, WO[...])

        f_relay_far(3, 5)
        ys = reduce_scatter(mixed_rows)
        for ch in range(NCH):
            ag_relay("gb", GB, ch)
        for ch in range(NCH):
            rs_finish(ys, ch)

            def norm2(u, _, ch=ch):
                q = pl.ds(pl.multiple_of(u * SUB, SUB), SUB)
                x = TOK[NCH * s + ch, q, :].astype(F32) + HO[ch, q, :]
                qo = pl.ds(pl.multiple_of(ch * CH + u * SUB, SUB), SUB)
                HID[qo, :] = x
                GH[qo, :] = TOK[NCH * s + ch, q, :]
                r = lax.rsqrt(jnp.mean(x * x, axis=1, keepdims=True) + EPSILON)
                N2[NCH * s + ch, q, :] = (x * r * gain2).astype(BF)
                return 0

            lax.fori_loop(0, CH // SUB, norm2, 0)
            ag_push("n2", N2, ch)
        c_wd.wait()
        for c in c_f:
            c.wait()
        f_wait(3, 5)
        for ch in range(NCH):
            ag_near("gb", GB, ch)
            ag_far("gb", GB, ch)

        def ffn(t):
            pair = pl.ds(2 * NCH * t, 2 * NCH)
            n = 2 * own
            for c in range(0, FW, 256):
                x = N2[pair].reshape(n, D)
                X[:, 0:256] = dot(x, WGU[:, c : c + 256])
                X[:, 256:512] = dot(x, WGU[:, FW + c : FW + c + 256])
                X[:, 512:768] = dot(GB[pair].reshape(n, D), WD[c : c + 256, :], 1, 1)

                def sub(u, _, c=c):
                    q = pl.ds(pl.multiple_of(u * 64, 64), 64)
                    at = pl.ds(pl.multiple_of(t * n + u * 64, 64), 64)
                    db = 2 * NCH * t + lax.div(u, BLK // 64)
                    dr = pl.ds(pl.multiple_of(lax.rem(u, BLK // 64) * 64, 64), 64)
                    gate, up, ga = X[q, 0:256], X[q, 256:512], X[q, 512:768]
                    sig = 1.0 / (1.0 + jnp.exp(-gate))
                    act = gate * sig
                    ACT[at, c : c + 256] = (act * up).astype(BF)
                    DGU[db, dr, c : c + 256] = (ga * up * (sig + act * (1.0 - sig))).astype(BF)
                    DGU[db, dr, FW + c : FW + c + 256] = (ga * act).astype(BF)
                    return 0

                lax.fori_loop(0, n // 64, sub, 0)

        chip = lax.div(s, 2)
        for ch in range(NCH):
            ag_near("n2", N2, ch)
        ffn(chip)
        for ch in range(NCH):
            ag_relay("n2", N2, ch)
        for ch in range(NCH):
            ag_far("n2", N2, ch)
        ffn(1 - chip)
        net.drain()

        ys = reduce_scatter(
            lambda t, ch: dot(DGU[NCH * t + ch], WGU[...], 1, 1)
        )

        def flat(ref, cols):
            v = ref[:, :, cols] if len(ref.shape) == 3 else ref[:, cols]
            return v.reshape(T, v.shape[-1])

        for t in range(S):
            n = FW // S
            GD[0, t] = dot(ACT[:, t * n : (t + 1) * n], GB[...].reshape(T, D), 0, 0).astype(BF)
        ticks.limit = ready[0]
        ticks.run(2)
        for ch in range(NCH):
            rs_finish(ys, ch)

            def norm2_back(u, acc, ch=ch):
                q = pl.ds(pl.multiple_of(u * SUB, SUB), SUB)
                qo = pl.ds(pl.multiple_of(ch * CH + u * SUB, SUB), SUB)
                x = HID[qo, :]
                du = HO[ch, q, :]
                r = lax.rsqrt(jnp.mean(x * x, axis=1, keepdims=True) + EPSILON)
                gd = du * gain2
                m = jnp.mean(x * gd, axis=1, keepdims=True)
                gh = GB[NCH * s + ch, q, :].astype(F32) + r * gd - x * (r * r * r * m)
                DX[qo, :] = gh
                GMI[NCH * s + ch, q, :] = gh.astype(BF)
                GG[:, D : 2 * D] = GG[:, D : 2 * D] + fold8(du * x * r)
                return acc

            lax.fori_loop(0, CH // SUB, norm2_back, 0)
            ag_push("gmi", GMI, ch)
            ticks.run()

        def wgrad_ffn(t, _):
            cols = pl.ds(pl.multiple_of(t * (D // S), 256), D // S)
            g = dot(flat(N2, cols), DGU[...].reshape(T, 2 * FW), 0, 0).astype(BF)
            GGU[0, t] = g[:, :FW]
            GGU[1, t] = g[:, FW:]
            return 0

        lax.fori_loop(0, S, wgrad_ffn, 0)
        ticks.limit = ready[1]
        ticks.run()
        for ch in range(NCH):
            ag_relay("gmi", GMI, ch)
        ticks.run()
        for ch in range(NCH):
            ag_near("gmi", GMI, ch)
            ag_far("gmi", GMI, ch)

        def gmix(i, _):
            a = GMI[meta[8 + 2 * i]]
            b = GMI[meta[9 + 2 * i]]
            gm = dot(jnp.concatenate([a, b], axis=0), WO[...], 1, 1).astype(BF)
            two = pl.ds(2 * i, 2)
            prod = gm.astype(F32) * MIXP[two].reshape(TILE, QW).astype(F32)
            r = rows_of(i, TILE)
            stat = LSE[r, :]
            for h in range(heads):
                inner = jnp.sum(prod[:, h * HD : (h + 1) * HD], axis=1, keepdims=True)
                stat = jnp.where(lane == heads + h, inner, stat)
            LSE[r, :] = stat
            GMP[two] = gm.reshape(2, BLK, QW)
            return 0

        lax.fori_loop(0, T // TILE, gmix, 0)
        for t in range(S):
            n = QW // S
            GO[0, t] = dot(MIXS[:, t * n : (t + 1) * n], GMI[...].reshape(T, D), 0, 0).astype(BF)
        ticks.limit = ready[2]
        ticks.run()
        net.drain()
        ys = reduce_scatter(lambda t, ch: dot(ACT[rows_of(t, own, ch, CH), :], WD[...]))

        def head_back(v, du, g):
            r = lax.rsqrt(jnp.mean(v * v, axis=1, keepdims=True) + EPSILON)
            gd = du * g
            m = jnp.mean(v * gd, axis=1, keepdims=True)
            return r * gd - v * (r * r * r * m), fold8(du * v * r)

        def unrotate(g, rr):
            co, si = rotation(rr)
            return g * co + pltpu.roll(g * si, HD // 2, 1)

        for k in range(T // HD):
            LT[:, k * HD : (k + 1) * HD] = LSE[k * HD : (k + 1) * HD, :].T[0:8]
        below = lax.broadcasted_iota(jnp.int32, (TILE, TILE), 0) <= lax.broadcasted_iota(
            jnp.int32, (TILE, TILE), 1
        )
        below = jnp.concatenate([below] * per, axis=1)

        def attend_back(kv, i):
            hs = [kv * per + k for k in range(per)]
            r = rows_of(i, TILE)
            q2 = jnp.concatenate([HEADS[r, head_cols(h)] for h in hs], axis=0)
            gm2 = jnp.concatenate(
                [GMP[2 * i : 2 * i + 2, :, head_cols(h)].reshape(TILE, HD) for h in hs], axis=0
            )
            lse2 = jnp.concatenate([LT[h : h + 1, i * TILE : (i + 1) * TILE] for h in hs], axis=1)
            in2 = jnp.concatenate(
                [LT[heads + h : heads + h + 1, i * TILE : (i + 1) * TILE] for h in hs], axis=1
            )

            def block(j, diagonal):
                rj = rows_of(j, TILE)
                kj = HEADS[rj, QW + kv * HD : QW + (kv + 1) * HD]
                vj = HEADS[rj, QK + kv * HD : QK + (kv + 1) * HD]
                sc = dot(kj, q2, 1, 1) * scale
                if diagonal:
                    sc = jnp.where(below, sc, -1e30)
                p = jnp.exp(sc - lse2)
                ds = (p * (dot(vj, gm2, 1, 1) - in2)).astype(BF)
                ck = slice(kv * HD, (kv + 1) * HD)
                cv = slice(KW + kv * HD, KW + (kv + 1) * HD)
                DKV[rj, cv] = DKV[rj, cv] + dot(p.astype(BF), gm2)
                DKV[rj, ck] = DKV[rj, ck] + dot(ds, q2) * scale
                return dot(kj, ds, 0, 0) * scale

            DQT[...] = block(i, True)
            if i:

                def off(j, _):
                    DQT[...] = DQT[...] + block(j, False)
                    return 0

                lax.fori_loop(0, i, off, 0)
            for k, h in enumerate(hs):
                dq = unrotate(DQT[:, k * TILE : (k + 1) * TILE].T, r)
                d, gg = head_back(RAW[r, head_cols(h)].astype(F32), dq, gq)
                DQKV[2 * i : 2 * i + 2, :, head_cols(h)] = d.astype(BF).reshape(2, BLK, HD)
                GG[:, 2 * D : 2 * D + HD] = GG[:, 2 * D : 2 * D + HD] + gg

        for kv in range(kvs):
            for i in range(T // TILE):
                attend_back(kv, i)
                ticks.run(2 if (kv * (T // TILE) + i) in TA else 1)

        def key_back(u, _):
            rr = rows_of(u, BLK)
            for kv in range(kvs):
                c = slice(QW + kv * HD, QW + (kv + 1) * HD)
                d, gg = head_back(
                    RAW[rr, c].astype(F32), unrotate(DKV[rr, kv * HD : (kv + 1) * HD], rr), gk
                )
                DQKV[u, :, c] = d.astype(BF)
                GG[:, 2 * D + HD : GW] = GG[:, 2 * D + HD : GW] + gg
            DQKV[u, :, QK:QKV] = DKV[rr, KW : 2 * KW].astype(BF)
            return 0

        lax.fori_loop(0, T // BLK, key_back, 0)
        for ch in range(NCH):
            rs_finish(ys, ch)

            blk = meta[NCH * s + ch]

            def out_rows(u, _, ch=ch, blk=blk):
                q = pl.ds(pl.multiple_of(u * SUB, SUB), SUB)
                qo = pl.ds(pl.multiple_of(ch * CH + u * SUB, SUB), SUB)
                pos = blk * BLK + u * SUB + lax.broadcasted_iota(jnp.int32, (SUB, D), 0)
                rows = jnp.where(pos < length, HID[qo, :] + HO[ch, q, :], 0.0)
                GB[NCH * s + ch, q, :] = rows.astype(BF)
                return 0

            lax.fori_loop(0, CH // SUB, out_rows, 0)
        c_out = [local(GB.at[NCH * s + ch], out_o.at[ch * CH : (ch + 1) * CH]) for ch in range(NCH)]
        net.drain()
        ticks.run()

        def back_rows(t, ch):
            src = meta[NCH * t + ch]
            return dot(DQKV[src, :, 0:QKV], WQKV[...], 1, 1)

        ys = reduce_scatter(back_rows)

        def wgrad_qkv(t, _):
            cols = pl.ds(pl.multiple_of(t * (D // S), 256), D // S)
            g = dot(NP[:, cols], flat(DQKV, slice(0, QKV)), 0, 0).astype(BF)
            GQ[0, t] = g[:, :QW]
            GKV[0, t] = g[:, QW:QK]
            GKV[1, t] = g[:, QK:]
            return 0

        lax.fori_loop(0, S, wgrad_qkv, 0)
        ticks.limit = ready[4]
        ticks.run(2)
        for ch in range(NCH):
            rs_finish(ys, ch)

            def norm1_back(u, acc, ch=ch):
                q = pl.ds(pl.multiple_of(u * SUB, SUB), SUB)
                qo = pl.ds(pl.multiple_of(ch * CH + u * SUB, SUB), SUB)
                x = GH[qo, :].astype(F32)
                du = HO[ch, q, :]
                r = lax.rsqrt(jnp.mean(x * x, axis=1, keepdims=True) + EPSILON)
                gd = du * gain1
                m = jnp.mean(x * gd, axis=1, keepdims=True)
                DX[qo, :] = DX[qo, :] + r * gd - x * (r * r * r * m)
                GG[:, 0:D] = GG[:, 0:D] + fold8(du * x * r)
                return acc

            lax.fori_loop(0, CH // SUB, norm1_back, 0)
            ticks.run()
        c_dx = local(DX, dx_o)
        def gain_part(t):
            c = pl.multiple_of(t * own, 256)
            return (
                (GG.at[:, pl.ds(c, own)], 0, own),
                (GG.at[:, pl.ds(pl.multiple_of(D + c, 256), own)], own, own),
                (GG.at[:, 2 * D : GW], 2 * own, 2 * HD),
            )

        n_slot = {}
        for k in (1, 2, 3):
            for j, (src, to, w) in enumerate(gain_part(s ^ k)):
                n_slot[k, j] = net.slot()
                net.push(n_slot[k, j], src, GS.at[k, :, to : to + w], tp.sh(k))
        mine = [local(src, GS.at[0, :, to : to + w]) for src, to, w in gain_part(s)]
        ticks.run()
        for c in mine:
            c.wait()
        for k in (1, 2, 3):
            for j, (src, to, w) in enumerate(gain_part(s ^ k)):
                net.arrived(n_slot[k, j], GS.at[k, :, to : to + w])
        GS[0] = (GS[0] + GS[1]) + (GS[2] + GS[3])
        r_slot = [net.slot() for _ in range(R)]
        for k in range(1, R):
            net.push(r_slot[k], GS.at[0], gg_o.at[tp.r], tp.rep(lax.rem(tp.r + k, R)))
        c_gg = local(GS.at[0], gg_o.at[tp.r])
        ticks.run()
        for k in range(1, R):
            net.arrived(r_slot[k], gg_o.at[lax.rem(tp.r + R - k, R)])
        ticks.finish()
        for c in c_out + [c_dx, c_gg]:
            c.wait()
        net.drain()

    any_ = pl.BlockSpec(memory_space=pl.ANY)
    specs = [pl.BlockSpec(memory_space=pltpu.SMEM)] + [any_] * 11
    return pl.pallas_call(
        body,
        out_shape=[jax.ShapeDtypeStruct(*o) for o in outs],
        in_specs=specs,
        out_specs=[any_] * len(outs),
        scratch_shapes=scratch,
        compiler_params=pltpu.CompilerParams(
            collective_id=2, has_side_effects=True, vmem_limit_bytes=64 << 20
        ),
        name="layer",
    )(*args)


def rotary_table(slot_len, head_width):
    middle = head_width // 2
    inverse = np.power(ROPE_BASE, -np.arange(middle) * 2.0 / head_width).astype(np.float32)
    phases = np.arange(slot_len, dtype=np.float32)[:, None] * inverse
    cosine = np.cos(phases.astype(np.float64))
    sine = np.sin(phases.astype(np.float64))
    table = np.concatenate([cosine, sine], axis=1)
    return table.astype(np.float32)


def shards(
    tokens,
    cotangent,
    lengths,
    block_order,
    norm1_gain,
    query_weight,
    key_weight,
    value_weight,
    output_weight,
    query_gain,
    key_gain,
    norm2_gain,
    gate_weight,
    up_weight,
    down_weight,
):
    S, R = lax.axis_size("shard"), lax.axis_size("replica")
    at = lax.axis_index("shard")
    z = layer_sizes(tokens[0], query_weight, key_weight, gate_weight, query_gain, S)
    D, HD = z["D"], z["HD"]
    gains = jnp.concatenate([norm1_gain, norm2_gain, query_gain, key_gain])
    gains = jnp.pad(gains, (0, 2 * z["own"] + HD - gains.shape[0])).astype(F32)
    gains = jnp.broadcast_to(gains[None], (8, gains.shape[0]))
    order = block_order[0]
    count = order.shape[0]
    place = jnp.arange(count, dtype=jnp.int32)
    inverse = jnp.sum(jnp.where(order[None, :] == place[:, None], place[None, :], 0), axis=1)
    meta = jnp.concatenate([order, inverse, lengths, jnp.zeros((15,), jnp.int32)])
    table = jnp.asarray(rotary_table(z["T"], HD))
    out, dx, gg, gd, ggu, go, gq, gkv = layer_call(
        z, S, R,
        (meta, tokens[0], cotangent[0], gains, table, query_weight, key_weight, value_weight,
         output_weight, gate_weight, up_weight, down_weight),
    )
    small = jnp.sum(gg, axis=(0, 1))
    own, hw = z["own"], HD // S

    def mine(first):
        return lax.dynamic_slice_in_dim(small, first + at * hw, hw)

    return (
        out[None],
        dx[None],
        small[:own],
        gq[0].astype(F32),
        gkv[0].astype(F32),
        gkv[1].astype(F32),
        go.astype(F32).reshape(-1, D),
        mine(2 * own),
        mine(2 * own + HD),
        small[own : 2 * own],
        ggu[0].astype(F32),
        ggu[1].astype(F32),
        gd.astype(F32).reshape(-1, D),
    )


def solution(mesh):
    rows, mat, vec = P("replica", "shard", None), P("shard", None), P("shard")
    placed = (rows, rows, P("replica"), P("replica", None), vec, mat, mat, mat, mat)
    placed += (vec, vec, vec, mat, mat, mat)
    outs = (rows, rows, vec, mat, mat, mat, mat, vec, vec, vec, mat, mat, mat)
    return jax.shard_map(shards, mesh=mesh, in_specs=placed, out_specs=outs, check_vma=False)
```
